128 devices in a mesh: dp: 32 (over z, y, core), section: 4 (over x).
Axes of the slice: x: 4, y: 4, z: 4, core: 2. Of those that a mesh axis runs over, the one named last changes fastest.
Arguments:
- real_in: bfloat16 [256, 144, 512], P('dp'), may hold values from -48 to 48
- fake_in: bfloat16 [256, 144, 512], P('dp'), may hold values from -48 to 48
- kernel_first: bfloat16 [5, 512, 1024], P(None, None, 'section'), may hold values from -0.15625 to 0.15625
- kernel_second: bfloat16 [5, 1024, 1024], P(None, None, 'section'), may hold values from -0.125 to 0.125
Outputs:
- layer_loss: float32 [2], replicated
- grad_first: float32 [512, 5, 1024], P('dp', None, 'section')
- grad_second: float32 [1024, 5, 1024], P('dp', None, 'section')
The draws below stay inside these ranges and needn't reach their ends.
All inputs are finite; a program needn't handle non-finite values.
Results may differ from the reference program's by a relative error of at most 0.012.
The reference program's roundings to bfloat16 on the way count: a program that leaves them out, or rounds other values in their place, can miss the bound.
Values may be sent and summed in bfloat16 or wider, within the bound.
No kernel may reach another device: no remote copies, remote signals or barrier semaphores. Data moves between devices by JAX's collectives and lax.ppermute only.
A program may use at most 128 MiB of HBM per device.

```python
import jax
import jax.numpy as jnp
from jax import lax

C = 1024
CIN = 512
K = 5
FRAMES = 48
COLS = 8
FRAMES_IN = 144
ROWS_ALL = 256


def draw_signal(key):
    subkeys = jax.random.split(key, 2)
    values_drawn = jnp.clip(jax.random.normal(subkeys[0], (ROWS_ALL, FRAMES_IN, CIN), jnp.float32), -4.0, 4.0)
    positions = jnp.arange(ROWS_ALL, dtype=jnp.float32)
    row_scale = 3.0 ** (positions / max(ROWS_ALL - 1, 1))
    channel_gain = jax.random.uniform(subkeys[1], (CIN,), jnp.float32, 0.5, 2.0)
    return (values_drawn * row_scale[:, None, None] * channel_gain).astype(jnp.bfloat16)


def draw_real_in(key, part):
    return draw_signal(jax.random.fold_in(key, 11))


def draw_fake_in(key, part):
    return draw_signal(jax.random.fold_in(key, 12))


def levels(own_key, dims, cuts, low, top_value):
    level, own = 1.0, jax.random.fold_in(own_key, 6)
    for axis_at, shards_of in cuts:
        draws = jnp.exp(jax.random.uniform(jax.random.fold_in(own, axis_at), (shards_of,), jnp.float32, low / len(cuts), top_value / len(cuts)))
        level = level * jnp.repeat(draws, dims[axis_at] // shards_of).reshape([-1 if axis == axis_at else 1 for axis in range(len(dims))])
    return level


def gaussian(own_key, dims, scale, reach, cuts=(), held_as=jnp.bfloat16):
    result = scale * jax.random.normal(own_key, dims, jnp.float32)
    if cuts:
        result = result * levels(own_key, dims, cuts, -0.22, 0.18)
    return jnp.clip(result, -reach, reach).astype(held_as)


def setup_inputs(seed: int = 0) -> dict:
    streams_of = jax.random.split(jax.random.key(seed), 5)
    real_in = draw_real_in(jax.random.fold_in(streams_of[4], 71), 0)
    fake_in = draw_fake_in(jax.random.fold_in(streams_of[4], 71), 0)
    kernel_first = gaussian(streams_of[2], (K, CIN, C), (K * CIN // 2) ** -0.5, 0.15625, ((2, 4),))
    kernel_second = gaussian(streams_of[3], (K, C, C), (K * C // 2) ** -0.5, 0.125, ((2, 4),))
    return dict(real_in=real_in, fake_in=fake_in, kernel_first=kernel_first, kernel_second=kernel_second)


smooth_width = 0.1
leak_slope = 0.1

def conv_strided(values, kernel, frames):
    padded = jnp.pad(values, ((0, 0), (2, 2), (0, 0)))
    summed = jnp.zeros((values.shape[0] * frames, kernel.shape[2]), jnp.float32)
    for tap in range(kernel.shape[0]):
        window = padded[:, tap:tap + 3 * frames - 2:3].reshape(-1, values.shape[2])
        summed = summed + jnp.dot(window, kernel[tap], preferred_element_type=jnp.float32)
    return summed.reshape(values.shape[0], frames, -1)

def conv_forward(values, kernel):
    frames = values.shape[1]
    padded = jnp.pad(values, ((0, 0), (2, 2), (0, 0)))
    summed = jnp.zeros((values.shape[0] * frames, kernel.shape[2]), jnp.float32)
    for tap in range(kernel.shape[0]):
        window = padded[:, tap:tap + frames].reshape(-1, values.shape[2])
        summed = summed + jnp.dot(window, kernel[tap], preferred_element_type=jnp.float32)
    return summed.reshape(values.shape[0], frames, -1)

def conv_backward(delta, kernel):
    frames = delta.shape[1]
    padded = jnp.pad(delta, ((0, 0), (2, 2), (0, 0)))
    summed = jnp.zeros((delta.shape[0] * frames, kernel.shape[1]), jnp.float32)
    for tap in range(kernel.shape[0]):
        window = padded[:, 4 - tap:4 - tap + frames].reshape(-1, delta.shape[2])
        summed = summed + lax.dot_general(window, kernel[tap], (((1,), (1,)), ((), ())), preferred_element_type=jnp.float32)
    return summed.reshape(delta.shape[0], frames, -1)

def weight_term(values, delta, offset, amount, stride):
    frames = delta.shape[1]
    padded = jnp.pad(values, ((0, 0), (2, 2), (0, 0)))
    padded = lax.dynamic_slice_in_dim(padded, offset, amount, 2)
    flat_delta = delta.reshape(-1, delta.shape[2])
    pieces = []
    for tap in range(K):
        window = padded[:, tap:tap + stride * (frames - 1) + 1:stride].reshape(-1, amount)
        pieces.append(lax.dot_general(window, flat_delta, (((0,), (0,)), ((), ())), preferred_element_type=jnp.float32))
    return jnp.stack(pieces, axis=1)

def activate(pre):
    return jnp.where(pre > 0, pre, leak_slope * pre).astype(jnp.bfloat16)

def local_grad(feature, normaliser):
    half = feature.shape[0] // 2
    difference = feature[:half].astype(jnp.float32) - feature[half:].astype(jnp.float32)
    slope = difference / jnp.sqrt(difference * difference + smooth_width * smooth_width) / normaliser
    return jnp.concatenate([slope, -slope], axis=0)

def smooth_total(feature):
    half = feature.shape[0] // 2
    difference = feature[:half].astype(jnp.float32) - feature[half:].astype(jnp.float32)
    return jnp.sum(jnp.sqrt(difference * difference + smooth_width * smooth_width) - smooth_width)

def reference(real_in, fake_in, kernel_first, kernel_second):
    row_total = real_in.shape[0]
    normaliser = float(COLS * FRAMES)
    values = jnp.concatenate([real_in, fake_in], axis=0)
    first = activate(conv_strided(values, kernel_first, FRAMES))
    second = activate(conv_forward(first, kernel_second))
    count_all = float(row_total * FRAMES * C)
    losses = jnp.stack([smooth_total(first) / count_all, smooth_total(second) / count_all])
    delta_second = (local_grad(second, normaliser) * jnp.where(second > 0, 1.0, leak_slope)).astype(jnp.bfloat16)
    grad_second = weight_term(first, delta_second, 0, C, 1)
    upstream = conv_backward(delta_second, kernel_second).astype(jnp.bfloat16).astype(jnp.float32)
    delta_first = ((local_grad(first, normaliser) + upstream) * jnp.where(first > 0, 1.0, leak_slope)).astype(jnp.bfloat16)
    grad_first = weight_term(values, delta_first, 0, CIN, 3)
    return (losses, grad_first, grad_second)
```

```python
import functools

import jax
import jax.numpy as jnp
from jax import lax
from jax.experimental import pallas as pl
from jax.experimental.pallas import tpu as pltpu
from jax.sharding import Mesh
from jax.sharding import PartitionSpec as P

DP = ("dp_0", "dp_1", "dp_2")
ZY = ("dp_0", "dp_1")
F32 = jnp.float32
BF16 = jnp.bfloat16

smooth_width = 0.1
leak_slope = 0.1


def leaky(pre):
    return jnp.where(pre > 0, pre, leak_slope * pre).astype(BF16)


def fold_rows(x):
    x = jnp.sum(x.reshape(-1, 8, x.shape[1]), axis=0)
    return sum(x[:, at : at + 128] for at in range(0, x.shape[1], 128))


def difference_terms(real, fake):
    difference = real.astype(F32) - fake.astype(F32)
    root = jnp.sqrt(difference * difference + smooth_width * smooth_width)
    return difference, root


def dot(a, b):
    return jnp.dot(a, b, preferred_element_type=F32)


def dot_rows(a, b):
    return lax.dot_general(a, b, (((0,), (0,)), ((), ())), preferred_element_type=F32)


def dot_lanes(a, b):
    return lax.dot_general(a, b, (((1,), (1,)), ((), ())), preferred_element_type=F32)


def first_kernel(real, fake, w, h_real, h_fake, phases, loss, padded):
    cols, span, _ = real.shape
    frames = span // 3
    half = cols * frames
    width = w.shape[2]
    row = lax.broadcasted_iota(jnp.int32, (span, span), 0)
    col = lax.broadcasted_iota(jnp.int32, (span, span), 1)
    phase = jnp.where(row >= 2 * frames, 2, jnp.where(row >= frames, 1, 0))
    select = (col == 3 * (row - frames * phase) + phase).astype(F32).astype(BF16)
    for source, base in ((real, 0), (fake, half)):

        def split(r, carry, source=source, base=base):
            parts = dot(select, source[r]).astype(BF16)
            at = pl.multiple_of(base + r * frames, 16)
            for p in range(3):
                phases[p, pl.ds(at, frames), :] = parts[p * frames : (p + 1) * frames]
            return carry

        lax.fori_loop(0, cols, split, 0)
    padded[:, :8, :] = jnp.zeros((2 * cols, 8, width), F32)
    earlier = dot(phases[1], w[0]) + dot(phases[2], w[1])
    padded[:, 8 : 8 + frames, :] = earlier.reshape(2 * cols, frames, width)
    same = dot(phases[0], w[2]) + dot(phases[1], w[3]) + dot(phases[2], w[4])
    pre = same + padded[:, 7 : 7 + frames, :].reshape(2 * half, width)
    h = leaky(pre)
    h_real[...] = h[:half]
    h_fake[...] = h[half:]
    _, root = difference_terms(h[:half], h[half:])
    loss[...] = fold_rows(root - smooth_width)


def second_kernel(
    normaliser, s_ref, own_r, own_f, prev_r, prev_f, next_r, next_f, far_r, far_f, w,
    h_all, shifted, t_r, t_f, loss, padded,
):
    half, width = own_r.shape
    taps = w.shape[0]
    frames = padded.shape[1] - 16
    s = s_ref[0]
    for (r, f), away in (
        ((own_r, own_f), 0), ((next_r, next_f), 1), ((far_r, far_f), 2), ((prev_r, prev_f), 3)
    ):
        at = pl.multiple_of(lax.rem(s + away, 4) * width, 256)
        h_all[:half, pl.ds(at, width)] = r[...]
        h_all[half:, pl.ds(at, width)] = f[...]
    zeros = jnp.zeros((padded.shape[0], 8, width), F32)
    padded[:, :8, :] = zeros
    padded[:, 8 + frames :, :] = zeros
    pre = dot(h_all[...], w[2])
    for k in (0, 1, 3, 4):
        padded[:, 8 : 8 + frames, :] = dot(h_all[...], w[k]).reshape(-1, frames, width)
        pre = pre + padded[:, 6 + k : 6 + k + frames, :].reshape(2 * half, width)
    h = leaky(pre)
    difference, root = difference_terms(h[:half], h[half:])
    loss[...] = fold_rows(root - smooth_width)
    slope = difference / root / normaliser
    for value, sign, at in ((h[:half], 1.0, 0), (h[half:], -1.0, half // frames)):
        gate = jnp.where(value.astype(F32) > 0, 1.0, leak_slope)
        delta = (sign * slope * gate).astype(BF16).astype(F32)
        padded[at : at + half // frames, 8 : 8 + frames, :] = delta.reshape(-1, frames, width)
    for k in range(taps):
        moved = padded[:, 10 - k : 10 - k + frames, :].reshape(2 * half, width)
        shifted[:, k * width : (k + 1) * width] = moved.astype(BF16)
    at = pl.multiple_of(lax.rem(s + 2, 4) * width, 256)
    term = back_term(shifted, w, at, width)
    t_r[...] = term[:half].astype(BF16)
    t_f[...] = term[half:].astype(BF16)


def back_term(shifted, w, at, width):
    term = None
    for k in range(w.shape[0]):
        part = dot_lanes(shifted[:, k * width : (k + 1) * width], w[k, pl.ds(at, width), :])
        term = part if term is None else term + part
    return term


def back_kernel(s_ref, shifted, w, own, next_r, next_f, prev_r, prev_f):
    width = w.shape[2]
    half = next_r.shape[0]
    s = s_ref[0]
    for away in (1, 3, 0):
        at = pl.multiple_of(lax.rem(s + away, 4) * width, 256)
        term = back_term(shifted, w, at, width).astype(BF16)
        if away == 0:
            own[...] = term
        else:
            r, f = (next_r, next_f) if away == 1 else (prev_r, prev_f)
            r[...] = term[:half]
            f[...] = term[half:]


def put(g, c, mine, theirs, at, k):
    rows = mine.shape[2]
    count = g.shape[0] // (2 * rows)
    g = g.astype(BF16).reshape(count, 2, rows, g.shape[1])
    even, odd = g[:, 0], g[:, 1]
    mine[at : at + count, k] = jnp.where(c == 0, even, odd)
    theirs[at : at + count, k] = jnp.where(c == 0, odd, even)


def weight_second_kernel(c_ref, h_all, shifted, mine, theirs):
    width = mine.shape[3]
    c = c_ref[0]
    step = 256
    for q in range(h_all.shape[1] // step):
        g = dot_rows(h_all[:, q * step : (q + 1) * step], shifted[...])
        for k in range(mine.shape[1]):
            put(g[:, k * width : (k + 1) * width], c, mine, theirs,
                q * step // (2 * mine.shape[2]), k)


def weight_first_kernel(
    normaliser, c_ref, h_real, h_fake, own, from_prev_r, from_prev_f, from_next_r, from_next_f,
    phases, mine, theirs, padded, moved,
):
    half, width = h_real.shape
    frames = padded.shape[1] - 8
    c = c_ref[0]
    difference, root = difference_terms(h_real[...], h_fake[...])
    slope = difference / root / normaliser
    padded[:, frames:, :] = jnp.zeros((padded.shape[0], 8, width), F32)
    for h, a, b, sign, at in (
        (h_real, from_prev_r, from_next_r, 1.0, 0), (h_fake, from_prev_f, from_next_f, -1.0, half)
    ):
        up = own[at : at + half, :].astype(F32) + a[...].astype(F32) + b[...].astype(F32)
        up = up.astype(BF16).astype(F32)
        gate = jnp.where(h[...].astype(F32) > 0, 1.0, leak_slope)
        delta = ((sign * slope + up) * gate).astype(BF16)
        moved[at : at + half, :width] = delta
        cols = half // frames
        lead = at // frames
        padded[lead : lead + cols, :frames, :] = delta.astype(F32).reshape(cols, frames, width)
    moved[:, width:] = padded[:, 1 : 1 + frames, :].reshape(2 * half, width).astype(BF16)
    for p in range(3):
        if p == 0:
            put(dot_rows(phases[p], moved[:, :width]), c, mine, theirs, 0, 2)
        else:
            g = dot_rows(phases[p], moved[...])
            put(g[:, :width], c, mine, theirs, 0, 2 + p)
            put(g[:, width:], c, mine, theirs, 0, p - 1)


def total_kernel(blocks, out):
    total = jnp.sum(blocks[...].astype(F32), axis=0)
    for k in range(total.shape[0]):
        out[:, k, :] = total[k]


def call(kernel, operands, outs, scratch=(), smem=0, flops=0, name=None):
    moved = sum(x.size * x.dtype.itemsize for x in operands)
    moved += sum(x.size * x.dtype.itemsize for x in outs)
    vmem, small = pl.BlockSpec(memory_space=pltpu.VMEM), pl.BlockSpec(memory_space=pltpu.SMEM)
    return pl.pallas_call(
        kernel,
        out_shape=outs,
        in_specs=[small if at < smem else vmem for at in range(len(operands))],
        out_specs=[vmem] * len(outs),
        scratch_shapes=list(scratch),
        compiler_params=pltpu.CompilerParams(vmem_limit_bytes=40 << 20),
        cost_estimate=pl.CostEstimate(flops=flops, bytes_accessed=moved, transcendentals=0),
        name=name,
    )(*operands)


def like(shape, dtype=BF16):
    return jax.ShapeDtypeStruct(shape, dtype)


def turn(x, step):
    count = lax.axis_size("section")
    return lax.ppermute(x, "section", [(i, (i + step) % count) for i in range(count)])


def across(x, axis, mask):
    return lax.ppermute(x, axis, [(i, i ^ mask) for i in range(lax.axis_size(axis))])


def add(*terms):
    return sum(t.astype(F32) for t in terms).astype(BF16)


def over_dp(mine, theirs, rows, taps, width):
    half = add(mine, across(theirs, "dp_2", 1))
    blocks = lax.all_to_all(half, ZY, 0, 0)
    return call(total_kernel, (blocks,), [like((rows, taps, width), F32)], name="total")[0]


def shards(real_in, fake_in, kernel_first, kernel_second):
    replicas = lax.axis_size(DP)
    cols, span, in_width = real_in.shape
    frames = span // 3
    taps, width_all, width = kernel_second.shape
    half = cols * frames
    rows = 2 * half
    normaliser = float(cols * frames)
    count_all = float(cols * replicas * frames * width_all)
    groups = replicas // 2
    s = lax.axis_index("section").reshape(1).astype(jnp.int32)
    c = lax.axis_index("dp_2").reshape(1).astype(jnp.int32)

    h_real, h_fake, phases, loss_first = call(
        first_kernel,
        (real_in, fake_in, kernel_first),
        [like((half, width)), like((half, width)), like((3, rows, in_width)), like((8, 128), F32)],
        [pltpu.VMEM((2 * cols, frames + 8, width), F32)],
        flops=2 * rows * taps * in_width * width,
        name="first",
    )
    prev_r = turn(h_real, 1)
    next_f = turn(h_fake, -1)
    prev_f = turn(h_fake, 1)
    next_r = turn(h_real, -1)
    far_r = turn(prev_r, 1)
    far_f = turn(next_f, -1)
    h_all, shifted, far_t_r, far_t_f, loss_second = call(
        functools.partial(second_kernel, normaliser),
        (s, h_real, h_fake, prev_r, prev_f, next_r, next_f, far_r, far_f, kernel_second),
        [like((rows, width_all)), like((rows, taps * width)), like((half, width)),
         like((half, width)), like((8, 128), F32)],
        [pltpu.VMEM((2 * cols, frames + 16, width), F32)],
        smem=1,
        flops=2 * rows * taps * (width_all + width) * width,
        name="second",
    )
    pass_r = turn(far_t_r, 1)
    pass_f = turn(far_t_f, -1)
    own_t, next_t_r, next_t_f, prev_t_r, prev_t_f = call(
        back_kernel,
        (s, shifted, kernel_second),
        [like((rows, width))] + [like((half, width))] * 4,
        smem=1,
        flops=2 * rows * taps * width * width * 3,
        name="back",
    )
    from_prev_f = turn(next_t_f, 1)
    from_next_r = turn(prev_t_r, -1)
    from_prev_r = turn(add(next_t_r, pass_r), 1)
    from_next_f = turn(add(prev_t_f, pass_f), -1)

    own_rows = width_all // replicas
    mine, theirs = call(
        weight_second_kernel,
        (c, h_all, shifted),
        [like((groups, taps, own_rows, width))] * 2,
        smem=1,
        flops=2 * rows * taps * width * width_all,
        name="weight_second",
    )
    grad_second = over_dp(mine, theirs, own_rows, taps, width)

    own_rows = in_width // replicas
    mine, theirs = call(
        functools.partial(weight_first_kernel, normaliser),
        (c, h_real, h_fake, own_t, from_prev_r, from_prev_f, from_next_r, from_next_f, phases),
        [like((groups, taps, own_rows, width))] * 2,
        [pltpu.VMEM((2 * cols, frames + 8, width), F32), pltpu.VMEM((rows, 2 * width), BF16)],
        smem=1,
        flops=2 * rows * taps * width * in_width,
        name="weight_first",
    )
    grad_first = over_dp(mine, theirs, own_rows, taps, width)

    losses = jnp.concatenate([loss_first, loss_second], axis=0)
    for axis, mask in (
        ("dp_2", 1), ("section", 1), ("section", 3), ("dp_1", 1), ("dp_1", 3), ("dp_0", 1),
        ("dp_0", 3),
    ):
        losses = losses + across(losses, axis, mask)
    layer_loss = jnp.sum(losses.reshape(2, 8 * 128), axis=1) / count_all
    return (layer_loss, grad_first, grad_second)


def solution(mesh):
    finer = Mesh(
        mesh.devices.reshape(4, 4, 2, mesh.shape["section"]), ("dp_0", "dp_1", "dp_2", "section")
    )
    return jax.shard_map(
        shards,
        mesh=finer,
        in_specs=(
            P(DP, None, None),
            P(DP, None, None),
            P(None, None, "section"),
            P(None, None, "section"),
        ),
        out_specs=(P(), P(DP, None, "section"), P(DP, None, "section")),
        check_vma=False,
    )
```

```python
import functools

import jax
import jax.numpy as jnp
from jax import lax
from jax.experimental import pallas as pl
from jax.experimental.pallas import tpu as pltpu
from jax.sharding import Mesh
from jax.sharding import PartitionSpec as P

DP = ("dp_0", "dp_1", "dp_2")
ZY = ("dp_0", "dp_1")
F32 = jnp.float32
BF16 = jnp.bfloat16
VMEM_LIMIT = 16 << 20

smooth_width = 0.1
leak_slope = 0.1


def leaky(pre):
    return jnp.where(pre > 0, pre, leak_slope * pre).astype(BF16)


def fold_rows(x):
    x = jnp.sum(x.reshape(-1, 8, x.shape[1]), axis=0)
    return sum(x[:, at : at + 128] for at in range(0, x.shape[1], 128))


def difference_terms(real, fake):
    difference = real.astype(F32) - fake.astype(F32)
    root = jnp.sqrt(difference * difference + smooth_width * smooth_width)
    return difference, root


def dot(a, b):
    return jnp.dot(a, b, preferred_element_type=F32)


def dot_rows(a, b):
    return lax.dot_general(a, b, (((0,), (0,)), ((), ())), preferred_element_type=F32)


def dot_lanes(a, b):
    return lax.dot_general(a, b, (((1,), (1,)), ((), ())), preferred_element_type=F32)


def losses_split(first, second):
    value = jnp.sum(jnp.concatenate([first, second], axis=1), axis=0, keepdims=True)
    return split_rows(value, 0)


def split_rows(value, base):
    row = lax.broadcasted_iota(jnp.int32, (8, value.shape[1]), 0) - base
    high = value.astype(BF16).astype(F32)
    middle = (value - high).astype(BF16).astype(F32)
    low = value - high - middle
    out = jnp.where(row == 0, high, jnp.where(row == 1, middle, jnp.where(row == 2, low, 0.0)))
    return out.astype(BF16)


def strided_conv(take, cols, span, w, h_out, phases_out, loss, padded, phases, out_sem):
    frames = span // 3
    rows = 2 * cols * frames
    width = w.shape[2]
    row = lax.broadcasted_iota(jnp.int32, (span, span), 0)
    col = lax.broadcasted_iota(jnp.int32, (span, span), 1)
    phase = jnp.where(row >= 2 * frames, 2, jnp.where(row >= frames, 1, 0))
    select = (col == 3 * (row - frames * phase) + phase).astype(F32).astype(BF16)
    for n in range(2 * cols):
        parts = dot(select, take(n)).astype(BF16)
        for p in range(3):
            phases[p, n * frames : (n + 1) * frames, :] = parts[p * frames : (p + 1) * frames]
    copy_out = pltpu.make_async_copy(phases, phases_out, out_sem)
    copy_out.start()
    padded[:, :8, :] = jnp.zeros((2 * cols, 8, width), F32)
    earlier = dot(phases[1], w[0]) + dot(phases[2], w[1])
    padded[:, 8 : 8 + frames, :] = earlier.reshape(2 * cols, frames, width)
    same = dot(phases[0], w[2]) + dot(phases[1], w[3]) + dot(phases[2], w[4])
    h = leaky(same + padded[:, 7 : 7 + frames, :].reshape(rows, width))
    h_out[...] = h
    _, root = difference_terms(h[: rows // 2], h[rows // 2 :])
    loss[...] = fold_rows(root - smooth_width)
    copy_out.wait()


def first_early_kernel(
    real, fake, w_hbm, h_out, phases_out, loss, w, rest,
    padded, phases, out_sem, held, held_sem, rest_sem, w_sem,
):
    cols = held.shape[0] // 2
    span = held.shape[1]
    for n in range(2 * cols):
        source = real if n < cols else fake
        pltpu.make_async_copy(source.at[n % cols], held.at[n], held_sem.at[n]).start()
    w_copy = pltpu.make_async_copy(w_hbm, w, w_sem)
    w_copy.start()
    rest_copies = [
        pltpu.make_async_copy(x.at[cols:], rest.at[at * cols : (at + 1) * cols], rest_sem.at[at])
        for at, x in enumerate((real, fake))
    ]
    for copy in rest_copies:
        copy.start()

    def take(n):
        source = real if n < cols else fake
        pltpu.make_async_copy(source.at[n % cols], held.at[n], held_sem.at[n]).wait()
        if n == 2 * cols - 1:
            w_copy.wait()
        return held[n]

    strided_conv(take, cols, span, w, h_out, phases_out, loss, padded, phases, out_sem)
    for copy in rest_copies:
        copy.wait()


def first_late_kernel(
    rest, w, w_next_hbm, h_out, phases_out, loss, w_next, padded, phases, out_sem, sem
):
    copy = pltpu.make_async_copy(w_next_hbm, w_next, sem)
    copy.start()
    cols, span = rest.shape[0] // 2, rest.shape[1]
    strided_conv(
        lambda n: rest[n], cols, span, w, h_out, phases_out, loss, padded, phases, out_sem
    )
    copy.wait()


def second_kernel(
    normaliser, whole, s_ref, own, prev, following, far, w, loss_first,
    all_out, shifted_out, far_t, loss, *rest,
):
    *backs, h_all, shifted, padded, in_sems, all_sem, shifted_sem = rest
    rows, width = own.shape
    half = rows // 2
    taps = w.shape[0]
    frames = padded.shape[1] - 16
    s = s_ref[0]
    copies = []
    for away, x in enumerate((own, following, far, prev)):
        at = pl.multiple_of(lax.rem(s + away, 4) * width, 256)
        copies.append(
            pltpu.make_async_copy(x, h_all.at[:, pl.ds(at, width)], in_sems.at[away])
        )
        copies[-1].start()
    for copy in copies:
        copy.wait()
    copy_all = pltpu.make_async_copy(h_all, all_out, all_sem)
    copy_all.start()
    zeros = jnp.zeros((padded.shape[0], 8, width), F32)
    padded[:, :8, :] = zeros
    padded[:, 8 + frames :, :] = zeros
    pre = dot(h_all[...], w[2])
    for k in (0, 1, 3, 4):
        padded[:, 8 : 8 + frames, :] = dot(h_all[...], w[k]).reshape(-1, frames, width)
        pre = pre + padded[:, 6 + k : 6 + k + frames, :].reshape(rows, width)
    h = leaky(pre)
    difference, root = difference_terms(h[:half], h[half:])
    loss_rows = losses_split(loss_first[...], fold_rows(root - smooth_width))
    loss[...] = loss_rows
    slope = difference / root / normaliser
    for value, sign, at in ((h[:half], 1.0, 0), (h[half:], -1.0, half // frames)):
        gate = jnp.where(value.astype(F32) > 0, 1.0, leak_slope)
        delta = (sign * slope * gate).astype(BF16).astype(F32)
        padded[at : at + half // frames, 8 : 8 + frames, :] = delta.reshape(-1, frames, width)
    for k in range(taps):
        moved = padded[:, 10 - k : 10 - k + frames, :].reshape(rows, width)
        shifted[:, k * width : (k + 1) * width] = moved.astype(BF16)
    copy_shifted = pltpu.make_async_copy(shifted, shifted_out, shifted_sem)
    copy_shifted.start()
    far_t[:rows] = back_term(s, 2, shifted, w)
    far_t[rows:] = loss_rows
    if whole:
        back_rest(s, shifted, w, loss_rows, 3, *backs)
    copy_all.wait()
    copy_shifted.wait()


def back_term(s, away, shifted, w):
    width = w.shape[2]
    at = pl.multiple_of(lax.rem(s + away, 4) * width, 256)
    term = None
    for k in range(w.shape[0]):
        part = dot_lanes(shifted[:, k * width : (k + 1) * width], w[k, pl.ds(at, width), :])
        term = part if term is None else term + part
    return term.astype(BF16)


def back_rest(s, shifted, w, loss_rows, with_loss, following, prev, own):
    rows = own.shape[0]
    for away, out in ((1, following), (3, prev)) if with_loss == 1 else ((3, prev), (1, following)):
        out[:rows] = back_term(s, away, shifted, w)
        out[rows:] = loss_rows if away == with_loss else jnp.zeros_like(loss_rows)
    own[...] = back_term(s, 0, shifted, w)


def back_kernel(s_ref, shifted_hbm, w, loss, following, prev, own, shifted, sem):
    copy = pltpu.make_async_copy(shifted_hbm, shifted, sem)
    copy.start()
    copy.wait()
    back_rest(s_ref[0], shifted, w, loss[...], 1, following, prev, own)


def add_kernel(a, b, out):
    out[...] = (a[...].astype(F32) + b[...].astype(F32)).astype(BF16)


def put(g, c, outs, at, rows, k):
    count = g.shape[0] // (2 * rows)
    g = g.astype(BF16).reshape(count, 2, rows, g.shape[1])
    even, odd = g[:, 0], g[:, 1]
    mine, theirs = outs
    mine[at : at + count, k * rows : (k + 1) * rows] = jnp.where(c == 0, even, odd)
    theirs[at : at + count, k * rows : (k + 1) * rows] = jnp.where(c == 0, odd, even)


def weight_second_kernel(
    taps, c_ref, h_a, h_b, shifted_a, shifted_b, mine, theirs, h_all, shifted, h_sem, shifted_sem
):
    own_rows, width = mine.shape[1] // taps, mine.shape[2]
    rows = h_a.shape[0]
    c = c_ref[0]
    step = 256
    count = h_all.shape[1] // step
    moves = []
    for n, x in enumerate((shifted_a, shifted_b)):
        moves.append(
            pltpu.make_async_copy(x, shifted.at[n * rows : (n + 1) * rows], shifted_sem.at[n])
        )
    parts = []
    for q in range(count):
        for n, x in enumerate((h_a, h_b)):
            cut = slice(q * step, (q + 1) * step)
            parts.append(
                pltpu.make_async_copy(
                    x.at[:, cut], h_all.at[n * rows : (n + 1) * rows, cut], h_sem.at[2 * q + n]
                )
            )
    for copy in moves + parts:
        copy.start()
    for copy in moves:
        copy.wait()
    for q in range(count):
        parts[2 * q].wait()
        parts[2 * q + 1].wait()
        g = dot_rows(h_all[:, q * step : (q + 1) * step], shifted[...])
        for k in range(taps):
            put(g[:, k * width : (k + 1) * width], c, (mine, theirs),
                q * step // (2 * own_rows), own_rows, k)


def weight_first_kernel(
    normaliser, taps, c_ref, loss_a, loss_b, *refs,
):
    *sources, phases_a, phases_b, mine, theirs, padded, moved, got, phases, sems, phase_sems = refs
    rows, width = sources[0].shape
    half = rows // 2
    frames = padded.shape[1] - 8
    c = c_ref[0]
    copies = []
    for n, x in enumerate(sources):
        copies.append(pltpu.make_async_copy(x, got.at[n, : x.shape[0]], sems.at[n]))
    phase_copies = []
    for p in range(3):
        for n, x in enumerate((phases_a, phases_b)):
            phase_copies.append(
                pltpu.make_async_copy(
                    x.at[p], phases.at[p, n * rows : (n + 1) * rows], phase_sems.at[2 * p + n]
                )
            )
    for copy in copies + phase_copies:
        copy.start()
    for copy in copies:
        copy.wait()
    padded[:, frames:, :] = jnp.zeros((padded.shape[0], 8, width), F32)
    for n in range(2):
        h, own, a, b = (got.at[2 * at + n] for at in range(4))
        difference, root = difference_terms(h[:half], h[half:rows])
        slope = difference / root / normaliser
        for at, sign in ((0, 1.0), (half, -1.0)):
            cut = slice(at, at + half)
            up = own[cut].astype(F32) + a[cut].astype(F32) + b[cut].astype(F32)
            up = up.astype(BF16).astype(F32)
            gate = jnp.where(h[cut].astype(F32) > 0, 1.0, leak_slope)
            delta = ((sign * slope + up) * gate).astype(BF16)
            base = n * rows + at
            moved[base : base + half, :width] = delta
            cols, lead = half // frames, base // frames
            padded[lead : lead + cols, :frames, :] = delta.astype(F32).reshape(cols, frames, width)
    moved[:, width:] = padded[:, 1 : 1 + frames, :].reshape(2 * rows, width).astype(BF16)
    groups = mine.shape[0]
    own_rows = (mine.shape[1] - 8) // taps
    outs = (mine, theirs)
    for p in range(3):
        phase_copies[2 * p].wait()
        phase_copies[2 * p + 1].wait()
        if p == 0:
            put(dot_rows(phases[p], moved[:, :width]), c, outs, 0, own_rows, 2)
        else:
            g = dot_rows(phases[p], moved[...])
            put(g[:, :width], c, outs, 0, own_rows, 2 + p)
            put(g[:, width:], c, outs, 0, own_rows, p - 1)
    total = loss_a[...].astype(F32) + loss_b[...].astype(F32)
    for at in range(4, 10):
        total = total + got[at, rows:].astype(F32)
    lines = split_rows(jnp.sum(total, axis=0, keepdims=True), 3 * c)
    for x in outs:
        x[:, taps * own_rows :, :] = jnp.broadcast_to(lines[None], (groups, 8, width))


def total_kernel(taps, blocks, out):
    total = jnp.sum(blocks[...].astype(F32), axis=0)
    out[...] = total.reshape(taps, -1, total.shape[1])


def total_loss_kernel(taps, count_all, blocks, out, loss):
    rows = out.shape[1]
    total = jnp.sum(blocks[...].astype(F32), axis=0)
    out[...] = total[: taps * rows].reshape(taps, rows, -1)
    lines = total[taps * rows :]
    loss[0] = jnp.sum(lines[:, :128]) / count_all
    loss[1] = jnp.sum(lines[:, 128:]) / count_all


def call(
    kernel, operands, outs, scratch=(), smem=0, hbm=(), loose=(), after=(), smem_outs=(),
    hbm_outs=(), flops=0, cost=1, name=None,
):
    moved = sum(x.size * x.dtype.itemsize for x in operands)
    moved += sum(x.size * x.dtype.itemsize for x in outs)
    vmem, small = pl.BlockSpec(memory_space=pltpu.VMEM), pl.BlockSpec(memory_space=pltpu.SMEM)
    far, anywhere = pl.BlockSpec(memory_space=pltpu.HBM), pl.BlockSpec(memory_space=pl.ANY)
    count = len(operands)
    operands = tuple(
        pltpu.with_memory_space_constraint(x, pltpu.HBM) if at in hbm else x
        for at, x in enumerate(operands)
    )

    def body(*refs):
        kernel(*refs[:count], *refs[count + len(after) :])

    return pl.pallas_call(
        body,
        out_shape=[
            pltpu.HBM(x.shape, x.dtype) if at in hbm_outs else x for at, x in enumerate(outs)
        ],
        in_specs=[
            small if at < smem else far if at in hbm else anywhere if at in loose else vmem
            for at in range(count)
        ]
        + [anywhere] * len(after),
        out_specs=[
            small if at in smem_outs else far if at in hbm_outs else vmem
            for at in range(len(outs))
        ],
        scratch_shapes=list(scratch),
        compiler_params=pltpu.CompilerParams(vmem_limit_bytes=VMEM_LIMIT),
        cost_estimate=pl.CostEstimate(
            flops=int(flops * cost), bytes_accessed=int(moved * cost), transcendentals=0
        ),
        name=name,
    )(*operands, *after)


def like(shape, dtype=BF16):
    return jax.ShapeDtypeStruct(shape, dtype)


def turn(x, step):
    count = lax.axis_size("section")
    return lax.ppermute(x, "section", [(i, (i + step) % count) for i in range(count)])


def added(a, b, name, after=()):
    return call(add_kernel, (a, b), [like(a.shape)], after=after, name=name)[0]


def other_core(x):
    return lax.ppermute(x, "dp_2", [(0, 1), (1, 0)])


def shards(real_in, fake_in, kernel_first, kernel_second):
    replicas = lax.axis_size(DP)
    cols, span, in_width = real_in.shape
    frames = span // 3
    taps, width_all, width = kernel_second.shape
    normaliser = float(cols * frames)
    count_all = float(cols * replicas * frames * width_all)
    groups = replicas // 2
    part = cols // 2
    rows = cols * frames
    s = lax.axis_index("section").reshape(1).astype(jnp.int32)
    c = lax.axis_index("dp_2").reshape(1).astype(jnp.int32)
    dma = pltpu.SemaphoreType.DMA
    chunk_outs = [like((rows, width)), like((3, rows, in_width)), like((8, 128), F32)]
    conv_scratch = [
        pltpu.VMEM((cols, frames + 8, width), F32), pltpu.VMEM((3, rows, in_width), BF16), dma
    ]
    flops = 2 * rows * taps * in_width * width

    h_a, phases_a, loss_a, w_first, rest = call(
        first_early_kernel,
        (real_in, fake_in, kernel_first),
        chunk_outs + [like(kernel_first.shape), like((cols, span, in_width))],
        conv_scratch
        + [pltpu.VMEM((cols, span, in_width), BF16), dma((cols,)), dma((2,)), dma],
        hbm=(0, 1, 2),
        hbm_outs=(1,),
        flops=flops,
        name="first_a",
    )
    prev_a = turn(h_a, 1)
    following_a = turn(h_a, -1)
    h_b, phases_b, loss_b, w_second = call(
        first_late_kernel,
        (rest, w_first, kernel_second),
        chunk_outs + [like(kernel_second.shape)],
        conv_scratch + [dma],
        hbm=(2,),
        hbm_outs=(1,),
        flops=flops,
        cost=1,
        name="first_b",
    )
    far_a = turn(prev_a, 1)
    following_b = turn(h_b, -1)
    prev_b = turn(h_b, 1)
    far_b = turn(following_b, -1)

    second_outs = [like((rows, width_all)), like((rows, taps * width)), like((rows + 8, width)),
                   like((8, width))]
    back_outs = [like((rows + 8, width)), like((rows + 8, width)), like((rows, width))]
    second_scratch = [
        pltpu.VMEM((rows, width_all), BF16), pltpu.VMEM((rows, taps * width), BF16),
        pltpu.VMEM((cols, frames + 16, width), F32), dma((4,)), dma, dma,
    ]
    flops = 2 * rows * taps * (width_all + width) * width
    all_a, shifted_a, far_t, loss_a, next_t, prev_t, own_a = call(
        functools.partial(second_kernel, normaliser, True),
        (s, h_a, prev_a, following_a, far_a, w_second, loss_a),
        second_outs + back_outs,
        second_scratch,
        smem=1,
        loose=(1, 2, 3, 4),
        hbm_outs=(0, 1),
        cost=1,
        flops=flops,
        name="second_a",
    )
    pass_a = turn(far_t, 1)
    from_following_a = turn(prev_t, -1)
    relayed_a = added(next_t, pass_a, "relay_a")
    from_prev_a = turn(relayed_a, 1)

    all_b, shifted_b, far_t, loss_b = call(
        functools.partial(second_kernel, normaliser, False),
        (s, h_b, prev_b, following_b, far_b, w_second, loss_b),
        second_outs,
        second_scratch,
        smem=1,
        loose=(1, 2, 3, 4),
        hbm_outs=(0, 1),
        cost=1,
        after=(own_a,),
        flops=flops,
        name="second_b",
    )
    pass_b = turn(far_t, -1)
    next_t, prev_t, own_b = call(
        back_kernel,
        (s, shifted_b, w_second, loss_b),
        back_outs,
        [pltpu.VMEM((rows, taps * width), BF16), dma],
        smem=1,
        hbm=(1,),
        cost=4,
        flops=2 * rows * taps * width * width * 3,
        name="back_b",
    )
    from_prev_b = turn(next_t, 1)
    relayed_b = added(prev_t, pass_b, "relay_b")
    from_following_b = turn(relayed_b, -1)

    own_rows = width_all // replicas
    mine_second, theirs = call(
        functools.partial(weight_second_kernel, taps),
        (c, all_a, all_b, shifted_a, shifted_b),
        [like((groups, taps * own_rows, width))] * 2,
        [pltpu.VMEM((2 * rows, width_all), BF16), pltpu.VMEM((2 * rows, taps * width), BF16),
         dma((2 * width_all // 256,)), dma((2,))],
        smem=1,
        hbm=(1, 2, 3, 4),
        cost=4,
        after=(relayed_a, relayed_b),
        flops=4 * rows * taps * width * width_all,
        name="weight_second",
    )
    theirs_second = other_core(theirs)

    first_rows = in_width // replicas
    mine_first, theirs = call(
        functools.partial(weight_first_kernel, normaliser, taps),
        (c, loss_a, loss_b, h_a, h_b, own_a, own_b, from_prev_a, from_prev_b, from_following_a,
         from_following_b, pass_a, pass_b, phases_a, phases_b),
        [like((groups, taps * first_rows + 8, width))] * 2,
        [pltpu.VMEM((2 * cols, frames + 8, width), F32), pltpu.VMEM((2 * rows, 2 * width), BF16),
         pltpu.VMEM((10, rows + 8, width), BF16), pltpu.VMEM((3, 2 * rows, in_width), BF16),
         dma((10,)), dma((6,))],
        smem=1,
        hbm=(13, 14),
        loose=tuple(range(3, 13)),
        cost=20,
        after=(mine_second,),
        flops=4 * rows * taps * width * in_width,
        name="weight_first",
    )
    theirs_first = other_core(theirs)
    summed_second = added(mine_second, theirs_second, "core_second", (mine_first,))
    blocks_second = lax.all_to_all(summed_second, ZY, 0, 0)
    summed_first = added(mine_first, theirs_first, "core_first", (summed_second,))
    blocks_first = lax.all_to_all(summed_first, ZY, 0, 0)

    (grad_second,) = call(
        functools.partial(total_kernel, taps),
        (blocks_second,),
        [like((taps, own_rows, width), F32)],
        name="total_second",
    )
    grad_first, layer_loss = call(
        functools.partial(total_loss_kernel, taps, count_all),
        (blocks_first,),
        [like((taps, first_rows, width), F32), like((2,), F32)],
        smem_outs=(1,),
        name="total_first",
    )
    return (layer_loss, jnp.transpose(grad_first, (1, 0, 2)), jnp.transpose(grad_second, (1, 0, 2)))


def solution(mesh):
    finer = Mesh(
        mesh.devices.reshape(4, 4, 2, mesh.shape["section"]), ("dp_0", "dp_1", "dp_2", "section")
    )
    return jax.shard_map(
        shards,
        mesh=finer,
        in_specs=(
            P(DP, None, None),
            P(DP, None, None),
            P(None, None, "section"),
            P(None, None, "section"),
        ),
        out_specs=(P(), P(DP, None, "section"), P(DP, None, "section")),
        check_vma=False,
    )
```

```python
import functools

import jax
import jax.numpy as jnp
from jax import lax
from jax.experimental import pallas as pl
from jax.experimental.pallas import tpu as pltpu
from jax.sharding import Mesh
from jax.sharding import PartitionSpec as P

DP = ("dp_0", "dp_1", "dp_2")
ZY = ("dp_0", "dp_1")
F32 = jnp.float32
BF16 = jnp.bfloat16
VMEM_LIMIT = 16 << 20

smooth_width = 0.1
leak_slope = 0.1


def leaky(pre):
    return jnp.where(pre > 0, pre, leak_slope * pre).astype(BF16)


def fold_rows(x):
    x = jnp.sum(x.reshape(-1, 8, x.shape[1]), axis=0)
    return sum(x[:, at : at + 128] for at in range(0, x.shape[1], 128))


def difference_terms(real, fake):
    difference = real.astype(F32) - fake.astype(F32)
    root = jnp.sqrt(difference * difference + smooth_width * smooth_width)
    return difference, root


def dot(a, b):
    return jnp.dot(a, b, preferred_element_type=F32)


def dot_rows(a, b):
    return lax.dot_general(a, b, (((0,), (0,)), ((), ())), preferred_element_type=F32)


def dot_lanes(a, b):
    return lax.dot_general(a, b, (((1,), (1,)), ((), ())), preferred_element_type=F32)


def losses_split(first, second):
    value = jnp.sum(jnp.concatenate([first, second], axis=1), axis=0, keepdims=True)
    return split_rows(value, 0)


def split_rows(value, base):
    row = lax.broadcasted_iota(jnp.int32, (8, value.shape[1]), 0) - base
    high = value.astype(BF16).astype(F32)
    middle = (value - high).astype(BF16).astype(F32)
    low = value - high - middle
    out = jnp.where(row == 0, high, jnp.where(row == 1, middle, jnp.where(row == 2, low, 0.0)))
    return out.astype(BF16)


def strided_conv(take, cols, span, w, h_out, phases_out, loss, padded, phases, out_sem):
    frames = span // 3
    rows = 2 * cols * frames
    width = w.shape[2]
    row = lax.broadcasted_iota(jnp.int32, (span, span), 0)
    col = lax.broadcasted_iota(jnp.int32, (span, span), 1)
    phase = jnp.where(row >= 2 * frames, 2, jnp.where(row >= frames, 1, 0))
    select = (col == 3 * (row - frames * phase) + phase).astype(F32).astype(BF16)
    for n in range(2 * cols):
        parts = dot(select, take(n)).astype(BF16)
        for p in range(3):
            phases[p, n * frames : (n + 1) * frames, :] = parts[p * frames : (p + 1) * frames]
    copy_out = pltpu.make_async_copy(phases, phases_out, out_sem)
    copy_out.start()
    padded[:, :8, :] = jnp.zeros((2 * cols, 8, width), F32)
    earlier = dot(phases[1], w[0]) + dot(phases[2], w[1])
    padded[:, 8 : 8 + frames, :] = earlier.reshape(2 * cols, frames, width)
    same = dot(phases[0], w[2]) + dot(phases[1], w[3]) + dot(phases[2], w[4])
    h = leaky(same + padded[:, 7 : 7 + frames, :].reshape(rows, width))
    h_out[...] = h
    _, root = difference_terms(h[: rows // 2], h[rows // 2 :])
    loss[...] = fold_rows(root - smooth_width)
    copy_out.wait()


def first_early_kernel(
    real, fake, w_hbm, h_out, phases_out, loss, w, rest,
    padded, phases, out_sem, held, held_sem, rest_sem, w_sem,
):
    cols = held.shape[0] // 2
    span = held.shape[1]
    for n in range(2 * cols):
        source = real if n < cols else fake
        pltpu.make_async_copy(source.at[n % cols], held.at[n], held_sem.at[n]).start()
    w_copy = pltpu.make_async_copy(w_hbm, w, w_sem)
    w_copy.start()
    rest_copies = [
        pltpu.make_async_copy(x.at[cols:], rest.at[at * cols : (at + 1) * cols], rest_sem.at[at])
        for at, x in enumerate((real, fake))
    ]
    for copy in rest_copies:
        copy.start()

    def take(n):
        source = real if n < cols else fake
        pltpu.make_async_copy(source.at[n % cols], held.at[n], held_sem.at[n]).wait()
        if n == 2 * cols - 1:
            w_copy.wait()
        return held[n]

    strided_conv(take, cols, span, w, h_out, phases_out, loss, padded, phases, out_sem)
    for copy in rest_copies:
        copy.wait()


def first_late_kernel(
    rest, w, w_next_hbm, h_out, phases_out, loss, w_next, padded, phases, out_sem, sem
):
    copy = pltpu.make_async_copy(w_next_hbm, w_next, sem)
    copy.start()
    cols, span = rest.shape[0] // 2, rest.shape[1]
    strided_conv(
        lambda n: rest[n], cols, span, w, h_out, phases_out, loss, padded, phases, out_sem
    )
    copy.wait()


def second_kernel(
    normaliser, whole, s_ref, own, prev, following, far, w, loss_first,
    all_out, shifted_out, far_t, loss, *rest,
):
    *backs, h_all, shifted, padded, in_sems, all_sem, shifted_sem = rest
    rows, width = own.shape
    half = rows // 2
    taps = w.shape[0]
    frames = padded.shape[1] - 16
    s = s_ref[0]
    copies = []
    for away, x in enumerate((own, following, far, prev)):
        at = pl.multiple_of(lax.rem(s + away, 4) * width, 256)
        copies.append(
            pltpu.make_async_copy(x, h_all.at[:, pl.ds(at, width)], in_sems.at[away])
        )
        copies[-1].start()
    for copy in copies:
        copy.wait()
    copy_all = pltpu.make_async_copy(h_all, all_out, all_sem)
    copy_all.start()
    zeros = jnp.zeros((padded.shape[0], 8, width), F32)
    padded[:, :8, :] = zeros
    padded[:, 8 + frames :, :] = zeros
    pre = dot(h_all[...], w[2])
    for k in (0, 1, 3, 4):
        padded[:, 8 : 8 + frames, :] = dot(h_all[...], w[k]).reshape(-1, frames, width)
        pre = pre + padded[:, 6 + k : 6 + k + frames, :].reshape(rows, width)
    h = leaky(pre)
    difference, root = difference_terms(h[:half], h[half:])
    loss_rows = losses_split(loss_first[...], fold_rows(root - smooth_width))
    loss[...] = loss_rows
    slope = difference / root / normaliser
    for value, sign, at in ((h[:half], 1.0, 0), (h[half:], -1.0, half // frames)):
        gate = jnp.where(value.astype(F32) > 0, 1.0, leak_slope)
        delta = (sign * slope * gate).astype(BF16).astype(F32)
        padded[at : at + half // frames, 8 : 8 + frames, :] = delta.reshape(-1, frames, width)
    for k in range(taps):
        moved = padded[:, 10 - k : 10 - k + frames, :].reshape(rows, width)
        shifted[:, k * width : (k + 1) * width] = moved.astype(BF16)
    copy_shifted = pltpu.make_async_copy(shifted, shifted_out, shifted_sem)
    copy_shifted.start()
    far_t[:rows] = back_term(s, 2, shifted, w)
    far_t[rows:] = loss_rows
    if whole:
        back_rest(s, shifted, w, loss_rows, 3, *backs)
    copy_all.wait()
    copy_shifted.wait()


def back_term(s, away, shifted, w):
    width = w.shape[2]
    at = pl.multiple_of(lax.rem(s + away, 4) * width, 256)
    term = None
    for k in range(w.shape[0]):
        part = dot_lanes(shifted[:, k * width : (k + 1) * width], w[k, pl.ds(at, width), :])
        term = part if term is None else term + part
    return term.astype(BF16)


def back_rest(s, shifted, w, loss_rows, with_loss, following, prev, own):
    rows = own.shape[0]
    for away, out in ((1, following), (3, prev)) if with_loss == 1 else ((3, prev), (1, following)):
        out[:rows] = back_term(s, away, shifted, w)
        out[rows:] = loss_rows if away == with_loss else jnp.zeros_like(loss_rows)
    own[...] = back_term(s, 0, shifted, w)


def back_kernel(s_ref, shifted_hbm, w, loss, following, prev, own, shifted, sem):
    copy = pltpu.make_async_copy(shifted_hbm, shifted, sem)
    copy.start()
    copy.wait()
    back_rest(s_ref[0], shifted, w, loss[...], 1, following, prev, own)


def add_kernel(a, b, out):
    out[...] = (a[...].astype(F32) + b[...].astype(F32)).astype(BF16)


def put(g, c, outs, at, rows, k):
    count = g.shape[0] // (2 * rows)
    g = g.astype(BF16).reshape(count, 2, rows, g.shape[1])
    even, odd = g[:, 0], g[:, 1]
    mine, theirs = outs
    mine[at : at + count, k * rows : (k + 1) * rows] = jnp.where(c == 0, even, odd)
    theirs[at : at + count, k * rows : (k + 1) * rows] = jnp.where(c == 0, odd, even)


def weight_second_kernel(
    taps, c_ref, h_a, h_b, shifted_a, shifted_b, mine, theirs, h_all, shifted, h_sem, shifted_sem
):
    own_rows, width = mine.shape[1] // taps, mine.shape[2]
    rows = h_a.shape[0]
    c = c_ref[0]
    step = 256
    count = h_all.shape[1] // step
    moves = []
    for n, x in enumerate((shifted_a, shifted_b)):
        moves.append(
            pltpu.make_async_copy(x, shifted.at[n * rows : (n + 1) * rows], shifted_sem.at[n])
        )
    parts = []
    for q in range(count):
        for n, x in enumerate((h_a, h_b)):
            cut = slice(q * step, (q + 1) * step)
            parts.append(
                pltpu.make_async_copy(
                    x.at[:, cut], h_all.at[n * rows : (n + 1) * rows, cut], h_sem.at[2 * q + n]
                )
            )
    for copy in moves + parts:
        copy.start()
    for copy in moves:
        copy.wait()
    for q in range(count):
        parts[2 * q].wait()
        parts[2 * q + 1].wait()
        g = dot_rows(h_all[:, q * step : (q + 1) * step], shifted[...])
        for k in range(taps):
            put(g[:, k * width : (k + 1) * width], c, (mine, theirs),
                q * step // (2 * own_rows), own_rows, k)


def weight_first_kernel(
    normaliser, taps, c_ref, loss_a, loss_b, *refs,
):
    *sources, phases_a, phases_b, mine, theirs, padded, moved, got, phases, sems, phase_sems = refs
    rows, width = sources[0].shape
    half = rows // 2
    frames = padded.shape[1] - 8
    c = c_ref[0]
    copies = []
    for n, x in enumerate(sources):
        copies.append(pltpu.make_async_copy(x, got.at[n, : x.shape[0]], sems.at[n]))
    phase_copies = []
    for p in range(3):
        for n, x in enumerate((phases_a, phases_b)):
            phase_copies.append(
                pltpu.make_async_copy(
                    x.at[p], phases.at[p, n * rows : (n + 1) * rows], phase_sems.at[2 * p + n]
                )
            )
    for copy in copies + phase_copies:
        copy.start()
    for copy in copies:
        copy.wait()
    padded[:, frames:, :] = jnp.zeros((padded.shape[0], 8, width), F32)
    for n in range(2):
        h, own, a, b = (got.at[2 * at + n] for at in range(4))
        difference, root = difference_terms(h[:half], h[half:rows])
        slope = difference / root / normaliser
        for at, sign in ((0, 1.0), (half, -1.0)):
            cut = slice(at, at + half)
            up = own[cut].astype(F32) + a[cut].astype(F32) + b[cut].astype(F32)
            up = up.astype(BF16).astype(F32)
            gate = jnp.where(h[cut].astype(F32) > 0, 1.0, leak_slope)
            delta = ((sign * slope + up) * gate).astype(BF16)
            base = n * rows + at
            moved[base : base + half, :width] = delta
            cols, lead = half // frames, base // frames
            padded[lead : lead + cols, :frames, :] = delta.astype(F32).reshape(cols, frames, width)
    moved[:, width:] = padded[:, 1 : 1 + frames, :].reshape(2 * rows, width).astype(BF16)
    groups = mine.shape[0]
    own_rows = (mine.shape[1] - 8) // taps
    outs = (mine, theirs)
    for p in range(3):
        phase_copies[2 * p].wait()
        phase_copies[2 * p + 1].wait()
        if p == 0:
            put(dot_rows(phases[p], moved[:, :width]), c, outs, 0, own_rows, 2)
        else:
            g = dot_rows(phases[p], moved[...])
            put(g[:, :width], c, outs, 0, own_rows, 2 + p)
            put(g[:, width:], c, outs, 0, own_rows, p - 1)
    total = loss_a[...].astype(F32) + loss_b[...].astype(F32)
    for at in range(4, 10):
        total = total + got[at, rows:].astype(F32)
    lines = split_rows(jnp.sum(total, axis=0, keepdims=True), 3 * c)
    for x in outs:
        x[:, taps * own_rows :, :] = jnp.broadcast_to(lines[None], (groups, 8, width))


def join_kernel(at, a, b, joint, summed, sem):
    summed[...] = (a[...].astype(F32) + b[...].astype(F32)).astype(BF16)
    copy = pltpu.make_async_copy(summed, joint.at[:, at : at + summed.shape[1]], sem)
    copy.start()
    copy.wait()


def join_late_kernel(at, a, b, held, joint, summed, sem):
    del held
    join_kernel(at, a, b, joint, summed, sem)


def total_kernel(taps, count_all, blocks, second, first, loss):
    total = jnp.sum(blocks[...].astype(F32), axis=0)
    at = 0
    for out in (second, first):
        rows = taps * out.shape[1]
        out[...] = total[at : at + rows].reshape(out.shape)
        at += rows
    lines = total[at:]
    loss[0] = jnp.sum(lines[:, :128]) / count_all
    loss[1] = jnp.sum(lines[:, 128:]) / count_all


def call(
    kernel, operands, outs, scratch=(), smem=0, hbm=(), loose=(), after=(), smem_outs=(),
    hbm_outs=(), aliases={}, flops=0, cost=1, name=None,
):
    moved = sum(x.size * x.dtype.itemsize for x in operands)
    moved += sum(x.size * x.dtype.itemsize for x in outs)
    vmem, small = pl.BlockSpec(memory_space=pltpu.VMEM), pl.BlockSpec(memory_space=pltpu.SMEM)
    far, anywhere = pl.BlockSpec(memory_space=pltpu.HBM), pl.BlockSpec(memory_space=pl.ANY)
    count = len(operands)
    operands = tuple(
        pltpu.with_memory_space_constraint(x, pltpu.HBM) if at in hbm else x
        for at, x in enumerate(operands)
    )

    def body(*refs):
        kernel(*refs[:count], *refs[count + len(after) :])

    return pl.pallas_call(
        body,
        out_shape=[
            pltpu.HBM(x.shape, x.dtype) if at in hbm_outs else x for at, x in enumerate(outs)
        ],
        in_specs=[
            small if at < smem else far if at in hbm else anywhere if at in loose else vmem
            for at in range(count)
        ]
        + [anywhere] * len(after),
        out_specs=[
            small if at in smem_outs else far if at in hbm_outs else vmem
            for at in range(len(outs))
        ],
        scratch_shapes=list(scratch),
        input_output_aliases=aliases,
        compiler_params=pltpu.CompilerParams(vmem_limit_bytes=VMEM_LIMIT),
        cost_estimate=pl.CostEstimate(
            flops=int(flops * cost), bytes_accessed=int(moved * cost), transcendentals=0
        ),
        name=name,
    )(*operands, *after)


def like(shape, dtype=BF16):
    return jax.ShapeDtypeStruct(shape, dtype)


def turn(x, step):
    count = lax.axis_size("section")
    return lax.ppermute(x, "section", [(i, (i + step) % count) for i in range(count)])


def added(a, b, name, after=()):
    return call(add_kernel, (a, b), [like(a.shape)], after=after, name=name)[0]


def other_core(x):
    return lax.ppermute(x, "dp_2", [(0, 1), (1, 0)])


def shards(real_in, fake_in, kernel_first, kernel_second):
    replicas = lax.axis_size(DP)
    cols, span, in_width = real_in.shape
    frames = span // 3
    taps, width_all, width = kernel_second.shape
    normaliser = float(cols * frames)
    count_all = float(cols * replicas * frames * width_all)
    groups = replicas // 2
    part = cols // 2
    rows = cols * frames
    s = lax.axis_index("section").reshape(1).astype(jnp.int32)
    c = lax.axis_index("dp_2").reshape(1).astype(jnp.int32)
    dma = pltpu.SemaphoreType.DMA
    chunk_outs = [like((rows, width)), like((3, rows, in_width)), like((8, 128), F32)]
    conv_scratch = [
        pltpu.VMEM((cols, frames + 8, width), F32), pltpu.VMEM((3, rows, in_width), BF16), dma
    ]
    flops = 2 * rows * taps * in_width * width

    h_a, phases_a, loss_a, w_first, rest = call(
        first_early_kernel,
        (real_in, fake_in, kernel_first),
        chunk_outs + [like(kernel_first.shape), like((cols, span, in_width))],
        conv_scratch
        + [pltpu.VMEM((cols, span, in_width), BF16), dma((cols,)), dma((2,)), dma],
        hbm=(0, 1, 2),
        hbm_outs=(1,),
        flops=flops,
        name="first_a",
    )
    prev_a = turn(h_a, 1)
    following_a = turn(h_a, -1)
    h_b, phases_b, loss_b, w_second = call(
        first_late_kernel,
        (rest, w_first, kernel_second),
        chunk_outs + [like(kernel_second.shape)],
        conv_scratch + [dma],
        hbm=(2,),
        hbm_outs=(1,),
        flops=flops,
        cost=1,
        name="first_b",
    )
    far_a = turn(prev_a, 1)
    following_b = turn(h_b, -1)
    prev_b = turn(h_b, 1)
    far_b = turn(following_b, -1)

    second_outs = [like((rows, width_all)), like((rows, taps * width)), like((rows + 8, width)),
                   like((8, width))]
    back_outs = [like((rows + 8, width)), like((rows + 8, width)), like((rows, width))]
    second_scratch = [
        pltpu.VMEM((rows, width_all), BF16), pltpu.VMEM((rows, taps * width), BF16),
        pltpu.VMEM((cols, frames + 16, width), F32), dma((4,)), dma, dma,
    ]
    flops = 2 * rows * taps * (width_all + width) * width
    all_a, shifted_a, far_t, loss_a, next_t, prev_t, own_a = call(
        functools.partial(second_kernel, normaliser, True),
        (s, h_a, prev_a, following_a, far_a, w_second, loss_a),
        second_outs + back_outs,
        second_scratch,
        smem=1,
        loose=(1, 2, 3, 4),
        hbm_outs=(0, 1),
        cost=1,
        flops=flops,
        name="second_a",
    )
    pass_a = turn(far_t, 1)
    from_following_a = turn(prev_t, -1)
    relayed_a = added(next_t, pass_a, "relay_a")
    from_prev_a = turn(relayed_a, 1)

    all_b, shifted_b, far_t, loss_b = call(
        functools.partial(second_kernel, normaliser, False),
        (s, h_b, prev_b, following_b, far_b, w_second, loss_b),
        second_outs,
        second_scratch,
        smem=1,
        loose=(1, 2, 3, 4),
        hbm_outs=(0, 1),
        cost=1,
        after=(own_a,),
        flops=flops,
        name="second_b",
    )
    pass_b = turn(far_t, -1)
    next_t, prev_t, own_b = call(
        back_kernel,
        (s, shifted_b, w_second, loss_b),
        back_outs,
        [pltpu.VMEM((rows, taps * width), BF16), dma],
        smem=1,
        hbm=(1,),
        cost=4,
        flops=2 * rows * taps * width * width * 3,
        name="back_b",
    )
    from_prev_b = turn(next_t, 1)
    relayed_b = added(prev_t, pass_b, "relay_b")
    from_following_b = turn(relayed_b, -1)

    own_rows = width_all // replicas
    mine_second, theirs = call(
        functools.partial(weight_second_kernel, taps),
        (c, all_a, all_b, shifted_a, shifted_b),
        [like((groups, taps * own_rows, width))] * 2,
        [pltpu.VMEM((2 * rows, width_all), BF16), pltpu.VMEM((2 * rows, taps * width), BF16),
         dma((2 * width_all // 256,)), dma((2,))],
        smem=1,
        hbm=(1, 2, 3, 4),
        cost=4,
        after=(relayed_a, relayed_b),
        flops=4 * rows * taps * width * width_all,
        name="weight_second",
    )
    first_rows = in_width // replicas
    size_second, size_first = taps * own_rows, taps * first_rows + 8
    joint_like = like((groups, size_second + size_first, width))
    (joint,) = call(
        functools.partial(join_kernel, 0),
        (mine_second, other_core(theirs)),
        [joint_like],
        [pltpu.VMEM((groups, size_second, width), BF16), dma],
        hbm_outs=(0,),
        name="join_second",
    )

    mine_first, theirs = call(
        functools.partial(weight_first_kernel, normaliser, taps),
        (c, loss_a, loss_b, h_a, h_b, own_a, own_b, from_prev_a, from_prev_b, from_following_a,
         from_following_b, pass_a, pass_b, phases_a, phases_b),
        [like((groups, taps * first_rows + 8, width))] * 2,
        [pltpu.VMEM((2 * cols, frames + 8, width), F32), pltpu.VMEM((2 * rows, 2 * width), BF16),
         pltpu.VMEM((10, rows + 8, width), BF16), pltpu.VMEM((3, 2 * rows, in_width), BF16),
         dma((10,)), dma((6,))],
        smem=1,
        hbm=(13, 14),
        loose=tuple(range(3, 13)),
        cost=20,
        after=(mine_second,),
        flops=4 * rows * taps * width * in_width,
        name="weight_first",
    )
    (joint,) = call(
        functools.partial(join_late_kernel, size_second),
        (mine_first, other_core(theirs), joint),
        [joint_like],
        [pltpu.VMEM((groups, size_first, width), BF16), dma],
        hbm=(2,),
        hbm_outs=(0,),
        aliases={2: 0},
        name="join_first",
    )
    blocks = lax.all_to_all(joint, ZY, 0, 0)
    grad_second, grad_first, layer_loss = call(
        functools.partial(total_kernel, taps, count_all),
        (blocks,),
        [like((taps, own_rows, width), F32), like((taps, first_rows, width), F32),
         like((2,), F32)],
        smem_outs=(2,),
        name="total",
    )
    return (layer_loss, jnp.transpose(grad_first, (1, 0, 2)), jnp.transpose(grad_second, (1, 0, 2)))


def solution(mesh):
    finer = Mesh(
        mesh.devices.reshape(4, 4, 2, mesh.shape["section"]), ("dp_0", "dp_1", "dp_2", "section")
    )
    return jax.shard_map(
        shards,
        mesh=finer,
        in_specs=(
            P(DP, None, None),
            P(DP, None, None),
            P(None, None, "section"),
            P(None, None, "section"),
        ),
        out_specs=(P(), P(DP, None, "section"), P(DP, None, "section")),
        check_vma=False,
    )
```

```python
import functools

import jax
import jax.numpy as jnp
from jax import lax
from jax.experimental import pallas as pl
from jax.experimental.pallas import tpu as pltpu
from jax.sharding import Mesh
from jax.sharding import PartitionSpec as P

DP = ("dp_0", "dp_1", "dp_2")
ZY = ("dp_0", "dp_1")
F32 = jnp.float32
BF16 = jnp.bfloat16
VMEM_LIMIT = 16 << 20
NEAR_PHASES = (False, False)
NEAR_ALL = (True, True)
NEAR_SMALL = True

smooth_width = 0.1
leak_slope = 0.1


def leaky(pre):
    return jnp.where(pre > 0, pre, leak_slope * pre).astype(BF16)


def fold_rows(x):
    x = jnp.sum(x.reshape(-1, 8, x.shape[1]), axis=0)
    return sum(x[:, at : at + 128] for at in range(0, x.shape[1], 128))


def difference_terms(real, fake):
    difference = real.astype(F32) - fake.astype(F32)
    root = jnp.sqrt(difference * difference + smooth_width * smooth_width)
    return difference, root


def dot(a, b):
    return jnp.dot(a, b, preferred_element_type=F32)


def dot_rows(a, b):
    return lax.dot_general(a, b, (((0,), (0,)), ((), ())), preferred_element_type=F32)


def dot_lanes(a, b):
    return lax.dot_general(a, b, (((1,), (1,)), ((), ())), preferred_element_type=F32)


def losses_split(first, second):
    value = jnp.sum(jnp.concatenate([first, second], axis=1), axis=0, keepdims=True)
    return split_rows(value, 0)


def split_rows(value, base):
    row = lax.broadcasted_iota(jnp.int32, (8, value.shape[1]), 0) - base
    high = value.astype(BF16).astype(F32)
    middle = (value - high).astype(BF16).astype(F32)
    low = value - high - middle
    out = jnp.where(row == 0, high, jnp.where(row == 1, middle, jnp.where(row == 2, low, 0.0)))
    return out.astype(BF16)


def strided_conv(take, cols, span, w, h_out, phases_out, loss, padded, *far):
    phases = far[0] if far else phases_out
    frames = span // 3
    rows = 2 * cols * frames
    width = w.shape[2]
    row = lax.broadcasted_iota(jnp.int32, (span, span), 0)
    col = lax.broadcasted_iota(jnp.int32, (span, span), 1)
    phase = jnp.where(row >= 2 * frames, 2, jnp.where(row >= frames, 1, 0))
    select = (col == 3 * (row - frames * phase) + phase).astype(F32).astype(BF16)
    for n in range(2 * cols):
        parts = dot(select, take(n)).astype(BF16)
        for p in range(3):
            phases[p, n * frames : (n + 1) * frames, :] = parts[p * frames : (p + 1) * frames]
    if far:
        copy_out = pltpu.make_async_copy(phases, phases_out, far[1])
        copy_out.start()
    padded[:, :8, :] = jnp.zeros((2 * cols, 8, width), F32)
    earlier = dot(phases[1], w[0]) + dot(phases[2], w[1])
    padded[:, 8 : 8 + frames, :] = earlier.reshape(2 * cols, frames, width)
    same = dot(phases[0], w[2]) + dot(phases[1], w[3]) + dot(phases[2], w[4])
    h = leaky(same + padded[:, 7 : 7 + frames, :].reshape(rows, width))
    h_out[...] = h
    _, root = difference_terms(h[: rows // 2], h[rows // 2 :])
    loss[...] = fold_rows(root - smooth_width)
    if far:
        copy_out.wait()


def first_early_kernel(
    real, fake, w_hbm, h_out, phases_out, loss, w, rest,
    padded, held, held_sem, rest_sem, w_sem, *far_scratch,
):
    cols = held.shape[0] // 2
    span = held.shape[1]
    for n in range(2 * cols):
        source = real if n < cols else fake
        pltpu.make_async_copy(source.at[n % cols], held.at[n], held_sem.at[n]).start()
    w_copy = pltpu.make_async_copy(w_hbm, w, w_sem)
    w_copy.start()
    rest_copies = [
        pltpu.make_async_copy(x.at[cols:], rest.at[at * cols : (at + 1) * cols], rest_sem.at[at])
        for at, x in enumerate((real, fake))
    ]
    for copy in rest_copies:
        copy.start()

    def take(n):
        source = real if n < cols else fake
        pltpu.make_async_copy(source.at[n % cols], held.at[n], held_sem.at[n]).wait()
        if n == 2 * cols - 1:
            w_copy.wait()
        return held[n]

    strided_conv(take, cols, span, w, h_out, phases_out, loss, padded, *far_scratch)
    for copy in rest_copies:
        copy.wait()


def first_late_kernel(rest, w, w_next_hbm, h_out, phases_out, loss, w_next, padded, sem, *far):
    copy = pltpu.make_async_copy(w_next_hbm, w_next, sem)
    copy.start()
    cols, span = rest.shape[0] // 2, rest.shape[1]
    strided_conv(lambda n: rest[n], cols, span, w, h_out, phases_out, loss, padded, *far)
    copy.wait()


def second_kernel(
    normaliser, whole, near, s_ref, own, prev, following, far, w, loss_first,
    all_out, shifted_out, far_t, loss, *rest,
):
    if near:
        h_all, shifted = all_out, shifted_out
        *backs, padded, in_sems = rest
    else:
        *backs, padded, in_sems, h_all, shifted, all_sem, shifted_sem = rest
    rows, width = own.shape
    half = rows // 2
    taps = w.shape[0]
    frames = padded.shape[1] - 16
    s = s_ref[0]
    copies = []
    for away, x in enumerate((own, following, far, prev)):
        at = pl.multiple_of(lax.rem(s + away, 4) * width, 256)
        copies.append(
            pltpu.make_async_copy(x, h_all.at[:, pl.ds(at, width)], in_sems.at[away])
        )
        copies[-1].start()
    for copy in copies:
        copy.wait()
    if not near:
        copy_all = pltpu.make_async_copy(h_all, all_out, all_sem)
        copy_all.start()
    zeros = jnp.zeros((padded.shape[0], 8, width), F32)
    padded[:, :8, :] = zeros
    padded[:, 8 + frames :, :] = zeros
    pre = dot(h_all[...], w[2])
    for k in (0, 1, 3, 4):
        padded[:, 8 : 8 + frames, :] = dot(h_all[...], w[k]).reshape(-1, frames, width)
        pre = pre + padded[:, 6 + k : 6 + k + frames, :].reshape(rows, width)
    h = leaky(pre)
    difference, root = difference_terms(h[:half], h[half:])
    loss_rows = losses_split(loss_first[...], fold_rows(root - smooth_width))
    loss[...] = loss_rows
    slope = difference / root / normaliser
    for value, sign, at in ((h[:half], 1.0, 0), (h[half:], -1.0, half // frames)):
        gate = jnp.where(value.astype(F32) > 0, 1.0, leak_slope)
        delta = (sign * slope * gate).astype(BF16).astype(F32)
        padded[at : at + half // frames, 8 : 8 + frames, :] = delta.reshape(-1, frames, width)
    for k in range(taps):
        moved = padded[:, 10 - k : 10 - k + frames, :].reshape(rows, width)
        shifted[:, k * width : (k + 1) * width] = moved.astype(BF16)
    if not near:
        copy_shifted = pltpu.make_async_copy(shifted, shifted_out, shifted_sem)
        copy_shifted.start()
    far_t[:rows] = back_term(s, 2, shifted, w)
    far_t[rows:] = loss_rows
    if whole:
        back_rest(s, shifted, w, loss_rows, 3, *backs)
    if not near:
        copy_all.wait()
        copy_shifted.wait()


def back_term(s, away, shifted, w):
    width = w.shape[2]
    at = pl.multiple_of(lax.rem(s + away, 4) * width, 256)
    term = None
    for k in range(w.shape[0]):
        part = dot_lanes(shifted[:, k * width : (k + 1) * width], w[k, pl.ds(at, width), :])
        term = part if term is None else term + part
    return term.astype(BF16)


def back_rest(s, shifted, w, loss_rows, with_loss, following, prev, own):
    rows = own.shape[0]
    for away, out in ((1, following), (3, prev)) if with_loss == 1 else ((3, prev), (1, following)):
        out[:rows] = back_term(s, away, shifted, w)
        out[rows:] = loss_rows if away == with_loss else jnp.zeros_like(loss_rows)
    own[...] = back_term(s, 0, shifted, w)


def back_kernel(s_ref, shifted, w, loss, following, prev, own, *rest):
    if rest:
        held, sem = rest
        copy = pltpu.make_async_copy(shifted, held, sem)
        copy.start()
        copy.wait()
        shifted = held
    back_rest(s_ref[0], shifted, w, loss[...], 1, following, prev, own)


def add_kernel(a, b, out):
    out[...] = (a[...].astype(F32) + b[...].astype(F32)).astype(BF16)


def put(g, c, outs, at, rows, k):
    count = g.shape[0] // (2 * rows)
    g = g.astype(BF16).reshape(count, 2, rows, g.shape[1])
    even, odd = g[:, 0], g[:, 1]
    mine, theirs = outs
    mine[at : at + count, k * rows : (k + 1) * rows] = jnp.where(c == 0, even, odd)
    theirs[at : at + count, k * rows : (k + 1) * rows] = jnp.where(c == 0, odd, even)


def weight_second_kernel(taps, nears, c_ref, h_a, h_b, shifted_a, shifted_b, mine, theirs, *rest):
    own_rows, width = mine.shape[1] // taps, mine.shape[2]
    c = c_ref[0]
    step = 256
    count = h_a.shape[1] // step
    rest = list(rest)
    pairs, first, later = [], [], [[] for _ in range(count)]
    for near, h, x in ((nears[0], h_a, shifted_a), (nears[1], h_b, shifted_b)):
        if not near:
            h_held, x_held, h_sem, x_sem = rest[:4]
            rest = rest[4:]
            first.append(pltpu.make_async_copy(x, x_held, x_sem))
            for q in range(count):
                cut = slice(q * step, (q + 1) * step)
                later[q].append(
                    pltpu.make_async_copy(h.at[:, cut], h_held.at[:, cut], h_sem.at[q])
                )
            h, x = h_held, x_held
        pairs.append((h, x))
    for copy in first + sum(later, []):
        copy.start()
    for copy in first:
        copy.wait()
    for q in range(count):
        for copy in later[q]:
            copy.wait()
        cut = slice(q * step, (q + 1) * step)
        g = sum(dot_rows(h[:, cut], x[...]) for h, x in pairs)
        for k in range(taps):
            put(g[:, k * width : (k + 1) * width], c, (mine, theirs),
                q * step // (2 * own_rows), own_rows, k)


def weight_first_kernel(
    normaliser, taps, nears, c_ref, loss_a, loss_b, *refs,
):
    *sources, phases_a, phases_b, mine, theirs, padded, moved = refs[:16]
    rest = list(refs[16:])
    rows, width = sources[0].shape
    half = rows // 2
    frames = padded.shape[1] - 8
    c = c_ref[0]
    small, large = [], []
    if not nears[0]:
        got, sems = rest[:2]
        rest = rest[2:]
        for n, x in enumerate(sources):
            small.append(pltpu.make_async_copy(x, got.at[n, : x.shape[0]], sems.at[n]))
        sources = [got.at[n, : x.shape[0]] for n, x in enumerate(sources)]
    phases = []
    for near, x in zip(nears[1:], (phases_a, phases_b)):
        if not near:
            held, sem = rest[:2]
            rest = rest[2:]
            large.append(pltpu.make_async_copy(x, held, sem))
            x = held
        phases.append(x)
    for copy in small + large:
        copy.start()
    for copy in small:
        copy.wait()
    padded[:, frames:, :] = jnp.zeros((padded.shape[0], 8, width), F32)
    for n in range(2):
        h, own, a, b = (sources[2 * at + n] for at in range(4))
        difference, root = difference_terms(h[:half], h[half:rows])
        slope = difference / root / normaliser
        for at, sign in ((0, 1.0), (half, -1.0)):
            cut = slice(at, at + half)
            up = own[cut].astype(F32) + a[cut].astype(F32) + b[cut].astype(F32)
            up = up.astype(BF16).astype(F32)
            gate = jnp.where(h[cut].astype(F32) > 0, 1.0, leak_slope)
            delta = ((sign * slope + up) * gate).astype(BF16)
            base = n * rows + at
            moved[base : base + half, :width] = delta
            cols, lead = half // frames, base // frames
            padded[lead : lead + cols, :frames, :] = delta.astype(F32).reshape(cols, frames, width)
    moved[:, width:] = padded[:, 1 : 1 + frames, :].reshape(2 * rows, width).astype(BF16)
    groups = mine.shape[0]
    own_rows = (mine.shape[1] - 8) // taps
    outs = (mine, theirs)
    for copy in large:
        copy.wait()
    for p in range(3):
        lanes = width if p == 0 else 2 * width
        g = dot_rows(phases[0][p], moved[:rows, :lanes])
        g = g + dot_rows(phases[1][p], moved[rows:, :lanes])
        put(g[:, :width], c, outs, 0, own_rows, 2 + p)
        if p > 0:
            put(g[:, width:], c, outs, 0, own_rows, p - 1)
    total = loss_a[...].astype(F32) + loss_b[...].astype(F32)
    for x in sources[4:]:
        total = total + x[rows:].astype(F32)
    lines = split_rows(jnp.sum(total, axis=0, keepdims=True), 3 * c)
    for x in outs:
        x[:, taps * own_rows :, :] = jnp.broadcast_to(lines[None], (groups, 8, width))


def join_kernel(at, a, b, joint, summed, sem):
    summed[...] = (a[...].astype(F32) + b[...].astype(F32)).astype(BF16)
    copy = pltpu.make_async_copy(summed, joint.at[:, at : at + summed.shape[1]], sem)
    copy.start()
    copy.wait()


def join_late_kernel(at, a, b, held, joint, summed, sem):
    del held
    join_kernel(at, a, b, joint, summed, sem)


def total_kernel(taps, count_all, blocks, second, first, loss):
    total = jnp.sum(blocks[...].astype(F32), axis=0)
    at = 0
    for out in (second, first):
        rows = taps * out.shape[1]
        out[...] = total[at : at + rows].reshape(out.shape)
        at += rows
    lines = total[at:]
    loss[0] = jnp.sum(lines[:, :128]) / count_all
    loss[1] = jnp.sum(lines[:, 128:]) / count_all


def call(
    kernel, operands, outs, scratch=(), smem=0, hbm=(), loose=(), after=(), smem_outs=(),
    hbm_outs=(), aliases={}, flops=0, cost=1, name=None,
):
    moved = sum(x.size * x.dtype.itemsize for x in operands)
    moved += sum(x.size * x.dtype.itemsize for x in outs)
    vmem, small = pl.BlockSpec(memory_space=pltpu.VMEM), pl.BlockSpec(memory_space=pltpu.SMEM)
    far, anywhere = pl.BlockSpec(memory_space=pltpu.HBM), pl.BlockSpec(memory_space=pl.ANY)
    count = len(operands)
    operands = tuple(
        pltpu.with_memory_space_constraint(x, pltpu.HBM) if at in hbm else x
        for at, x in enumerate(operands)
    )

    def body(*refs):
        kernel(*refs[:count], *refs[count + len(after) :])

    return pl.pallas_call(
        body,
        out_shape=[
            pltpu.HBM(x.shape, x.dtype) if at in hbm_outs else x for at, x in enumerate(outs)
        ],
        in_specs=[
            small if at < smem else far if at in hbm else anywhere if at in loose else vmem
            for at in range(count)
        ]
        + [anywhere] * len(after),
        out_specs=[
            small if at in smem_outs else far if at in hbm_outs else vmem
            for at in range(len(outs))
        ],
        scratch_shapes=list(scratch),
        input_output_aliases=aliases,
        compiler_params=pltpu.CompilerParams(vmem_limit_bytes=VMEM_LIMIT),
        cost_estimate=pl.CostEstimate(
            flops=int(flops * cost), bytes_accessed=int(moved * cost), transcendentals=0
        ),
        name=name,
    )(*operands, *after)


def like(shape, dtype=BF16):
    return jax.ShapeDtypeStruct(shape, dtype)


def turn(x, step):
    count = lax.axis_size("section")
    return lax.ppermute(x, "section", [(i, (i + step) % count) for i in range(count)])


def added(a, b, name, after=()):
    return call(add_kernel, (a, b), [like(a.shape)], after=after, name=name)[0]


def other_core(x):
    return lax.ppermute(x, "dp_2", [(0, 1), (1, 0)])


def shards(real_in, fake_in, kernel_first, kernel_second):
    replicas = lax.axis_size(DP)
    cols, span, in_width = real_in.shape
    frames = span // 3
    taps, width_all, width = kernel_second.shape
    normaliser = float(cols * frames)
    count_all = float(cols * replicas * frames * width_all)
    groups = replicas // 2
    part = cols // 2
    rows = cols * frames
    s = lax.axis_index("section").reshape(1).astype(jnp.int32)
    c = lax.axis_index("dp_2").reshape(1).astype(jnp.int32)
    dma = pltpu.SemaphoreType.DMA
    chunk_outs = [like((rows, width)), like((3, rows, in_width)), like((8, 128), F32)]
    conv_scratch = [pltpu.VMEM((cols, frames + 8, width), F32)]
    phases_far = [pltpu.VMEM((3, rows, in_width), BF16), dma]
    all_far = [pltpu.VMEM((rows, width_all), BF16), pltpu.VMEM((rows, taps * width), BF16)]
    flops = 2 * rows * taps * in_width * width

    h_a, phases_a, loss_a, w_first, rest = call(
        first_early_kernel,
        (real_in, fake_in, kernel_first),
        chunk_outs + [like(kernel_first.shape), like((cols, span, in_width))],
        conv_scratch
        + [pltpu.VMEM((cols, span, in_width), BF16), dma((cols,)), dma((2,)), dma]
        + phases_far * (not NEAR_PHASES[0]),
        hbm=(0, 1, 2),
        hbm_outs=() if NEAR_PHASES[0] else (1,),
        flops=flops,
        name="first_a",
    )
    prev_a = turn(h_a, 1)
    following_a = turn(h_a, -1)
    h_b, phases_b, loss_b, w_second = call(
        first_late_kernel,
        (rest, w_first, kernel_second),
        chunk_outs + [like(kernel_second.shape)],
        conv_scratch + [dma] + phases_far * (not NEAR_PHASES[1]),
        hbm=(2,),
        hbm_outs=() if NEAR_PHASES[1] else (1,),
        flops=flops,
        cost=1,
        name="first_b",
    )
    far_a = turn(prev_a, 1)
    following_b = turn(h_b, -1)
    prev_b = turn(h_b, 1)
    far_b = turn(following_b, -1)

    second_outs = [like((rows, width_all)), like((rows, taps * width)), like((rows + 8, width)),
                   like((8, width))]
    back_outs = [like((rows + 8, width)), like((rows + 8, width)), like((rows, width))]
    second_scratch = [
        pltpu.VMEM((cols, frames + 16, width), F32), dma((4,)),
    ]
    copies = all_far + [dma, dma]
    flops = 2 * rows * taps * (width_all + width) * width
    all_a, shifted_a, far_t, loss_a, next_t, prev_t, own_a = call(
        functools.partial(second_kernel, normaliser, True, NEAR_ALL[0]),
        (s, h_a, prev_a, following_a, far_a, w_second, loss_a),
        second_outs + back_outs,
        second_scratch + copies * (not NEAR_ALL[0]),
        smem=1,
        loose=(1, 2, 3, 4),
        hbm_outs=() if NEAR_ALL[0] else (0, 1),
        cost=1,
        flops=flops,
        name="second_a",
    )
    pass_a = turn(far_t, 1)
    from_following_a = turn(prev_t, -1)
    relayed_a = added(next_t, pass_a, "relay_a")
    from_prev_a = turn(relayed_a, 1)

    all_b, shifted_b, far_t, loss_b = call(
        functools.partial(second_kernel, normaliser, False, NEAR_ALL[1]),
        (s, h_b, prev_b, following_b, far_b, w_second, loss_b),
        second_outs,
        second_scratch + copies * (not NEAR_ALL[1]),
        smem=1,
        loose=(1, 2, 3, 4),
        hbm_outs=() if NEAR_ALL[1] else (0, 1),
        cost=1,
        after=(own_a,),
        flops=flops,
        name="second_b",
    )
    pass_b = turn(far_t, -1)
    next_t, prev_t, own_b = call(
        back_kernel,
        (s, shifted_b, w_second, loss_b),
        back_outs,
        [] if NEAR_ALL[1] else [pltpu.VMEM((rows, taps * width), BF16), dma],
        smem=1,
        hbm=() if NEAR_ALL[1] else (1,),
        cost=4,
        flops=2 * rows * taps * width * width * 3,
        name="back_b",
    )
    from_prev_b = turn(next_t, 1)
    relayed_b = added(prev_t, pass_b, "relay_b")
    from_following_b = turn(relayed_b, -1)

    own_rows = width_all // replicas
    mine_second, theirs = call(
        functools.partial(weight_second_kernel, taps, NEAR_ALL),
        (c, all_a, all_b, shifted_a, shifted_b),
        [like((groups, taps * own_rows, width))] * 2,
        (all_far + [dma((width_all // 256,)), dma]) * (2 - sum(NEAR_ALL)),
        smem=1,
        hbm=tuple(at for at in (1, 2, 3, 4) if not NEAR_ALL[(at - 1) % 2]),
        cost=4,
        after=(relayed_a, relayed_b),
        flops=4 * rows * taps * width * width_all,
        name="weight_second",
    )
    first_rows = in_width // replicas
    size_second, size_first = taps * own_rows, taps * first_rows + 8
    joint_like = like((groups, size_second + size_first, width))
    (joint,) = call(
        functools.partial(join_kernel, 0),
        (mine_second, other_core(theirs)),
        [joint_like],
        [pltpu.VMEM((groups, size_second, width), BF16), dma],
        hbm_outs=(0,),
        name="join_second",
    )

    mine_first, theirs = call(
        functools.partial(weight_first_kernel, normaliser, taps, (NEAR_SMALL, *NEAR_PHASES)),
        (c, loss_a, loss_b, h_a, h_b, own_a, own_b, from_prev_a, from_prev_b, from_following_a,
         from_following_b, pass_a, pass_b, phases_a, phases_b),
        [like((groups, taps * first_rows + 8, width))] * 2,
        [pltpu.VMEM((2 * cols, frames + 8, width), F32), pltpu.VMEM((2 * rows, 2 * width), BF16)]
        + [pltpu.VMEM((10, rows + 8, width), BF16), dma((10,))] * (not NEAR_SMALL)
        + phases_far * (2 - sum(NEAR_PHASES)),
        smem=1,
        hbm=tuple(at for at in (13, 14) if not NEAR_PHASES[at - 13]),
        loose=() if NEAR_SMALL else tuple(range(3, 13)),
        cost=20,
        after=(mine_second,),
        flops=4 * rows * taps * width * in_width,
        name="weight_first",
    )
    (joint,) = call(
        functools.partial(join_late_kernel, size_second),
        (mine_first, other_core(theirs), joint),
        [joint_like],
        [pltpu.VMEM((groups, size_first, width), BF16), dma],
        hbm=(2,),
        hbm_outs=(0,),
        aliases={2: 0},
        name="join_first",
    )
    blocks = lax.all_to_all(joint, ZY, 0, 0)
    grad_second, grad_first, layer_loss = call(
        functools.partial(total_kernel, taps, count_all),
        (blocks,),
        [like((taps, own_rows, width), F32), like((taps, first_rows, width), F32),
         like((2,), F32)],
        smem_outs=(2,),
        name="total",
    )
    return (layer_loss, jnp.transpose(grad_first, (1, 0, 2)), jnp.transpose(grad_second, (1, 0, 2)))


def solution(mesh):
    finer = Mesh(
        mesh.devices.reshape(4, 4, 2, mesh.shape["section"]), ("dp_0", "dp_1", "dp_2", "section")
    )
    return jax.shard_map(
        shards,
        mesh=finer,
        in_specs=(
            P(DP, None, None),
            P(DP, None, None),
            P(None, None, "section"),
            P(None, None, "section"),
        ),
        out_specs=(P(), P(DP, None, "section"), P(DP, None, "section")),
        check_vma=False,
    )
```

```python
import functools

import jax
import jax.numpy as jnp
from jax import lax
from jax.experimental import pallas as pl
from jax.experimental.pallas import tpu as pltpu
from jax.sharding import Mesh
from jax.sharding import PartitionSpec as P

DP = ("dp_0", "dp_1", "dp_2")
ZY = ("dp_0", "dp_1")
F32 = jnp.float32
BF16 = jnp.bfloat16
VMEM_LIMIT = 51 << 20
NEAR_PHASES = (False, False)
NEAR_ALL = (False, True)
NEAR_SMALL = True

smooth_width = 0.1
leak_slope = 0.1


def leaky(pre):
    return jnp.where(pre > 0, pre, leak_slope * pre).astype(BF16)


def fold_rows(x):
    x = jnp.sum(x.reshape(-1, 8, x.shape[1]), axis=0)
    return sum(x[:, at : at + 128] for at in range(0, x.shape[1], 128))


def difference_terms(real, fake):
    difference = real.astype(F32) - fake.astype(F32)
    root = jnp.sqrt(difference * difference + smooth_width * smooth_width)
    return difference, root


def dot(a, b):
    return jnp.dot(a, b, preferred_element_type=F32)


def dot_rows(a, b):
    return lax.dot_general(a, b, (((0,), (0,)), ((), ())), preferred_element_type=F32)


def dot_lanes(a, b):
    return lax.dot_general(a, b, (((1,), (1,)), ((), ())), preferred_element_type=F32)


def losses_split(first, second):
    value = jnp.sum(jnp.concatenate([first, second], axis=1), axis=0, keepdims=True)
    return split_rows(value, 0)


def split_rows(value, base):
    row = lax.broadcasted_iota(jnp.int32, (8, value.shape[1]), 0) - base
    high = value.astype(BF16).astype(F32)
    middle = (value - high).astype(BF16).astype(F32)
    low = value - high - middle
    out = jnp.where(row == 0, high, jnp.where(row == 1, middle, jnp.where(row == 2, low, 0.0)))
    return out.astype(BF16)


def strided_conv(take, cols, span, w, h_out, phases_out, loss, padded, *far):
    phases = far[0] if far else phases_out
    frames = span // 3
    rows = 2 * cols * frames
    width = w.shape[2]
    row = lax.broadcasted_iota(jnp.int32, (span, span), 0)
    col = lax.broadcasted_iota(jnp.int32, (span, span), 1)
    phase = jnp.where(row >= 2 * frames, 2, jnp.where(row >= frames, 1, 0))
    select = (col == 3 * (row - frames * phase) + phase).astype(F32).astype(BF16)
    for n in range(2 * cols):
        parts = dot(select, take(n)).astype(BF16)
        for p in range(3):
            phases[p, n * frames : (n + 1) * frames, :] = parts[p * frames : (p + 1) * frames]
    if far:
        copy_out = pltpu.make_async_copy(phases, phases_out, far[1])
        copy_out.start()
    padded[:, :8, :] = jnp.zeros((2 * cols, 8, width), F32)
    earlier = dot(phases[1], w[0]) + dot(phases[2], w[1])
    padded[:, 8 : 8 + frames, :] = earlier.reshape(2 * cols, frames, width)
    same = dot(phases[0], w[2]) + dot(phases[1], w[3]) + dot(phases[2], w[4])
    h = leaky(same + padded[:, 7 : 7 + frames, :].reshape(rows, width))
    h_out[...] = h
    _, root = difference_terms(h[: rows // 2], h[rows // 2 :])
    loss[...] = fold_rows(root - smooth_width)
    if far:
        copy_out.wait()


def first_early_kernel(
    real, fake, w_hbm, h_out, phases_out, loss, w, rest,
    padded, held, held_sem, rest_sem, w_sem, *far_scratch,
):
    cols = held.shape[0] // 2
    span = held.shape[1]
    for n in range(2 * cols):
        source = real if n < cols else fake
        pltpu.make_async_copy(source.at[n % cols], held.at[n], held_sem.at[n]).start()
    w_copy = pltpu.make_async_copy(w_hbm, w, w_sem)
    w_copy.start()
    rest_copies = [
        pltpu.make_async_copy(x.at[cols:], rest.at[at * cols : (at + 1) * cols], rest_sem.at[at])
        for at, x in enumerate((real, fake))
    ]
    for copy in rest_copies:
        copy.start()

    def take(n):
        source = real if n < cols else fake
        pltpu.make_async_copy(source.at[n % cols], held.at[n], held_sem.at[n]).wait()
        if n == 2 * cols - 1:
            w_copy.wait()
        return held[n]

    strided_conv(take, cols, span, w, h_out, phases_out, loss, padded, *far_scratch)
    for copy in rest_copies:
        copy.wait()


def first_late_kernel(rest, w, w_next_hbm, h_out, phases_out, loss, w_next, padded, sem, *far):
    copy = pltpu.make_async_copy(w_next_hbm, w_next, sem)
    copy.start()
    cols, span = rest.shape[0] // 2, rest.shape[1]
    strided_conv(lambda n: rest[n], cols, span, w, h_out, phases_out, loss, padded, *far)
    copy.wait()


def second_kernel(
    normaliser, whole, near, s_ref, own, prev, following, far, w, loss_first,
    all_out, shifted_out, far_t, loss, *rest,
):
    if near:
        h_all, shifted = all_out, shifted_out
        *backs, padded, in_sems = rest
    else:
        *backs, padded, in_sems, h_all, shifted, all_sem, shifted_sem = rest
    rows, width = own.shape
    half = rows // 2
    taps = w.shape[0]
    frames = padded.shape[1] - 16
    s = s_ref[0]
    copies = []
    for away, x in enumerate((own, following, far, prev)):
        at = pl.multiple_of(lax.rem(s + away, 4) * width, 256)
        copies.append(
            pltpu.make_async_copy(x, h_all.at[:, pl.ds(at, width)], in_sems.at[away])
        )
        copies[-1].start()
    for copy in copies:
        copy.wait()
    if not near:
        copy_all = pltpu.make_async_copy(h_all, all_out, all_sem)
        copy_all.start()
    zeros = jnp.zeros((padded.shape[0], 8, width), F32)
    padded[:, :8, :] = zeros
    padded[:, 8 + frames :, :] = zeros
    pre = dot(h_all[...], w[2])
    for k in (0, 1, 3, 4):
        padded[:, 8 : 8 + frames, :] = dot(h_all[...], w[k]).reshape(-1, frames, width)
        pre = pre + padded[:, 6 + k : 6 + k + frames, :].reshape(rows, width)
    h = leaky(pre)
    difference, root = difference_terms(h[:half], h[half:])
    loss_rows = losses_split(loss_first[...], fold_rows(root - smooth_width))
    loss[...] = loss_rows
    slope = difference / root / normaliser
    for value, sign, at in ((h[:half], 1.0, 0), (h[half:], -1.0, half // frames)):
        gate = jnp.where(value.astype(F32) > 0, 1.0, leak_slope)
        delta = (sign * slope * gate).astype(BF16).astype(F32)
        padded[at : at + half // frames, 8 : 8 + frames, :] = delta.reshape(-1, frames, width)
    for k in range(taps):
        moved = padded[:, 10 - k : 10 - k + frames, :].reshape(rows, width)
        shifted[:, k * width : (k + 1) * width] = moved.astype(BF16)
    if not near:
        copy_shifted = pltpu.make_async_copy(shifted, shifted_out, shifted_sem)
        copy_shifted.start()
    far_t[:rows] = back_term(s, 2, shifted, w)
    far_t[rows:] = loss_rows
    if whole:
        back_rest(s, shifted, w, loss_rows, 3, *backs)
    if not near:
        copy_all.wait()
        copy_shifted.wait()


def back_term(s, away, shifted, w):
    width = w.shape[2]
    at = pl.multiple_of(lax.rem(s + away, 4) * width, 256)
    term = None
    for k in range(w.shape[0]):
        part = dot_lanes(shifted[:, k * width : (k + 1) * width], w[k, pl.ds(at, width), :])
        term = part if term is None else term + part
    return term.astype(BF16)


def back_rest(s, shifted, w, loss_rows, with_loss, following, prev, own):
    rows = own.shape[0]
    for away, out in ((1, following), (3, prev)) if with_loss == 1 else ((3, prev), (1, following)):
        out[:rows] = back_term(s, away, shifted, w)
        out[rows:] = loss_rows if away == with_loss else jnp.zeros_like(loss_rows)
    own[...] = back_term(s, 0, shifted, w)


def back_kernel(s_ref, shifted, w, loss, following, prev, own, *rest):
    if rest:
        held, sem = rest
        copy = pltpu.make_async_copy(shifted, held, sem)
        copy.start()
        copy.wait()
        shifted = held
    back_rest(s_ref[0], shifted, w, loss[...], 1, following, prev, own)


def add_kernel(a, b, out):
    out[...] = (a[...].astype(F32) + b[...].astype(F32)).astype(BF16)


def put(g, c, outs, at, rows, k):
    count = g.shape[0] // (2 * rows)
    g = g.astype(BF16).reshape(count, 2, rows, g.shape[1])
    even, odd = g[:, 0], g[:, 1]
    mine, theirs = outs
    mine[at : at + count, k * rows : (k + 1) * rows] = jnp.where(c == 0, even, odd)
    theirs[at : at + count, k * rows : (k + 1) * rows] = jnp.where(c == 0, odd, even)


def weight_second_kernel(taps, nears, c_ref, h_a, h_b, shifted_a, shifted_b, mine, theirs, *rest):
    own_rows, width = mine.shape[1] // taps, mine.shape[2]
    c = c_ref[0]
    step = 256
    count = h_a.shape[1] // step
    rest = list(rest)
    pairs, first, later = [], [], [[] for _ in range(count)]
    for near, h, x in ((nears[0], h_a, shifted_a), (nears[1], h_b, shifted_b)):
        if not near:
            h_held, x_held, h_sem, x_sem = rest[:4]
            rest = rest[4:]
            first.append(pltpu.make_async_copy(x, x_held, x_sem))
            for q in range(count):
                cut = slice(q * step, (q + 1) * step)
                later[q].append(
                    pltpu.make_async_copy(h.at[:, cut], h_held.at[:, cut], h_sem.at[q])
                )
            h, x = h_held, x_held
        pairs.append((h, x))
    for copy in first + sum(later, []):
        copy.start()
    for copy in first:
        copy.wait()
    for q in range(count):
        for copy in later[q]:
            copy.wait()
        cut = slice(q * step, (q + 1) * step)
        g = sum(dot_rows(h[:, cut], x[...]) for h, x in pairs)
        for k in range(taps):
            put(g[:, k * width : (k + 1) * width], c, (mine, theirs),
                q * step // (2 * own_rows), own_rows, k)


def weight_first_kernel(
    normaliser, taps, nears, c_ref, loss_a, loss_b, *refs,
):
    *sources, phases_a, phases_b, mine, theirs, padded, moved = refs[:16]
    rest = list(refs[16:])
    rows, width = sources[0].shape
    half = rows // 2
    frames = padded.shape[1] - 8
    c = c_ref[0]
    small, large = [], []
    if not nears[0]:
        got, sems = rest[:2]
        rest = rest[2:]
        for n, x in enumerate(sources):
            small.append(pltpu.make_async_copy(x, got.at[n, : x.shape[0]], sems.at[n]))
        sources = [got.at[n, : x.shape[0]] for n, x in enumerate(sources)]
    phases = []
    for near, x in zip(nears[1:], (phases_a, phases_b)):
        if not near:
            held, sem = rest[:2]
            rest = rest[2:]
            large.append(pltpu.make_async_copy(x, held, sem))
            x = held
        phases.append(x)
    for copy in small + large:
        copy.start()
    for copy in small:
        copy.wait()
    padded[:, frames:, :] = jnp.zeros((padded.shape[0], 8, width), F32)
    for n in range(2):
        h, own, a, b = (sources[2 * at + n] for at in range(4))
        difference, root = difference_terms(h[:half], h[half:rows])
        slope = difference / root / normaliser
        for at, sign in ((0, 1.0), (half, -1.0)):
            cut = slice(at, at + half)
            up = own[cut].astype(F32) + a[cut].astype(F32) + b[cut].astype(F32)
            up = up.astype(BF16).astype(F32)
            gate = jnp.where(h[cut].astype(F32) > 0, 1.0, leak_slope)
            delta = ((sign * slope + up) * gate).astype(BF16)
            base = n * rows + at
            moved[base : base + half, :width] = delta
            cols, lead = half // frames, base // frames
            padded[lead : lead + cols, :frames, :] = delta.astype(F32).reshape(cols, frames, width)
    moved[:, width:] = padded[:, 1 : 1 + frames, :].reshape(2 * rows, width).astype(BF16)
    groups = mine.shape[0]
    own_rows = (mine.shape[1] - 8) // taps
    outs = (mine, theirs)
    for copy in large:
        copy.wait()
    for p in range(3):
        lanes = width if p == 0 else 2 * width
        g = dot_rows(phases[0][p], moved[:rows, :lanes])
        g = g + dot_rows(phases[1][p], moved[rows:, :lanes])
        put(g[:, :width], c, outs, 0, own_rows, 2 + p)
        if p > 0:
            put(g[:, width:], c, outs, 0, own_rows, p - 1)
    total = loss_a[...].astype(F32) + loss_b[...].astype(F32)
    for x in sources[4:]:
        total = total + x[rows:].astype(F32)
    lines = split_rows(jnp.sum(total, axis=0, keepdims=True), 3 * c)
    for x in outs:
        x[:, taps * own_rows :, :] = jnp.broadcast_to(lines[None], (groups, 8, width))


def same_kernel(a, out):
    out[...] = a[...]


def join_kernel(at, a, b, joint, summed, sem):
    summed[...] = (a[...].astype(F32) + b[...].astype(F32)).astype(BF16)
    copy = pltpu.make_async_copy(summed, joint.at[:, at : at + summed.shape[1]], sem)
    copy.start()
    copy.wait()


def join_late_kernel(at, a, b, held, joint, summed, sem):
    del held
    join_kernel(at, a, b, joint, summed, sem)


def total_kernel(taps, count_all, blocks, second, first, loss):
    total = jnp.sum(blocks[...].astype(F32), axis=0)
    at = 0
    for out in (second, first):
        rows = taps * out.shape[1]
        out[...] = total[at : at + rows].reshape(out.shape)
        at += rows
    lines = total[at:]
    loss[0] = jnp.sum(lines[:, :128]) / count_all
    loss[1] = jnp.sum(lines[:, 128:]) / count_all


def call(
    kernel, operands, outs, scratch=(), smem=0, hbm=(), loose=(), after=(), smem_outs=(),
    hbm_outs=(), aliases={}, flops=0, cost=1, name=None,
):
    moved = sum(x.size * x.dtype.itemsize for x in operands)
    moved += sum(x.size * x.dtype.itemsize for x in outs)
    vmem, small = pl.BlockSpec(memory_space=pltpu.VMEM), pl.BlockSpec(memory_space=pltpu.SMEM)
    far, anywhere = pl.BlockSpec(memory_space=pltpu.HBM), pl.BlockSpec(memory_space=pl.ANY)
    count = len(operands)
    operands = tuple(
        pltpu.with_memory_space_constraint(x, pltpu.HBM) if at in hbm else x
        for at, x in enumerate(operands)
    )

    def body(*refs):
        kernel(*refs[:count], *refs[count + len(after) :])

    return pl.pallas_call(
        body,
        out_shape=[
            pltpu.HBM(x.shape, x.dtype) if at in hbm_outs else x for at, x in enumerate(outs)
        ],
        in_specs=[
            small if at < smem else far if at in hbm else anywhere if at in loose else vmem
            for at in range(count)
        ]
        + [anywhere] * len(after),
        out_specs=[
            small if at in smem_outs else far if at in hbm_outs else vmem
            for at in range(len(outs))
        ],
        scratch_shapes=list(scratch),
        input_output_aliases=aliases,
        compiler_params=pltpu.CompilerParams(vmem_limit_bytes=VMEM_LIMIT),
        cost_estimate=pl.CostEstimate(
            flops=int(flops * cost), bytes_accessed=int(moved * cost), transcendentals=0
        ),
        name=name,
    )(*operands, *after)


def like(shape, dtype=BF16):
    return jax.ShapeDtypeStruct(shape, dtype)


def turn(x, step):
    count = lax.axis_size("section")
    return lax.ppermute(x, "section", [(i, (i + step) % count) for i in range(count)])


def later(x, after, name):
    return call(same_kernel, (x,), [like(x.shape)], after=after, name=name)[0]


def added(a, b, name, after=()):
    return call(add_kernel, (a, b), [like(a.shape)], after=after, name=name)[0]


def other_core(x):
    return lax.ppermute(x, "dp_2", [(0, 1), (1, 0)])


def shards(real_in, fake_in, kernel_first, kernel_second):
    replicas = lax.axis_size(DP)
    cols, span, in_width = real_in.shape
    frames = span // 3
    taps, width_all, width = kernel_second.shape
    normaliser = float(cols * frames)
    count_all = float(cols * replicas * frames * width_all)
    groups = replicas // 2
    part = cols // 2
    rows = cols * frames
    s = lax.axis_index("section").reshape(1).astype(jnp.int32)
    c = lax.axis_index("dp_2").reshape(1).astype(jnp.int32)
    dma = pltpu.SemaphoreType.DMA
    chunk_outs = [like((rows, width)), like((3, rows, in_width)), like((8, 128), F32)]
    conv_scratch = [pltpu.VMEM((cols, frames + 8, width), F32)]
    phases_far = [pltpu.VMEM((3, rows, in_width), BF16), dma]
    all_far = [pltpu.VMEM((rows, width_all), BF16), pltpu.VMEM((rows, taps * width), BF16)]
    flops = 2 * rows * taps * in_width * width

    h_a, phases_a, loss_a, w_first, rest = call(
        first_early_kernel,
        (real_in, fake_in, kernel_first),
        chunk_outs + [like(kernel_first.shape), like((cols, span, in_width))],
        conv_scratch
        + [pltpu.VMEM((cols, span, in_width), BF16), dma((cols,)), dma((2,)), dma]
        + phases_far * (not NEAR_PHASES[0]),
        hbm=(0, 1, 2),
        hbm_outs=() if NEAR_PHASES[0] else (1,),
        flops=flops,
        name="first_a",
    )
    prev_a = turn(h_a, 1)
    following_a = turn(h_a, -1)
    h_b, phases_b, loss_b, w_second = call(
        first_late_kernel,
        (rest, w_first, kernel_second),
        chunk_outs + [like(kernel_second.shape)],
        conv_scratch + [dma] + phases_far * (not NEAR_PHASES[1]),
        hbm=(2,),
        hbm_outs=() if NEAR_PHASES[1] else (1,),
        flops=flops,
        cost=1,
        name="first_b",
    )
    far_a = turn(prev_a, 1)
    following_b = turn(h_b, -1)
    prev_b = turn(h_b, 1)
    far_b = turn(later(following_b, (following_a,), "ordered"), -1)

    second_outs = [like((rows, width_all)), like((rows, taps * width)), like((rows + 8, width)),
                   like((8, width))]
    back_outs = [like((rows + 8, width)), like((rows + 8, width)), like((rows, width))]
    second_scratch = [
        pltpu.VMEM((cols, frames + 16, width), F32), dma((4,)),
    ]
    copies = all_far + [dma, dma]
    flops = 2 * rows * taps * (width_all + width) * width
    all_a, shifted_a, far_t, loss_a, next_t, prev_t, own_a = call(
        functools.partial(second_kernel, normaliser, True, NEAR_ALL[0]),
        (s, h_a, prev_a, following_a, far_a, w_second, loss_a),
        second_outs + back_outs,
        second_scratch + copies * (not NEAR_ALL[0]),
        smem=1,
        loose=(1, 2, 3, 4),
        hbm_outs=() if NEAR_ALL[0] else (0, 1),
        cost=1,
        flops=flops,
        name="second_a",
    )
    pass_a = turn(far_t, 1)
    from_following_a = turn(prev_t, -1)
    relayed_a = added(next_t, pass_a, "relay_a")
    from_prev_a = turn(relayed_a, 1)

    all_b, shifted_b, far_t, loss_b = call(
        functools.partial(second_kernel, normaliser, False, NEAR_ALL[1]),
        (s, h_b, prev_b, following_b, far_b, w_second, loss_b),
        second_outs,
        second_scratch + copies * (not NEAR_ALL[1]),
        smem=1,
        loose=(1, 2, 3, 4),
        hbm_outs=() if NEAR_ALL[1] else (0, 1),
        cost=1,
        after=(own_a,),
        flops=flops,
        name="second_b",
    )
    pass_b = turn(far_t, -1)
    next_t, prev_t, own_b = call(
        back_kernel,
        (s, shifted_b, w_second, loss_b),
        back_outs,
        [] if NEAR_ALL[1] else [pltpu.VMEM((rows, taps * width), BF16), dma],
        smem=1,
        hbm=() if NEAR_ALL[1] else (1,),
        cost=4,
        flops=2 * rows * taps * width * width * 3,
        after=(relayed_a, from_following_a),
        name="back_b",
    )
    from_prev_b = turn(next_t, 1)
    relayed_b = added(prev_t, pass_b, "relay_b")
    from_following_b = turn(relayed_b, -1)

    own_rows = width_all // replicas
    mine_second, theirs = call(
        functools.partial(weight_second_kernel, taps, NEAR_ALL),
        (c, all_a, all_b, shifted_a, shifted_b),
        [like((groups, taps * own_rows, width))] * 2,
        (all_far + [dma((width_all // 256,)), dma]) * (2 - sum(NEAR_ALL)),
        smem=1,
        hbm=tuple(at for at in (1, 2, 3, 4) if not NEAR_ALL[(at - 1) % 2]),
        cost=4,
        after=(relayed_a, relayed_b),
        flops=4 * rows * taps * width * width_all,
        name="weight_second",
    )
    first_rows = in_width // replicas
    size_second, size_first = taps * own_rows, taps * first_rows + 8
    joint_like = like((groups, size_second + size_first, width))
    (joint,) = call(
        functools.partial(join_kernel, 0),
        (mine_second, other_core(theirs)),
        [joint_like],
        [pltpu.VMEM((groups, size_second, width), BF16), dma],
        hbm_outs=(0,),
        name="join_second",
    )

    mine_first, theirs = call(
        functools.partial(weight_first_kernel, normaliser, taps, (NEAR_SMALL, *NEAR_PHASES)),
        (c, loss_a, loss_b, h_a, h_b, own_a, own_b, from_prev_a, from_prev_b, from_following_a,
         from_following_b, pass_a, pass_b, phases_a, phases_b),
        [like((groups, taps * first_rows + 8, width))] * 2,
        [pltpu.VMEM((2 * cols, frames + 8, width), F32), pltpu.VMEM((2 * rows, 2 * width), BF16)]
        + [pltpu.VMEM((10, rows + 8, width), BF16), dma((10,))] * (not NEAR_SMALL)
        + phases_far * (2 - sum(NEAR_PHASES)),
        smem=1,
        hbm=tuple(at for at in (13, 14) if not NEAR_PHASES[at - 13]),
        loose=() if NEAR_SMALL else tuple(range(3, 13)),
        cost=20,
        after=(mine_second,),
        flops=4 * rows * taps * width * in_width,
        name="weight_first",
    )
    (joint,) = call(
        functools.partial(join_late_kernel, size_second),
        (mine_first, other_core(theirs), joint),
        [joint_like],
        [pltpu.VMEM((groups, size_first, width), BF16), dma],
        hbm=(2,),
        hbm_outs=(0,),
        aliases={2: 0},
        name="join_first",
    )
    blocks = lax.all_to_all(joint, ZY, 0, 0)
    grad_second, grad_first, layer_loss = call(
        functools.partial(total_kernel, taps, count_all),
        (blocks,),
        [like((taps, own_rows, width), F32), like((taps, first_rows, width), F32),
         like((2,), F32)],
        smem_outs=(2,),
        name="total",
    )
    return (layer_loss, jnp.transpose(grad_first, (1, 0, 2)), jnp.transpose(grad_second, (1, 0, 2)))


def solution(mesh):
    finer = Mesh(
        mesh.devices.reshape(4, 4, 2, mesh.shape["section"]), ("dp_0", "dp_1", "dp_2", "section")
    )
    return jax.shard_map(
        shards,
        mesh=finer,
        in_specs=(
            P(DP, None, None),
            P(DP, None, None),
            P(None, None, "section"),
            P(None, None, "section"),
        ),
        out_specs=(P(), P(DP, None, "section"), P(DP, None, "section")),
        check_vma=False,
    )
```

```python
import functools

import jax
import jax.numpy as jnp
from jax import lax
from jax.experimental import pallas as pl
from jax.experimental.pallas import tpu as pltpu
from jax.sharding import Mesh
from jax.sharding import PartitionSpec as P

DP = ("dp_0", "dp_1", "dp_2")
ZY = ("dp_0", "dp_1")
F32 = jnp.float32
BF16 = jnp.bfloat16
VMEM_LIMIT = 16 << 20
NEAR_PHASES = (False, False)
NEAR_ALL = (False, True)
NEAR_SMALL = True

smooth_width = 0.1
leak_slope = 0.1


def leaky(pre):
    return jnp.where(pre > 0, pre, leak_slope * pre).astype(BF16)


def fold_rows(x):
    x = jnp.sum(x.reshape(-1, 8, x.shape[1]), axis=0)
    return sum(x[:, at : at + 128] for at in range(0, x.shape[1], 128))


def difference_terms(real, fake):
    difference = real.astype(F32) - fake.astype(F32)
    root = jnp.sqrt(difference * difference + smooth_width * smooth_width)
    return difference, root


def dot(a, b):
    return jnp.dot(a, b, preferred_element_type=F32)


def dot_rows(a, b):
    return lax.dot_general(a, b, (((0,), (0,)), ((), ())), preferred_element_type=F32)


def dot_lanes(a, b):
    return lax.dot_general(a, b, (((1,), (1,)), ((), ())), preferred_element_type=F32)


def losses_split(first, second):
    value = jnp.sum(jnp.concatenate([first, second], axis=1), axis=0, keepdims=True)
    return split_rows(value, 0)


def split_rows(value, base):
    row = lax.broadcasted_iota(jnp.int32, (8, value.shape[1]), 0) - base
    high = value.astype(BF16).astype(F32)
    middle = (value - high).astype(BF16).astype(F32)
    low = value - high - middle
    out = jnp.where(row == 0, high, jnp.where(row == 1, middle, jnp.where(row == 2, low, 0.0)))
    return out.astype(BF16)


def strided_conv(take, cols, span, w, h_out, phases_out, loss, padded, *far):
    phases = far[0] if far else phases_out
    frames = span // 3
    rows = 2 * cols * frames
    width = w.shape[2]
    row = lax.broadcasted_iota(jnp.int32, (span, span), 0)
    col = lax.broadcasted_iota(jnp.int32, (span, span), 1)
    phase = jnp.where(row >= 2 * frames, 2, jnp.where(row >= frames, 1, 0))
    select = (col == 3 * (row - frames * phase) + phase).astype(F32).astype(BF16)
    for n in range(2 * cols):
        parts = dot(select, take(n)).astype(BF16)
        for p in range(3):
            phases[p, n * frames : (n + 1) * frames, :] = parts[p * frames : (p + 1) * frames]
    if far:
        copy_out = pltpu.make_async_copy(phases, phases_out, far[1])
        copy_out.start()
    padded[:, :8, :] = jnp.zeros((2 * cols, 8, width), F32)
    earlier = dot(phases[1], w[0]) + dot(phases[2], w[1])
    padded[:, 8 : 8 + frames, :] = earlier.reshape(2 * cols, frames, width)
    same = dot(phases[0], w[2]) + dot(phases[1], w[3]) + dot(phases[2], w[4])
    h = leaky(same + padded[:, 7 : 7 + frames, :].reshape(rows, width))
    h_out[...] = h
    _, root = difference_terms(h[: rows // 2], h[rows // 2 :])
    loss[...] = fold_rows(root - smooth_width)
    if far:
        copy_out.wait()


def first_early_kernel(
    real, fake, w_hbm, h_out, phases_out, loss, w, rest,
    padded, held, held_sem, rest_sem, w_sem, *far_scratch,
):
    cols = held.shape[0] // 2
    span = held.shape[1]
    for n in range(2 * cols):
        source = real if n < cols else fake
        pltpu.make_async_copy(source.at[n % cols], held.at[n], held_sem.at[n]).start()
    w_copy = pltpu.make_async_copy(w_hbm, w, w_sem)
    w_copy.start()
    rest_copies = [
        pltpu.make_async_copy(x.at[cols:], rest.at[at * cols : (at + 1) * cols], rest_sem.at[at])
        for at, x in enumerate((real, fake))
    ]
    for copy in rest_copies:
        copy.start()

    def take(n):
        source = real if n < cols else fake
        pltpu.make_async_copy(source.at[n % cols], held.at[n], held_sem.at[n]).wait()
        if n == 2 * cols - 1:
            w_copy.wait()
        return held[n]

    strided_conv(take, cols, span, w, h_out, phases_out, loss, padded, *far_scratch)
    for copy in rest_copies:
        copy.wait()


def first_late_kernel(rest, w, w_next_hbm, h_out, phases_out, loss, w_next, padded, sem, *far):
    copy = pltpu.make_async_copy(w_next_hbm, w_next, sem)
    copy.start()
    cols, span = rest.shape[0] // 2, rest.shape[1]
    strided_conv(lambda n: rest[n], cols, span, w, h_out, phases_out, loss, padded, *far)
    copy.wait()


def second_kernel(
    normaliser, whole, near, s_ref, own, prev, following, far, w, loss_first,
    all_out, shifted_out, far_t, loss, *rest,
):
    if near:
        h_all, shifted = all_out, shifted_out
        *backs, padded, in_sems = rest
    else:
        *backs, padded, in_sems, h_all, shifted, all_sem, shifted_sem = rest
    rows, width = own.shape
    half = rows // 2
    taps = w.shape[0]
    frames = padded.shape[1] - 16
    s = s_ref[0]
    copies = []
    for away, x in enumerate((own, following, far, prev)):
        at = pl.multiple_of(lax.rem(s + away, 4) * width, 256)
        copies.append(
            pltpu.make_async_copy(x, h_all.at[:, pl.ds(at, width)], in_sems.at[away])
        )
        copies[-1].start()
    for copy in copies:
        copy.wait()
    if not near:
        copy_all = pltpu.make_async_copy(h_all, all_out, all_sem)
        copy_all.start()
    zeros = jnp.zeros((padded.shape[0], 8, width), F32)
    padded[:, :8, :] = zeros
    padded[:, 8 + frames :, :] = zeros
    pre = dot(h_all[...], w[2])
    for k in (0, 1, 3, 4):
        padded[:, 8 : 8 + frames, :] = dot(h_all[...], w[k]).reshape(-1, frames, width)
        pre = pre + padded[:, 6 + k : 6 + k + frames, :].reshape(rows, width)
    h = leaky(pre)
    difference, root = difference_terms(h[:half], h[half:])
    loss_rows = losses_split(loss_first[...], fold_rows(root - smooth_width))
    loss[...] = loss_rows
    slope = difference / root / normaliser
    for value, sign, at in ((h[:half], 1.0, 0), (h[half:], -1.0, half // frames)):
        gate = jnp.where(value.astype(F32) > 0, 1.0, leak_slope)
        delta = (sign * slope * gate).astype(BF16).astype(F32)
        padded[at : at + half // frames, 8 : 8 + frames, :] = delta.reshape(-1, frames, width)
    for k in range(taps):
        moved = padded[:, 10 - k : 10 - k + frames, :].reshape(rows, width)
        shifted[:, k * width : (k + 1) * width] = moved.astype(BF16)
    if not near:
        copy_shifted = pltpu.make_async_copy(shifted, shifted_out, shifted_sem)
        copy_shifted.start()
    far_t[:rows] = back_term(s, 2, shifted, w)
    far_t[rows:] = loss_rows
    if whole:
        back_rest(s, shifted, w, loss_rows, 3, *backs)
    if not near:
        copy_all.wait()
        copy_shifted.wait()


def back_term(s, away, shifted, w):
    width = w.shape[2]
    at = pl.multiple_of(lax.rem(s + away, 4) * width, 256)
    term = None
    for k in range(w.shape[0]):
        part = dot_lanes(shifted[:, k * width : (k + 1) * width], w[k, pl.ds(at, width), :])
        term = part if term is None else term + part
    return term.astype(BF16)


def back_rest(s, shifted, w, loss_rows, with_loss, following, prev, own):
    rows = own.shape[0]
    for away, out in ((1, following), (3, prev)) if with_loss == 1 else ((3, prev), (1, following)):
        out[:rows] = back_term(s, away, shifted, w)
        out[rows:] = loss_rows if away == with_loss else jnp.zeros_like(loss_rows)
    own[...] = back_term(s, 0, shifted, w)


def back_kernel(s_ref, shifted, w, loss, following, prev, own, *rest):
    if rest:
        held, sem = rest
        copy = pltpu.make_async_copy(shifted, held, sem)
        copy.start()
        copy.wait()
        shifted = held
    back_rest(s_ref[0], shifted, w, loss[...], 1, following, prev, own)


def add_kernel(a, b, out):
    out[...] = (a[...].astype(F32) + b[...].astype(F32)).astype(BF16)


def put(g, c, outs, at, rows, k):
    count = g.shape[0] // (2 * rows)
    g = g.astype(BF16).reshape(count, 2, rows, g.shape[1])
    even, odd = g[:, 0], g[:, 1]
    mine, theirs = outs
    mine[at : at + count, k * rows : (k + 1) * rows] = jnp.where(c == 0, even, odd)
    theirs[at : at + count, k * rows : (k + 1) * rows] = jnp.where(c == 0, odd, even)


def weight_second_kernel(taps, nears, c_ref, h_a, h_b, shifted_a, shifted_b, mine, theirs, *rest):
    own_rows, width = mine.shape[1] // taps, mine.shape[2]
    c = c_ref[0]
    step = 256
    count = h_a.shape[1] // step
    rest = list(rest)
    pairs, first, later = [], [], [[] for _ in range(count)]
    for near, h, x in ((nears[0], h_a, shifted_a), (nears[1], h_b, shifted_b)):
        if not near:
            h_held, x_held, h_sem, x_sem = rest[:4]
            rest = rest[4:]
            first.append(pltpu.make_async_copy(x, x_held, x_sem))
            for q in range(count):
                cut = slice(q * step, (q + 1) * step)
                later[q].append(
                    pltpu.make_async_copy(h.at[:, cut], h_held.at[:, cut], h_sem.at[q])
                )
            h, x = h_held, x_held
        pairs.append((h, x))
    for copy in first + sum(later, []):
        copy.start()
    for copy in first:
        copy.wait()
    for q in range(count):
        for copy in later[q]:
            copy.wait()
        cut = slice(q * step, (q + 1) * step)
        g = sum(dot_rows(h[:, cut], x[...]) for h, x in pairs)
        for k in range(taps):
            put(g[:, k * width : (k + 1) * width], c, (mine, theirs),
                q * step // (2 * own_rows), own_rows, k)


def weight_first_kernel(
    normaliser, taps, nears, c_ref, loss_a, loss_b, *refs,
):
    *sources, phases_a, phases_b, mine, theirs, padded, moved = refs[:16]
    rest = list(refs[16:])
    rows, width = sources[0].shape
    half = rows // 2
    frames = padded.shape[1] - 8
    c = c_ref[0]
    small, large = [], []
    if not nears[0]:
        got, sems = rest[:2]
        rest = rest[2:]
        for n, x in enumerate(sources):
            small.append(pltpu.make_async_copy(x, got.at[n, : x.shape[0]], sems.at[n]))
        sources = [got.at[n, : x.shape[0]] for n, x in enumerate(sources)]
    phases = []
    for near, x in zip(nears[1:], (phases_a, phases_b)):
        if not near:
            held, sem = rest[:2]
            rest = rest[2:]
            large.append(pltpu.make_async_copy(x, held, sem))
            x = held
        phases.append(x)
    for copy in small + large:
        copy.start()
    for copy in small:
        copy.wait()
    padded[:, frames:, :] = jnp.zeros((padded.shape[0], 8, width), F32)
    for n in range(2):
        h, own, a, b = (sources[2 * at + n] for at in range(4))
        difference, root = difference_terms(h[:half], h[half:rows])
        slope = difference / root / normaliser
        for at, sign in ((0, 1.0), (half, -1.0)):
            cut = slice(at, at + half)
            up = own[cut].astype(F32) + a[cut].astype(F32) + b[cut].astype(F32)
            up = up.astype(BF16).astype(F32)
            gate = jnp.where(h[cut].astype(F32) > 0, 1.0, leak_slope)
            delta = ((sign * slope + up) * gate).astype(BF16)
            base = n * rows + at
            moved[base : base + half, :width] = delta
            cols, lead = half // frames, base // frames
            padded[lead : lead + cols, :frames, :] = delta.astype(F32).reshape(cols, frames, width)
    moved[:, width:] = padded[:, 1 : 1 + frames, :].reshape(2 * rows, width).astype(BF16)
    groups = mine.shape[0]
    own_rows = (mine.shape[1] - 8) // taps
    outs = (mine, theirs)
    for copy in large:
        copy.wait()
    for p in range(3):
        lanes = width if p == 0 else 2 * width
        g = dot_rows(phases[0][p], moved[:rows, :lanes])
        g = g + dot_rows(phases[1][p], moved[rows:, :lanes])
        put(g[:, :width], c, outs, 0, own_rows, 2 + p)
        if p > 0:
            put(g[:, width:], c, outs, 0, own_rows, p - 1)
    total = loss_a[...].astype(F32) + loss_b[...].astype(F32)
    for x in sources[4:]:
        total = total + x[rows:].astype(F32)
    lines = split_rows(jnp.sum(total, axis=0, keepdims=True), 3 * c)
    for x in outs:
        x[:, taps * own_rows :, :] = jnp.broadcast_to(lines[None], (groups, 8, width))


def same_kernel(a, out):
    out[...] = a[...]


def join_kernel(at, a, b, joint, summed, sem):
    summed[...] = (a[...].astype(F32) + b[...].astype(F32)).astype(BF16)
    copy = pltpu.make_async_copy(summed, joint.at[:, at : at + summed.shape[1]], sem)
    copy.start()
    copy.wait()


def join_late_kernel(at, a, b, held, joint, summed, sem):
    del held
    join_kernel(at, a, b, joint, summed, sem)


def total_kernel(taps, count_all, blocks, second, first, loss):
    total = jnp.sum(blocks[...].astype(F32), axis=0)
    at = 0
    for out in (second, first):
        rows = taps * out.shape[1]
        out[...] = total[at : at + rows].reshape(out.shape)
        at += rows
    lines = total[at:]
    loss[0] = jnp.sum(lines[:, :128]) / count_all
    loss[1] = jnp.sum(lines[:, 128:]) / count_all


def call(
    kernel, operands, outs, scratch=(), smem=0, hbm=(), loose=(), after=(), smem_outs=(),
    hbm_outs=(), aliases={}, flops=0, cost=1, name=None,
):
    moved = sum(x.size * x.dtype.itemsize for x in operands)
    moved += sum(x.size * x.dtype.itemsize for x in outs)
    vmem, small = pl.BlockSpec(memory_space=pltpu.VMEM), pl.BlockSpec(memory_space=pltpu.SMEM)
    far, anywhere = pl.BlockSpec(memory_space=pltpu.HBM), pl.BlockSpec(memory_space=pl.ANY)
    count = len(operands)
    operands = tuple(
        pltpu.with_memory_space_constraint(x, pltpu.HBM) if at in hbm else x
        for at, x in enumerate(operands)
    )

    def body(*refs):
        kernel(*refs[:count], *refs[count + len(after) :])

    return pl.pallas_call(
        body,
        out_shape=[
            pltpu.HBM(x.shape, x.dtype) if at in hbm_outs else x for at, x in enumerate(outs)
        ],
        in_specs=[
            small if at < smem else far if at in hbm else anywhere if at in loose else vmem
            for at in range(count)
        ]
        + [anywhere] * len(after),
        out_specs=[
            small if at in smem_outs else far if at in hbm_outs else vmem
            for at in range(len(outs))
        ],
        scratch_shapes=list(scratch),
        input_output_aliases=aliases,
        compiler_params=pltpu.CompilerParams(vmem_limit_bytes=VMEM_LIMIT),
        cost_estimate=pl.CostEstimate(
            flops=int(flops * cost), bytes_accessed=int(moved * cost), transcendentals=0
        ),
        name=name,
    )(*operands, *after)


def like(shape, dtype=BF16):
    return jax.ShapeDtypeStruct(shape, dtype)


def turn(x, step):
    count = lax.axis_size("section")
    return lax.ppermute(x, "section", [(i, (i + step) % count) for i in range(count)])


def later(x, after, name):
    return call(same_kernel, (x,), [like(x.shape)], after=after, name=name)[0]


def added(a, b, name, after=()):
    return call(add_kernel, (a, b), [like(a.shape)], after=after, name=name)[0]


def other_core(x):
    return lax.ppermute(x, "dp_2", [(0, 1), (1, 0)])


def shards(real_in, fake_in, kernel_first, kernel_second):
    replicas = lax.axis_size(DP)
    cols, span, in_width = real_in.shape
    frames = span // 3
    taps, width_all, width = kernel_second.shape
    normaliser = float(cols * frames)
    count_all = float(cols * replicas * frames * width_all)
    groups = replicas // 2
    part = cols // 2
    rows = cols * frames
    s = lax.axis_index("section").reshape(1).astype(jnp.int32)
    c = lax.axis_index("dp_2").reshape(1).astype(jnp.int32)
    dma = pltpu.SemaphoreType.DMA
    chunk_outs = [like((rows, width)), like((3, rows, in_width)), like((8, 128), F32)]
    conv_scratch = [pltpu.VMEM((cols, frames + 8, width), F32)]
    phases_far = [pltpu.VMEM((3, rows, in_width), BF16), dma]
    all_far = [pltpu.VMEM((rows, width_all), BF16), pltpu.VMEM((rows, taps * width), BF16)]
    flops = 2 * rows * taps * in_width * width

    h_a, phases_a, loss_a, w_first, rest = call(
        first_early_kernel,
        (real_in, fake_in, kernel_first),
        chunk_outs + [like(kernel_first.shape), like((cols, span, in_width))],
        conv_scratch
        + [pltpu.VMEM((cols, span, in_width), BF16), dma((cols,)), dma((2,)), dma]
        + phases_far * (not NEAR_PHASES[0]),
        hbm=(0, 1, 2),
        hbm_outs=() if NEAR_PHASES[0] else (1,),
        flops=flops,
        name="first_a",
    )
    prev_a = turn(h_a, 1)
    following_a = turn(h_a, -1)
    h_b, phases_b, loss_b, w_second = call(
        first_late_kernel,
        (rest, w_first, kernel_second),
        chunk_outs + [like(kernel_second.shape)],
        conv_scratch + [dma] + phases_far * (not NEAR_PHASES[1]),
        hbm=(2,),
        hbm_outs=() if NEAR_PHASES[1] else (1,),
        flops=flops,
        cost=1,
        name="first_b",
    )
    far_a = turn(prev_a, 1)
    following_b = turn(h_b, -1)
    prev_b = turn(h_b, 1)
    far_b = turn(later(following_b, (following_a, h_a, prev_a, w_second), "ordered"), -1)

    second_outs = [like((rows, width_all)), like((rows, taps * width)), like((rows + 8, width)),
                   like((8, width))]
    back_outs = [like((rows + 8, width)), like((rows + 8, width)), like((rows, width))]
    second_scratch = [
        pltpu.VMEM((cols, frames + 16, width), F32), dma((4,)),
    ]
    copies = all_far + [dma, dma]
    flops = 2 * rows * taps * (width_all + width) * width
    all_a, shifted_a, far_t, loss_a, next_t, prev_t, own_a = call(
        functools.partial(second_kernel, normaliser, True, NEAR_ALL[0]),
        (s, h_a, prev_a, following_a, far_a, w_second, loss_a),
        second_outs + back_outs,
        second_scratch + copies * (not NEAR_ALL[0]),
        smem=1,
        loose=(1, 2, 3, 4),
        hbm_outs=() if NEAR_ALL[0] else (0, 1),
        cost=1,
        flops=flops,
        name="second_a",
    )
    pass_a = turn(far_t, 1)
    from_following_a = turn(prev_t, -1)
    relayed_a = added(next_t, pass_a, "relay_a")
    from_prev_a = turn(relayed_a, 1)

    all_b, shifted_b, far_t, loss_b = call(
        functools.partial(second_kernel, normaliser, False, NEAR_ALL[1]),
        (s, h_b, prev_b, following_b, far_b, w_second, loss_b),
        second_outs,
        second_scratch + copies * (not NEAR_ALL[1]),
        smem=1,
        loose=(1, 2, 3, 4),
        hbm_outs=() if NEAR_ALL[1] else (0, 1),
        cost=1,
        after=(loss_a,),
        flops=flops,
        name="second_b",
    )
    pass_b = turn(far_t, -1)
    next_t, prev_t, own_b = call(
        back_kernel,
        (s, shifted_b, w_second, loss_b),
        back_outs,
        [] if NEAR_ALL[1] else [pltpu.VMEM((rows, taps * width), BF16), dma],
        smem=1,
        hbm=() if NEAR_ALL[1] else (1,),
        cost=4,
        flops=2 * rows * taps * width * width * 3,
        after=(relayed_a, from_following_a),
        name="back_b",
    )
    from_prev_b = turn(next_t, 1)
    relayed_b = added(prev_t, pass_b, "relay_b")
    from_following_b = turn(relayed_b, -1)

    own_rows = width_all // replicas
    mine_second, theirs = call(
        functools.partial(weight_second_kernel, taps, NEAR_ALL),
        (c, all_a, all_b, shifted_a, shifted_b),
        [like((groups, taps * own_rows, width))] * 2,
        (all_far + [dma((width_all // 256,)), dma]) * (2 - sum(NEAR_ALL)),
        smem=1,
        hbm=tuple(at for at in (1, 2, 3, 4) if not NEAR_ALL[(at - 1) % 2]),
        cost=4,
        after=(relayed_a, relayed_b),
        flops=4 * rows * taps * width * width_all,
        name="weight_second",
    )
    first_rows = in_width // replicas
    size_second, size_first = taps * own_rows, taps * first_rows + 8
    joint_like = like((groups, size_second + size_first, width))
    (joint,) = call(
        functools.partial(join_kernel, 0),
        (mine_second, other_core(theirs)),
        [joint_like],
        [pltpu.VMEM((groups, size_second, width), BF16), dma],
        hbm_outs=(0,),
        name="join_second",
    )

    mine_first, theirs = call(
        functools.partial(weight_first_kernel, normaliser, taps, (NEAR_SMALL, *NEAR_PHASES)),
        (c, loss_a, loss_b, h_a, h_b, own_a, own_b, from_prev_a, from_prev_b, from_following_a,
         from_following_b, pass_a, pass_b, phases_a, phases_b),
        [like((groups, taps * first_rows + 8, width))] * 2,
        [pltpu.VMEM((2 * cols, frames + 8, width), F32), pltpu.VMEM((2 * rows, 2 * width), BF16)]
        + [pltpu.VMEM((10, rows + 8, width), BF16), dma((10,))] * (not NEAR_SMALL)
        + phases_far * (2 - sum(NEAR_PHASES)),
        smem=1,
        hbm=tuple(at for at in (13, 14) if not NEAR_PHASES[at - 13]),
        loose=() if NEAR_SMALL else tuple(range(3, 13)),
        cost=20,
        after=(mine_second,),
        flops=4 * rows * taps * width * in_width,
        name="weight_first",
    )
    (joint,) = call(
        functools.partial(join_late_kernel, size_second),
        (mine_first, other_core(theirs), joint),
        [joint_like],
        [pltpu.VMEM((groups, size_first, width), BF16), dma],
        hbm=(2,),
        hbm_outs=(0,),
        aliases={2: 0},
        name="join_first",
    )
    blocks = lax.all_to_all(joint, ZY, 0, 0)
    grad_second, grad_first, layer_loss = call(
        functools.partial(total_kernel, taps, count_all),
        (blocks,),
        [like((taps, own_rows, width), F32), like((taps, first_rows, width), F32),
         like((2,), F32)],
        smem_outs=(2,),
        name="total",
    )
    return (layer_loss, jnp.transpose(grad_first, (1, 0, 2)), jnp.transpose(grad_second, (1, 0, 2)))


def solution(mesh):
    finer = Mesh(
        mesh.devices.reshape(4, 4, 2, mesh.shape["section"]), ("dp_0", "dp_1", "dp_2", "section")
    )
    return jax.shard_map(
        shards,
        mesh=finer,
        in_specs=(
            P(DP, None, None),
            P(DP, None, None),
            P(None, None, "section"),
            P(None, None, "section"),
        ),
        out_specs=(P(), P(DP, None, "section"), P(DP, None, "section")),
        check_vma=False,
    )
```

```python
import functools

import jax
import jax.numpy as jnp
from jax import lax
from jax.experimental import pallas as pl
from jax.experimental.pallas import tpu as pltpu
from jax.sharding import Mesh
from jax.sharding import PartitionSpec as P

DP = ("dp_0", "dp_1", "dp_2")
ZY = ("dp_0", "dp_1")
F32 = jnp.float32
BF16 = jnp.bfloat16
VMEM_LIMIT = 16 << 20
NEAR_PHASES = (False, False)
NEAR_ALL = (True, True)
NEAR_SMALL = True

smooth_width = 0.1
leak_slope = 0.1


def leaky(pre):
    return jnp.where(pre > 0, pre, leak_slope * pre).astype(BF16)


def fold_rows(x):
    x = jnp.sum(x.reshape(-1, 8, x.shape[1]), axis=0)
    return sum(x[:, at : at + 128] for at in range(0, x.shape[1], 128))


def difference_terms(real, fake):
    difference = real.astype(F32) - fake.astype(F32)
    square = difference * difference + smooth_width * smooth_width
    inverse = lax.rsqrt(square)
    return difference * inverse, square * inverse


def dot(a, b):
    return jnp.dot(a, b, preferred_element_type=F32)


def dot_rows(a, b):
    return lax.dot_general(a, b, (((0,), (0,)), ((), ())), preferred_element_type=F32)


def dot_lanes(a, b):
    return lax.dot_general(a, b, (((1,), (1,)), ((), ())), preferred_element_type=F32)


def losses_split(first, second):
    value = jnp.sum(jnp.concatenate([first, second], axis=1), axis=0, keepdims=True)
    return split_rows(value, 0)


def split_rows(value, base):
    row = lax.broadcasted_iota(jnp.int32, (8, value.shape[1]), 0) - base
    high = value.astype(BF16).astype(F32)
    middle = (value - high).astype(BF16).astype(F32)
    low = value - high - middle
    out = jnp.where(row == 0, high, jnp.where(row == 1, middle, jnp.where(row == 2, low, 0.0)))
    return out.astype(BF16)


def strided_conv(take, cols, span, w, h_out, phases_out, loss, padded, *far):
    phases = far[0] if far else phases_out
    frames = span // 3
    rows = 2 * cols * frames
    width = w.shape[2]
    row = lax.broadcasted_iota(jnp.int32, (span, span), 0)
    col = lax.broadcasted_iota(jnp.int32, (span, span), 1)
    phase = jnp.where(row >= 2 * frames, 2, jnp.where(row >= frames, 1, 0))
    select = (col == 3 * (row - frames * phase) + phase).astype(F32).astype(BF16)
    for n in range(2 * cols):
        parts = dot(select, take(n)).astype(BF16)
        for p in range(3):
            phases[p, n * frames : (n + 1) * frames, :] = parts[p * frames : (p + 1) * frames]
    if far:
        copy_out = pltpu.make_async_copy(phases, phases_out, far[1])
        copy_out.start()
    padded[:, :8, :] = jnp.zeros((2 * cols, 8, width), F32)
    earlier = dot(phases[1], w[0]) + dot(phases[2], w[1])
    padded[:, 8 : 8 + frames, :] = earlier.reshape(2 * cols, frames, width)
    same = dot(phases[0], w[2]) + dot(phases[1], w[3]) + dot(phases[2], w[4])
    h = leaky(same + padded[:, 7 : 7 + frames, :].reshape(rows, width))
    h_out[...] = h
    _, root = difference_terms(h[: rows // 2], h[rows // 2 :])
    loss[...] = fold_rows(root - smooth_width)
    if far:
        copy_out.wait()


def copies_of(source, target, sems):
    return [
        pltpu.make_async_copy(source.at[n], target.at[n], sems.at[n])
        for n in range(source.shape[0])
    ]


def first_early_kernel(
    real, fake, w_hbm, h_out, phases_out, loss, w, rest,
    padded, held, held_sem, rest_sem, w_sem, *far_scratch,
):
    cols = held.shape[0] // 2
    span = held.shape[1]
    for n in range(2 * cols):
        source = real if n < cols else fake
        pltpu.make_async_copy(source.at[n % cols], held.at[n], held_sem.at[n]).start()
    w_copies = copies_of(w_hbm, w, w_sem)
    for copy in w_copies:
        copy.start()
    rest_copies = [
        pltpu.make_async_copy(x.at[cols:], rest.at[at * cols : (at + 1) * cols], rest_sem.at[at])
        for at, x in enumerate((real, fake))
    ]

    def take(n):
        source = real if n < cols else fake
        pltpu.make_async_copy(source.at[n % cols], held.at[n], held_sem.at[n]).wait()
        if n == 2 * cols - 1:
            for copy in rest_copies:
                copy.start()
            for copy in w_copies:
                copy.wait()
        return held[n]

    strided_conv(take, cols, span, w, h_out, phases_out, loss, padded, *far_scratch)
    for copy in rest_copies:
        copy.wait()


def first_late_kernel(rest, w, w_next_hbm, h_out, phases_out, loss, w_next, padded, sem, *far):
    copies = copies_of(w_next_hbm, w_next, sem)
    for copy in copies:
        copy.start()
    cols, span = rest.shape[0] // 2, rest.shape[1]
    strided_conv(lambda n: rest[n], cols, span, w, h_out, phases_out, loss, padded, *far)
    for copy in copies:
        copy.wait()


def second_kernel(
    normaliser, whole, near, s_ref, own, prev, following, far, w, loss_first,
    all_out, shifted_out, far_t, loss, *rest,
):
    if near:
        h_all, shifted = all_out, shifted_out
        *backs, padded, in_sems = rest
    else:
        *backs, padded, in_sems, h_all, shifted, all_sem, shifted_sem = rest
    rows, width = own.shape
    half = rows // 2
    taps = w.shape[0]
    frames = padded.shape[1] - 16
    s = s_ref[0]
    copies = []
    for away, x in enumerate((own, following, far, prev)):
        at = pl.multiple_of(lax.rem(s + away, 4) * width, 256)
        copies.append(
            pltpu.make_async_copy(x, h_all.at[:, pl.ds(at, width)], in_sems.at[away])
        )
        copies[-1].start()
    for copy in copies:
        copy.wait()
    if not near:
        copy_all = pltpu.make_async_copy(h_all, all_out, all_sem)
        copy_all.start()
    zeros = jnp.zeros((padded.shape[0], 8, width), F32)
    padded[:, :8, :] = zeros
    padded[:, 8 + frames :, :] = zeros
    pre = dot(h_all[...], w[2])
    for k in (0, 1, 3, 4):
        padded[:, 8 : 8 + frames, :] = dot(h_all[...], w[k]).reshape(-1, frames, width)
        pre = pre + padded[:, 6 + k : 6 + k + frames, :].reshape(rows, width)
    h = leaky(pre)
    slope, root = difference_terms(h[:half], h[half:])
    loss_rows = losses_split(loss_first[...], fold_rows(root - smooth_width))
    loss[...] = loss_rows
    slope = slope * (1.0 / normaliser)
    for value, sign, at in ((h[:half], 1.0, 0), (h[half:], -1.0, half // frames)):
        gate = jnp.where(value.astype(F32) > 0, 1.0, leak_slope)
        delta = (sign * slope * gate).astype(BF16).astype(F32)
        padded[at : at + half // frames, 8 : 8 + frames, :] = delta.reshape(-1, frames, width)
    for k in range(taps):
        moved = padded[:, 10 - k : 10 - k + frames, :].reshape(rows, width)
        shifted[:, k * width : (k + 1) * width] = moved.astype(BF16)
    if not near:
        copy_shifted = pltpu.make_async_copy(shifted, shifted_out, shifted_sem)
        copy_shifted.start()
    far_t[:rows] = back_term(s, 2, shifted, w)
    far_t[rows:] = loss_rows
    if whole:
        back_rest(s, shifted, w, loss_rows, 3, *backs)
    if not near:
        copy_all.wait()
        copy_shifted.wait()


def back_term(s, away, shifted, w):
    width = w.shape[2]
    at = pl.multiple_of(lax.rem(s + away, 4) * width, 256)
    term = None
    for k in range(w.shape[0]):
        part = dot_lanes(shifted[:, k * width : (k + 1) * width], w[k, pl.ds(at, width), :])
        term = part if term is None else term + part
    return term.astype(BF16)


def back_rest(s, shifted, w, loss_rows, with_loss, following, prev, own):
    rows = own.shape[0]
    for away, out in ((1, following), (3, prev)) if with_loss == 1 else ((3, prev), (1, following)):
        out[:rows] = back_term(s, away, shifted, w)
        out[rows:] = loss_rows if away == with_loss else jnp.zeros_like(loss_rows)
    own[...] = back_term(s, 0, shifted, w)


def back_kernel(s_ref, shifted, w, loss, following, prev, own, *rest):
    if rest:
        held, sem = rest
        copy = pltpu.make_async_copy(shifted, held, sem)
        copy.start()
        copy.wait()
        shifted = held
    back_rest(s_ref[0], shifted, w, loss[...], 1, following, prev, own)


def add_kernel(a, b, out):
    out[...] = (a[...].astype(F32) + b[...].astype(F32)).astype(BF16)


def put(g, c, outs, at, rows, k):
    count = g.shape[0] // (2 * rows)
    g = g.astype(BF16).reshape(count, 2, rows, g.shape[1])
    even, odd = g[:, 0], g[:, 1]
    mine, theirs = outs
    mine[at : at + count, k * rows : (k + 1) * rows] = jnp.where(c == 0, even, odd)
    theirs[at : at + count, k * rows : (k + 1) * rows] = jnp.where(c == 0, odd, even)


def weight_second_kernel(taps, nears, c_ref, h_a, h_b, shifted_a, shifted_b, mine, theirs, *rest):
    own_rows, width = mine.shape[1] // taps, mine.shape[2]
    c = c_ref[0]
    step = 256
    count = h_a.shape[1] // step
    rest = list(rest)
    pairs, first, later = [], [], [[] for _ in range(count)]
    for near, h, x in ((nears[0], h_a, shifted_a), (nears[1], h_b, shifted_b)):
        if not near:
            h_held, x_held, h_sem, x_sem = rest[:4]
            rest = rest[4:]
            first.append(pltpu.make_async_copy(x, x_held, x_sem))
            for q in range(count):
                cut = slice(q * step, (q + 1) * step)
                later[q].append(
                    pltpu.make_async_copy(h.at[:, cut], h_held.at[:, cut], h_sem.at[q])
                )
            h, x = h_held, x_held
        pairs.append((h, x))
    for copy in first + sum(later, []):
        copy.start()
    for copy in first:
        copy.wait()
    for q in range(count):
        for copy in later[q]:
            copy.wait()
        cut = slice(q * step, (q + 1) * step)
        g = sum(dot_rows(h[:, cut], x[...]) for h, x in pairs)
        for k in range(taps):
            put(g[:, k * width : (k + 1) * width], c, (mine, theirs),
                q * step // (2 * own_rows), own_rows, k)


def weight_first_kernel(
    normaliser, taps, nears, c_ref, loss_a, loss_b, *refs,
):
    *sources, phases_a, phases_b, mine, theirs, padded, moved = refs[:16]
    rest = list(refs[16:])
    rows, width = sources[0].shape
    half = rows // 2
    frames = padded.shape[1] - 8
    c = c_ref[0]
    small, large = [], []
    if not nears[0]:
        got, sems = rest[:2]
        rest = rest[2:]
        for n, x in enumerate(sources):
            small.append(pltpu.make_async_copy(x, got.at[n, : x.shape[0]], sems.at[n]))
        sources = [got.at[n, : x.shape[0]] for n, x in enumerate(sources)]
    phases = []
    for near, x in zip(nears[1:], (phases_a, phases_b)):
        if not near:
            held, sem = rest[:2]
            rest = rest[2:]
            large.append(copies_of(x, held, sem))
            x = held
        phases.append(x)
    for copy in small + [copies[p] for p in range(3) for copies in large]:
        copy.start()
    for copy in small:
        copy.wait()
    padded[:, frames:, :] = jnp.zeros((padded.shape[0], 8, width), F32)
    for n in range(2):
        h, own, a, b = (sources[2 * at + n] for at in range(4))
        slope, _ = difference_terms(h[:half], h[half:rows])
        slope = slope * (1.0 / normaliser)
        for at, sign in ((0, 1.0), (half, -1.0)):
            cut = slice(at, at + half)
            up = own[cut].astype(F32) + a[cut].astype(F32) + b[cut].astype(F32)
            up = up.astype(BF16).astype(F32)
            gate = jnp.where(h[cut].astype(F32) > 0, 1.0, leak_slope)
            delta = ((sign * slope + up) * gate).astype(BF16)
            base = n * rows + at
            moved[base : base + half, :width] = delta
            cols, lead = half // frames, base // frames
            padded[lead : lead + cols, :frames, :] = delta.astype(F32).reshape(cols, frames, width)
    moved[:, width:] = padded[:, 1 : 1 + frames, :].reshape(2 * rows, width).astype(BF16)
    groups = mine.shape[0]
    own_rows = (mine.shape[1] - 8) // taps
    outs = (mine, theirs)
    for p in range(3):
        for copies in large:
            copies[p].wait()
        lanes = width if p == 0 else 2 * width
        g = dot_rows(phases[0][p], moved[:rows, :lanes])
        g = g + dot_rows(phases[1][p], moved[rows:, :lanes])
        put(g[:, :width], c, outs, 0, own_rows, 2 + p)
        if p > 0:
            put(g[:, width:], c, outs, 0, own_rows, p - 1)
    total = loss_a[...].astype(F32) + loss_b[...].astype(F32)
    for x in sources[4:]:
        total = total + x[rows:].astype(F32)
    lines = split_rows(jnp.sum(total, axis=0, keepdims=True), 3 * c)
    for x in outs:
        x[:, taps * own_rows :, :] = jnp.broadcast_to(lines[None], (groups, 8, width))


def join_kernel(at, a, b, joint, summed, sems):
    count = sems.shape[0]
    step = a.shape[0] // count
    copies = []
    for n in range(count):
        cut = slice(n * step, (n + 1) * step)
        summed[cut] = (a[cut].astype(F32) + b[cut].astype(F32)).astype(BF16)
        copies.append(
            pltpu.make_async_copy(
                summed.at[cut], joint.at[cut, at : at + summed.shape[1]], sems.at[n]
            )
        )
        copies[-1].start()
    for copy in copies:
        copy.wait()


def join_late_kernel(at, a, b, held, joint, summed, sem):
    del held
    join_kernel(at, a, b, joint, summed, sem)


def total_kernel(taps, count_all, blocks, second, first, loss):
    total = jnp.sum(blocks[...].astype(F32), axis=0)
    at = 0
    for out in (second, first):
        rows = taps * out.shape[1]
        out[...] = total[at : at + rows].reshape(out.shape)
        at += rows
    lines = total[at:]
    loss[0] = jnp.sum(lines[:, :128]) / count_all
    loss[1] = jnp.sum(lines[:, 128:]) / count_all


def call(
    kernel, operands, outs, scratch=(), smem=0, hbm=(), loose=(), after=(), smem_outs=(),
    hbm_outs=(), aliases={}, flops=0, cost=1, name=None,
):
    moved = sum(x.size * x.dtype.itemsize for x in operands)
    moved += sum(x.size * x.dtype.itemsize for x in outs)
    vmem, small = pl.BlockSpec(memory_space=pltpu.VMEM), pl.BlockSpec(memory_space=pltpu.SMEM)
    far, anywhere = pl.BlockSpec(memory_space=pltpu.HBM), pl.BlockSpec(memory_space=pl.ANY)
    count = len(operands)
    operands = tuple(
        pltpu.with_memory_space_constraint(x, pltpu.HBM) if at in hbm else x
        for at, x in enumerate(operands)
    )

    def body(*refs):
        kernel(*refs[:count], *refs[count + len(after) :])

    return pl.pallas_call(
        body,
        out_shape=[
            pltpu.HBM(x.shape, x.dtype) if at in hbm_outs else x for at, x in enumerate(outs)
        ],
        in_specs=[
            small if at < smem else far if at in hbm else anywhere if at in loose else vmem
            for at in range(count)
        ]
        + [anywhere] * len(after),
        out_specs=[
            small if at in smem_outs else far if at in hbm_outs else vmem
            for at in range(len(outs))
        ],
        scratch_shapes=list(scratch),
        input_output_aliases=aliases,
        compiler_params=pltpu.CompilerParams(vmem_limit_bytes=VMEM_LIMIT),
        cost_estimate=pl.CostEstimate(
            flops=int(flops * cost), bytes_accessed=int(moved * cost), transcendentals=0
        ),
        name=name,
    )(*operands, *after)


def like(shape, dtype=BF16):
    return jax.ShapeDtypeStruct(shape, dtype)


def turn(x, step):
    count = lax.axis_size("section")
    return lax.ppermute(x, "section", [(i, (i + step) % count) for i in range(count)])


def added(a, b, name, after=()):
    return call(add_kernel, (a, b), [like(a.shape)], after=after, name=name)[0]


def other_core(x):
    return lax.ppermute(x, "dp_2", [(0, 1), (1, 0)])


def shards(real_in, fake_in, kernel_first, kernel_second):
    replicas = lax.axis_size(DP)
    cols, span, in_width = real_in.shape
    frames = span // 3
    taps, width_all, width = kernel_second.shape
    normaliser = float(cols * frames)
    count_all = float(cols * replicas * frames * width_all)
    groups = replicas // 2
    part = cols // 2
    rows = cols * frames
    s = lax.axis_index("section").reshape(1).astype(jnp.int32)
    c = lax.axis_index("dp_2").reshape(1).astype(jnp.int32)
    dma = pltpu.SemaphoreType.DMA
    chunk_outs = [like((rows, width)), like((3, rows, in_width)), like((8, 128), F32)]
    conv_scratch = [pltpu.VMEM((cols, frames + 8, width), F32)]
    phases_far = [pltpu.VMEM((3, rows, in_width), BF16), dma]
    all_far = [pltpu.VMEM((rows, width_all), BF16), pltpu.VMEM((rows, taps * width), BF16)]
    flops = 2 * rows * taps * in_width * width

    h_a, phases_a, loss_a, w_first, rest = call(
        first_early_kernel,
        (real_in, fake_in, kernel_first),
        chunk_outs + [like(kernel_first.shape), like((cols, span, in_width))],
        conv_scratch
        + [pltpu.VMEM((cols, span, in_width), BF16), dma((cols,)), dma((2,)), dma((taps,))]
        + phases_far * (not NEAR_PHASES[0]),
        hbm=(0, 1, 2),
        hbm_outs=() if NEAR_PHASES[0] else (1,),
        flops=flops,
        name="first_a",
    )
    prev_a = turn(h_a, 1)
    following_a = turn(h_a, -1)
    h_b, phases_b, loss_b, w_second = call(
        first_late_kernel,
        (rest, w_first, kernel_second),
        chunk_outs + [like(kernel_second.shape)],
        conv_scratch + [dma((taps,))] + phases_far * (not NEAR_PHASES[1]),
        hbm=(2,),
        hbm_outs=() if NEAR_PHASES[1] else (1,),
        flops=flops,
        cost=1,
        name="first_b",
    )
    far_a = turn(prev_a, 1)
    following_b = turn(h_b, -1)
    prev_b = turn(h_b, 1)
    far_b = turn(following_b, -1)

    second_outs = [like((rows, width_all)), like((rows, taps * width)), like((rows + 8, width)),
                   like((8, width))]
    back_outs = [like((rows + 8, width)), like((rows + 8, width)), like((rows, width))]
    second_scratch = [
        pltpu.VMEM((cols, frames + 16, width), F32), dma((4,)),
    ]
    copies = all_far + [dma, dma]
    flops = 2 * rows * taps * (width_all + width) * width
    all_a, shifted_a, far_t, loss_a, next_t, prev_t, own_a = call(
        functools.partial(second_kernel, normaliser, True, NEAR_ALL[0]),
        (s, h_a, prev_a, following_a, far_a, w_second, loss_a),
        second_outs + back_outs,
        second_scratch + copies * (not NEAR_ALL[0]),
        smem=1,
        loose=(1, 2, 3, 4),
        hbm_outs=() if NEAR_ALL[0] else (0, 1),
        cost=1,
        flops=flops,
        name="second_a",
    )
    pass_a = turn(far_t, 1)
    from_following_a = turn(prev_t, -1)
    relayed_a = added(next_t, pass_a, "relay_a")
    from_prev_a = turn(relayed_a, 1)

    all_b, shifted_b, far_t, loss_b = call(
        functools.partial(second_kernel, normaliser, False, NEAR_ALL[1]),
        (s, h_b, prev_b, following_b, far_b, w_second, loss_b),
        second_outs,
        second_scratch + copies * (not NEAR_ALL[1]),
        smem=1,
        loose=(1, 2, 3, 4),
        hbm_outs=() if NEAR_ALL[1] else (0, 1),
        cost=1,
        after=(own_a,),
        flops=flops,
        name="second_b",
    )
    pass_b = turn(far_t, -1)
    next_t, prev_t, own_b = call(
        back_kernel,
        (s, shifted_b, w_second, loss_b),
        back_outs,
        [] if NEAR_ALL[1] else [pltpu.VMEM((rows, taps * width), BF16), dma],
        smem=1,
        hbm=() if NEAR_ALL[1] else (1,),
        cost=4,
        flops=2 * rows * taps * width * width * 3,
        name="back_b",
    )
    from_prev_b = turn(next_t, 1)
    relayed_b = added(prev_t, pass_b, "relay_b")
    from_following_b = turn(relayed_b, -1)

    own_rows = width_all // replicas
    mine_second, theirs = call(
        functools.partial(weight_second_kernel, taps, NEAR_ALL),
        (c, all_a, all_b, shifted_a, shifted_b),
        [like((groups, taps * own_rows, width))] * 2,
        (all_far + [dma((width_all // 256,)), dma]) * (2 - sum(NEAR_ALL)),
        smem=1,
        hbm=tuple(at for at in (1, 2, 3, 4) if not NEAR_ALL[(at - 1) % 2]),
        cost=4,
        after=(relayed_a, relayed_b),
        flops=4 * rows * taps * width * width_all,
        name="weight_second",
    )
    first_rows = in_width // replicas
    size_second, size_first = taps * own_rows, taps * first_rows + 8
    joint_like = like((groups, size_second + size_first, width))
    (joint,) = call(
        functools.partial(join_kernel, 0),
        (mine_second, other_core(theirs)),
        [joint_like],
        [pltpu.VMEM((groups, size_second, width), BF16), dma((4,))],
        hbm_outs=(0,),
        name="join_second",
    )

    mine_first, theirs = call(
        functools.partial(weight_first_kernel, normaliser, taps, (NEAR_SMALL, *NEAR_PHASES)),
        (c, loss_a, loss_b, h_a, h_b, own_a, own_b, from_prev_a, from_prev_b, from_following_a,
         from_following_b, pass_a, pass_b, phases_a, phases_b),
        [like((groups, taps * first_rows + 8, width))] * 2,
        [pltpu.VMEM((2 * cols, frames + 8, width), F32), pltpu.VMEM((2 * rows, 2 * width), BF16)]
        + [pltpu.VMEM((10, rows + 8, width), BF16), dma((10,))] * (not NEAR_SMALL)
        + [phases_far[0], dma((3,))] * (2 - sum(NEAR_PHASES)),
        smem=1,
        hbm=tuple(at for at in (13, 14) if not NEAR_PHASES[at - 13]),
        loose=() if NEAR_SMALL else tuple(range(3, 13)),
        cost=20,
        after=(mine_second,),
        flops=4 * rows * taps * width * in_width,
        name="weight_first",
    )
    (joint,) = call(
        functools.partial(join_late_kernel, size_second),
        (mine_first, other_core(theirs), joint),
        [joint_like],
        [pltpu.VMEM((groups, size_first, width), BF16), dma((4,))],
        hbm=(2,),
        hbm_outs=(0,),
        aliases={2: 0},
        name="join_first",
    )
    blocks = lax.all_to_all(joint, ZY, 0, 0)
    grad_second, grad_first, layer_loss = call(
        functools.partial(total_kernel, taps, count_all),
        (blocks,),
        [like((taps, own_rows, width), F32), like((taps, first_rows, width), F32),
         like((2,), F32)],
        smem_outs=(2,),
        name="total",
    )
    return (layer_loss, jnp.transpose(grad_first, (1, 0, 2)), jnp.transpose(grad_second, (1, 0, 2)))


def solution(mesh):
    finer = Mesh(
        mesh.devices.reshape(4, 4, 2, mesh.shape["section"]), ("dp_0", "dp_1", "dp_2", "section")
    )
    return jax.shard_map(
        shards,
        mesh=finer,
        in_specs=(
            P(DP, None, None),
            P(DP, None, None),
            P(None, None, "section"),
            P(None, None, "section"),
        ),
        out_specs=(P(), P(DP, None, "section"), P(DP, None, "section")),
        check_vma=False,
    )
```

```python
import functools

import jax
import jax.numpy as jnp
from jax import lax
from jax.experimental import pallas as pl
from jax.experimental.pallas import tpu as pltpu
from jax.sharding import Mesh
from jax.sharding import PartitionSpec as P

DP = ("dp_0", "dp_1", "dp_2")
ZY = ("dp_0", "dp_1")
F32 = jnp.float32
BF16 = jnp.bfloat16
VMEM_LIMIT = 16 << 20
NEAR_PHASES = (True, False)
NEAR_ALL = (True, True)
NEAR_SMALL = True

smooth_width = 0.1
leak_slope = 0.1


def leaky(pre):
    return jnp.where(pre > 0, pre, leak_slope * pre).astype(BF16)


def fold_rows(x):
    x = jnp.sum(x.reshape(-1, 8, x.shape[1]), axis=0)
    return sum(x[:, at : at + 128] for at in range(0, x.shape[1], 128))


def difference_terms(real, fake):
    difference = real.astype(F32) - fake.astype(F32)
    square = difference * difference + smooth_width * smooth_width
    inverse = lax.rsqrt(square)
    return difference * inverse, square * inverse


def dot(a, b):
    return jnp.dot(a, b, preferred_element_type=F32)


def dot_rows(a, b):
    return lax.dot_general(a, b, (((0,), (0,)), ((), ())), preferred_element_type=F32)


def dot_lanes(a, b):
    return lax.dot_general(a, b, (((1,), (1,)), ((), ())), preferred_element_type=F32)


def losses_split(first, second):
    value = jnp.sum(jnp.concatenate([first, second], axis=1), axis=0, keepdims=True)
    return split_rows(value, 0)


def split_rows(value, base):
    row = lax.broadcasted_iota(jnp.int32, (8, value.shape[1]), 0) - base
    high = value.astype(BF16).astype(F32)
    middle = (value - high).astype(BF16).astype(F32)
    low = value - high - middle
    out = jnp.where(row == 0, high, jnp.where(row == 1, middle, jnp.where(row == 2, low, 0.0)))
    return out.astype(BF16)


def strided_conv(take, cols, span, w, h_out, phases_out, loss, padded, *far):
    phases = far[0] if far else phases_out
    frames = span // 3
    rows = 2 * cols * frames
    width = w.shape[2]
    row = lax.broadcasted_iota(jnp.int32, (span, span), 0)
    col = lax.broadcasted_iota(jnp.int32, (span, span), 1)
    phase = jnp.where(row >= 2 * frames, 2, jnp.where(row >= frames, 1, 0))
    select = (col == 3 * (row - frames * phase) + phase).astype(F32).astype(BF16)
    for n in range(2 * cols):
        parts = dot(select, take(n)).astype(BF16)
        for p in range(3):
            phases[p, n * frames : (n + 1) * frames, :] = parts[p * frames : (p + 1) * frames]
    if far:
        copy_out = pltpu.make_async_copy(phases, phases_out, far[1])
        copy_out.start()
    padded[:, :8, :] = jnp.zeros((2 * cols, 8, width), F32)
    earlier = dot(phases[1], w[0]) + dot(phases[2], w[1])
    padded[:, 8 : 8 + frames, :] = earlier.reshape(2 * cols, frames, width)
    same = dot(phases[0], w[2]) + dot(phases[1], w[3]) + dot(phases[2], w[4])
    h = leaky(same + padded[:, 7 : 7 + frames, :].reshape(rows, width))
    h_out[...] = h
    _, root = difference_terms(h[: rows // 2], h[rows // 2 :])
    loss[...] = fold_rows(root - smooth_width)
    if far:
        copy_out.wait()


def copies_of(source, target, sems):
    return [
        pltpu.make_async_copy(source.at[n], target.at[n], sems.at[n])
        for n in range(source.shape[0])
    ]


def first_early_kernel(
    real, fake, w_hbm, h_out, phases_out, loss, w, rest,
    padded, held, held_sem, rest_sem, w_sem, *far_scratch,
):
    cols = held.shape[0] // 2
    span = held.shape[1]
    for n in range(2 * cols):
        source = real if n < cols else fake
        pltpu.make_async_copy(source.at[n % cols], held.at[n], held_sem.at[n]).start()
    w_copies = copies_of(w_hbm, w, w_sem)
    for copy in w_copies:
        copy.start()
    rest_copies = [
        pltpu.make_async_copy(x.at[cols:], rest.at[at * cols : (at + 1) * cols], rest_sem.at[at])
        for at, x in enumerate((real, fake))
    ]

    for copy in rest_copies:
        copy.start()

    def take(n):
        source = real if n < cols else fake
        pltpu.make_async_copy(source.at[n % cols], held.at[n], held_sem.at[n]).wait()
        if n == 2 * cols - 1:
            for copy in w_copies:
                copy.wait()
        return held[n]

    strided_conv(take, cols, span, w, h_out, phases_out, loss, padded, *far_scratch)
    for copy in rest_copies:
        copy.wait()


def first_late_kernel(rest, w, w_next_hbm, h_out, phases_out, loss, w_next, padded, sem, *far):
    copies = copies_of(w_next_hbm, w_next, sem)
    for copy in copies:
        copy.start()
    cols, span = rest.shape[0] // 2, rest.shape[1]
    strided_conv(lambda n: rest[n], cols, span, w, h_out, phases_out, loss, padded, *far)
    for copy in copies:
        copy.wait()


def second_kernel(
    normaliser, whole, near, s_ref, own, prev, following, far, w, loss_first,
    all_out, shifted_out, far_t, loss, *rest,
):
    if near:
        h_all, shifted = all_out, shifted_out
        *backs, padded, in_sems = rest
    else:
        *backs, padded, in_sems, h_all, shifted, all_sem, shifted_sem = rest
    rows, width = own.shape
    half = rows // 2
    taps = w.shape[0]
    frames = padded.shape[1] - 16
    s = s_ref[0]
    copies = []
    for away, x in enumerate((own, following, far, prev)):
        at = pl.multiple_of(lax.rem(s + away, 4) * width, 256)
        copies.append(
            pltpu.make_async_copy(x, h_all.at[:, pl.ds(at, width)], in_sems.at[away])
        )
        copies[-1].start()
    for copy in copies:
        copy.wait()
    if not near:
        copy_all = pltpu.make_async_copy(h_all, all_out, all_sem)
        copy_all.start()
    zeros = jnp.zeros((padded.shape[0], 8, width), F32)
    padded[:, :8, :] = zeros
    padded[:, 8 + frames :, :] = zeros
    pre = dot(h_all[...], w[2])
    for k in (0, 1, 3, 4):
        padded[:, 8 : 8 + frames, :] = dot(h_all[...], w[k]).reshape(-1, frames, width)
        pre = pre + padded[:, 6 + k : 6 + k + frames, :].reshape(rows, width)
    h = leaky(pre)
    slope, root = difference_terms(h[:half], h[half:])
    loss_rows = losses_split(loss_first[...], fold_rows(root - smooth_width))
    loss[...] = loss_rows
    slope = slope * (1.0 / normaliser)
    for value, sign, at in ((h[:half], 1.0, 0), (h[half:], -1.0, half // frames)):
        gate = jnp.where(value.astype(F32) > 0, 1.0, leak_slope)
        delta = (sign * slope * gate).astype(BF16).astype(F32)
        padded[at : at + half // frames, 8 : 8 + frames, :] = delta.reshape(-1, frames, width)
    for k in range(taps):
        moved = padded[:, 10 - k : 10 - k + frames, :].reshape(rows, width)
        shifted[:, k * width : (k + 1) * width] = moved.astype(BF16)
    if not near:
        copy_shifted = pltpu.make_async_copy(shifted, shifted_out, shifted_sem)
        copy_shifted.start()
    far_t[:rows] = back_term(s, 2, shifted, w)
    far_t[rows:] = loss_rows
    if whole:
        back_rest(s, shifted, w, loss_rows, 3, *backs)
    if not near:
        copy_all.wait()
        copy_shifted.wait()


def back_term(s, away, shifted, w):
    width = w.shape[2]
    at = pl.multiple_of(lax.rem(s + away, 4) * width, 256)
    term = None
    for k in range(w.shape[0]):
        part = dot_lanes(shifted[:, k * width : (k + 1) * width], w[k, pl.ds(at, width), :])
        term = part if term is None else term + part
    return term.astype(BF16)


def back_rest(s, shifted, w, loss_rows, with_loss, following, prev, own):
    rows = own.shape[0]
    for away, out in ((1, following), (3, prev)) if with_loss == 1 else ((3, prev), (1, following)):
        out[:rows] = back_term(s, away, shifted, w)
        out[rows:] = loss_rows if away == with_loss else jnp.zeros_like(loss_rows)
    own[...] = back_term(s, 0, shifted, w)


def back_kernel(s_ref, shifted, w, loss, following, prev, own, *rest):
    if rest:
        held, sem = rest
        copy = pltpu.make_async_copy(shifted, held, sem)
        copy.start()
        copy.wait()
        shifted = held
    back_rest(s_ref[0], shifted, w, loss[...], 1, following, prev, own)


def add_kernel(a, b, out):
    out[...] = (a[...].astype(F32) + b[...].astype(F32)).astype(BF16)


def put(g, c, outs, at, rows, k):
    count = g.shape[0] // (2 * rows)
    g = g.astype(BF16).reshape(count, 2, rows, g.shape[1])
    even, odd = g[:, 0], g[:, 1]
    mine, theirs = outs
    mine[at : at + count, k * rows : (k + 1) * rows] = jnp.where(c == 0, even, odd)
    theirs[at : at + count, k * rows : (k + 1) * rows] = jnp.where(c == 0, odd, even)


def weight_second_kernel(taps, nears, c_ref, h_a, h_b, shifted_a, shifted_b, mine, theirs, *rest):
    own_rows, width = mine.shape[1] // taps, mine.shape[2]
    c = c_ref[0]
    step = 256
    count = h_a.shape[1] // step
    rest = list(rest)
    pairs, first, later = [], [], [[] for _ in range(count)]
    for near, h, x in ((nears[0], h_a, shifted_a), (nears[1], h_b, shifted_b)):
        if not near:
            h_held, x_held, h_sem, x_sem = rest[:4]
            rest = rest[4:]
            first.append(pltpu.make_async_copy(x, x_held, x_sem))
            for q in range(count):
                cut = slice(q * step, (q + 1) * step)
                later[q].append(
                    pltpu.make_async_copy(h.at[:, cut], h_held.at[:, cut], h_sem.at[q])
                )
            h, x = h_held, x_held
        pairs.append((h, x))
    for copy in first + sum(later, []):
        copy.start()
    for copy in first:
        copy.wait()
    for q in range(count):
        for copy in later[q]:
            copy.wait()
        cut = slice(q * step, (q + 1) * step)
        g = sum(dot_rows(h[:, cut], x[...]) for h, x in pairs)
        for k in range(taps):
            put(g[:, k * width : (k + 1) * width], c, (mine, theirs),
                q * step // (2 * own_rows), own_rows, k)


def weight_first_kernel(
    normaliser, taps, nears, c_ref, loss_a, loss_b, *refs,
):
    *sources, phases_a, phases_b, mine, theirs, padded, moved = refs[:16]
    rest = list(refs[16:])
    rows, width = sources[0].shape
    half = rows // 2
    frames = padded.shape[1] - 8
    c = c_ref[0]
    small, large = [], []
    if not nears[0]:
        got, sems = rest[:2]
        rest = rest[2:]
        for n, x in enumerate(sources):
            small.append(pltpu.make_async_copy(x, got.at[n, : x.shape[0]], sems.at[n]))
        sources = [got.at[n, : x.shape[0]] for n, x in enumerate(sources)]
    phases = []
    for near, x in zip(nears[1:], (phases_a, phases_b)):
        if not near:
            held, sem = rest[:2]
            rest = rest[2:]
            large.append(pltpu.make_async_copy(x, held, sem))
            x = held
        phases.append(x)
    for copy in small + large:
        copy.start()
    for copy in small:
        copy.wait()
    padded[:, frames:, :] = jnp.zeros((padded.shape[0], 8, width), F32)
    for n in range(2):
        h, own, a, b = (sources[2 * at + n] for at in range(4))
        slope, _ = difference_terms(h[:half], h[half:rows])
        slope = slope * (1.0 / normaliser)
        for at, sign in ((0, 1.0), (half, -1.0)):
            cut = slice(at, at + half)
            up = own[cut].astype(F32) + a[cut].astype(F32) + b[cut].astype(F32)
            up = up.astype(BF16).astype(F32)
            gate = jnp.where(h[cut].astype(F32) > 0, 1.0, leak_slope)
            delta = ((sign * slope + up) * gate).astype(BF16)
            base = n * rows + at
            moved[base : base + half, :width] = delta
            cols, lead = half // frames, base // frames
            padded[lead : lead + cols, :frames, :] = delta.astype(F32).reshape(cols, frames, width)
    moved[:, width:] = padded[:, 1 : 1 + frames, :].reshape(2 * rows, width).astype(BF16)
    groups = mine.shape[0]
    own_rows = (mine.shape[1] - 8) // taps
    outs = (mine, theirs)
    for copy in large:
        copy.wait()
    for p in range(3):
        lanes = width if p == 0 else 2 * width
        g = dot_rows(phases[0][p], moved[:rows, :lanes])
        g = g + dot_rows(phases[1][p], moved[rows:, :lanes])
        put(g[:, :width], c, outs, 0, own_rows, 2 + p)
        if p > 0:
            put(g[:, width:], c, outs, 0, own_rows, p - 1)
    total = loss_a[...].astype(F32) + loss_b[...].astype(F32)
    for x in sources[4:]:
        total = total + x[rows:].astype(F32)
    lines = split_rows(jnp.sum(total, axis=0, keepdims=True), 3 * c)
    for x in outs:
        x[:, taps * own_rows :, :] = jnp.broadcast_to(lines[None], (groups, 8, width))


def join_kernel(at, a, b, joint, summed, sems):
    count = sems.shape[0]
    step = a.shape[0] // count
    copies = []
    for n in range(count):
        cut = slice(n * step, (n + 1) * step)
        summed[cut] = (a[cut].astype(F32) + b[cut].astype(F32)).astype(BF16)
        copies.append(
            pltpu.make_async_copy(
                summed.at[cut], joint.at[cut, at : at + summed.shape[1]], sems.at[n]
            )
        )
        copies[-1].start()
    for copy in copies:
        copy.wait()


def join_late_kernel(at, a, b, held, joint, summed, sem):
    del held
    join_kernel(at, a, b, joint, summed, sem)


def total_kernel(taps, count_all, blocks, second, first, loss):
    total = jnp.sum(blocks[...].astype(F32), axis=0)
    at = 0
    for out in (second, first):
        rows = taps * out.shape[1]
        out[...] = total[at : at + rows].reshape(out.shape)
        at += rows
    lines = total[at:]
    loss[0] = jnp.sum(lines[:, :128]) / count_all
    loss[1] = jnp.sum(lines[:, 128:]) / count_all


def call(
    kernel, operands, outs, scratch=(), smem=0, hbm=(), loose=(), after=(), smem_outs=(),
    hbm_outs=(), aliases={}, flops=0, cost=1, name=None,
):
    moved = sum(x.size * x.dtype.itemsize for x in operands)
    moved += sum(x.size * x.dtype.itemsize for x in outs)
    vmem, small = pl.BlockSpec(memory_space=pltpu.VMEM), pl.BlockSpec(memory_space=pltpu.SMEM)
    far, anywhere = pl.BlockSpec(memory_space=pltpu.HBM), pl.BlockSpec(memory_space=pl.ANY)
    count = len(operands)
    operands = tuple(
        pltpu.with_memory_space_constraint(x, pltpu.HBM) if at in hbm else x
        for at, x in enumerate(operands)
    )

    def body(*refs):
        kernel(*refs[:count], *refs[count + len(after) :])

    return pl.pallas_call(
        body,
        out_shape=[
            pltpu.HBM(x.shape, x.dtype) if at in hbm_outs else x for at, x in enumerate(outs)
        ],
        in_specs=[
            small if at < smem else far if at in hbm else anywhere if at in loose else vmem
            for at in range(count)
        ]
        + [anywhere] * len(after),
        out_specs=[
            small if at in smem_outs else far if at in hbm_outs else vmem
            for at in range(len(outs))
        ],
        scratch_shapes=list(scratch),
        input_output_aliases=aliases,
        compiler_params=pltpu.CompilerParams(vmem_limit_bytes=VMEM_LIMIT),
        cost_estimate=pl.CostEstimate(
            flops=int(flops * cost), bytes_accessed=int(moved * cost), transcendentals=0
        ),
        name=name,
    )(*operands, *after)


def like(shape, dtype=BF16):
    return jax.ShapeDtypeStruct(shape, dtype)


def turn(x, step):
    count = lax.axis_size("section")
    return lax.ppermute(x, "section", [(i, (i + step) % count) for i in range(count)])


def added(a, b, name, after=()):
    return call(add_kernel, (a, b), [like(a.shape)], after=after, name=name)[0]


def other_core(x):
    return lax.ppermute(x, "dp_2", [(0, 1), (1, 0)])


def shards(real_in, fake_in, kernel_first, kernel_second):
    replicas = lax.axis_size(DP)
    cols, span, in_width = real_in.shape
    frames = span // 3
    taps, width_all, width = kernel_second.shape
    normaliser = float(cols * frames)
    count_all = float(cols * replicas * frames * width_all)
    groups = replicas // 2
    part = cols // 2
    rows = cols * frames
    s = lax.axis_index("section").reshape(1).astype(jnp.int32)
    c = lax.axis_index("dp_2").reshape(1).astype(jnp.int32)
    dma = pltpu.SemaphoreType.DMA
    chunk_outs = [like((rows, width)), like((3, rows, in_width)), like((8, 128), F32)]
    conv_scratch = [pltpu.VMEM((cols, frames + 8, width), F32)]
    phases_far = [pltpu.VMEM((3, rows, in_width), BF16), dma]
    all_far = [pltpu.VMEM((rows, width_all), BF16), pltpu.VMEM((rows, taps * width), BF16)]
    flops = 2 * rows * taps * in_width * width

    h_a, phases_a, loss_a, w_first, rest = call(
        first_early_kernel,
        (real_in, fake_in, kernel_first),
        chunk_outs + [like(kernel_first.shape), like((cols, span, in_width))],
        conv_scratch
        + [pltpu.VMEM((cols, span, in_width), BF16), dma((cols,)), dma((2,)), dma((taps,))]
        + phases_far * (not NEAR_PHASES[0]),
        hbm=(0, 1, 2),
        hbm_outs=() if NEAR_PHASES[0] else (1,),
        flops=flops,
        name="first_a",
    )
    prev_a = turn(h_a, 1)
    following_a = turn(h_a, -1)
    h_b, phases_b, loss_b, w_second = call(
        first_late_kernel,
        (rest, w_first, kernel_second),
        chunk_outs + [like(kernel_second.shape)],
        conv_scratch + [dma((taps,))] + phases_far * (not NEAR_PHASES[1]),
        hbm=(2,),
        hbm_outs=() if NEAR_PHASES[1] else (1,),
        flops=flops,
        cost=1,
        name="first_b",
    )
    far_a = turn(prev_a, 1)
    following_b = turn(h_b, -1)
    prev_b = turn(h_b, 1)
    far_b = turn(following_b, -1)

    second_outs = [like((rows, width_all)), like((rows, taps * width)), like((rows + 8, width)),
                   like((8, width))]
    back_outs = [like((rows + 8, width)), like((rows + 8, width)), like((rows, width))]
    second_scratch = [
        pltpu.VMEM((cols, frames + 16, width), F32), dma((4,)),
    ]
    copies = all_far + [dma, dma]
    flops = 2 * rows * taps * (width_all + width) * width
    all_a, shifted_a, far_t, loss_a, next_t, prev_t, own_a = call(
        functools.partial(second_kernel, normaliser, True, NEAR_ALL[0]),
        (s, h_a, prev_a, following_a, far_a, w_second, loss_a),
        second_outs + back_outs,
        second_scratch + copies * (not NEAR_ALL[0]),
        smem=1,
        loose=(1, 2, 3, 4),
        hbm_outs=() if NEAR_ALL[0] else (0, 1),
        cost=1,
        flops=flops,
        name="second_a",
    )
    pass_a = turn(far_t, 1)
    from_following_a = turn(prev_t, -1)
    relayed_a = added(next_t, pass_a, "relay_a")
    from_prev_a = turn(relayed_a, 1)

    all_b, shifted_b, far_t, loss_b = call(
        functools.partial(second_kernel, normaliser, False, NEAR_ALL[1]),
        (s, h_b, prev_b, following_b, far_b, w_second, loss_b),
        second_outs,
        second_scratch + copies * (not NEAR_ALL[1]),
        smem=1,
        loose=(1, 2, 3, 4),
        hbm_outs=() if NEAR_ALL[1] else (0, 1),
        cost=1,
        after=(own_a,),
        flops=flops,
        name="second_b",
    )
    pass_b = turn(far_t, -1)
    next_t, prev_t, own_b = call(
        back_kernel,
        (s, shifted_b, w_second, loss_b),
        back_outs,
        [] if NEAR_ALL[1] else [pltpu.VMEM((rows, taps * width), BF16), dma],
        smem=1,
        hbm=() if NEAR_ALL[1] else (1,),
        cost=4,
        flops=2 * rows * taps * width * width * 3,
        name="back_b",
    )
    from_prev_b = turn(next_t, 1)
    relayed_b = added(prev_t, pass_b, "relay_b")
    from_following_b = turn(relayed_b, -1)

    own_rows = width_all // replicas
    mine_second, theirs = call(
        functools.partial(weight_second_kernel, taps, NEAR_ALL),
        (c, all_a, all_b, shifted_a, shifted_b),
        [like((groups, taps * own_rows, width))] * 2,
        (all_far + [dma((width_all // 256,)), dma]) * (2 - sum(NEAR_ALL)),
        smem=1,
        hbm=tuple(at for at in (1, 2, 3, 4) if not NEAR_ALL[(at - 1) % 2]),
        cost=4,
        after=(relayed_a, relayed_b),
        flops=4 * rows * taps * width * width_all,
        name="weight_second",
    )
    first_rows = in_width // replicas
    size_second, size_first = taps * own_rows, taps * first_rows + 8
    joint_like = like((groups, size_second + size_first, width))
    (joint,) = call(
        functools.partial(join_kernel, 0),
        (mine_second, other_core(theirs)),
        [joint_like],
        [pltpu.VMEM((groups, size_second, width), BF16), dma((4,))],
        hbm_outs=(0,),
        name="join_second",
    )

    mine_first, theirs = call(
        functools.partial(weight_first_kernel, normaliser, taps, (NEAR_SMALL, *NEAR_PHASES)),
        (c, loss_a, loss_b, h_a, h_b, own_a, own_b, from_prev_a, from_prev_b, from_following_a,
         from_following_b, pass_a, pass_b, phases_a, phases_b),
        [like((groups, taps * first_rows + 8, width))] * 2,
        [pltpu.VMEM((2 * cols, frames + 8, width), F32), pltpu.VMEM((2 * rows, 2 * width), BF16)]
        + [pltpu.VMEM((10, rows + 8, width), BF16), dma((10,))] * (not NEAR_SMALL)
        + phases_far * (2 - sum(NEAR_PHASES)),
        smem=1,
        hbm=tuple(at for at in (13, 14) if not NEAR_PHASES[at - 13]),
        loose=() if NEAR_SMALL else tuple(range(3, 13)),
        cost=20,
        after=(mine_second,),
        flops=4 * rows * taps * width * in_width,
        name="weight_first",
    )
    (joint,) = call(
        functools.partial(join_late_kernel, size_second),
        (mine_first, other_core(theirs), joint),
        [joint_like],
        [pltpu.VMEM((groups, size_first, width), BF16), dma((4,))],
        hbm=(2,),
        hbm_outs=(0,),
        aliases={2: 0},
        name="join_first",
    )
    blocks = lax.all_to_all(joint, ZY, 0, 0)
    grad_second, grad_first, layer_loss = call(
        functools.partial(total_kernel, taps, count_all),
        (blocks,),
        [like((taps, own_rows, width), F32), like((taps, first_rows, width), F32),
         like((2,), F32)],
        smem_outs=(2,),
        name="total",
    )
    return (layer_loss, jnp.transpose(grad_first, (1, 0, 2)), jnp.transpose(grad_second, (1, 0, 2)))


def solution(mesh):
    finer = Mesh(
        mesh.devices.reshape(4, 4, 2, mesh.shape["section"]), ("dp_0", "dp_1", "dp_2", "section")
    )
    return jax.shard_map(
        shards,
        mesh=finer,
        in_specs=(
            P(DP, None, None),
            P(DP, None, None),
            P(None, None, "section"),
            P(None, None, "section"),
        ),
        out_specs=(P(), P(DP, None, "section"), P(DP, None, "section")),
        check_vma=False,
    )
```

```python
import functools

import jax
import jax.numpy as jnp
from jax import lax
from jax.experimental import pallas as pl
from jax.experimental.pallas import tpu as pltpu
from jax.sharding import Mesh
from jax.sharding import PartitionSpec as P

DP = ("dp_0", "dp_1", "dp_2")
ZY = ("dp_0", "dp_1")
F32 = jnp.float32
BF16 = jnp.bfloat16
VMEM_LIMIT = 16 << 20
NEAR_PHASES = (True, False)
NEAR_ALL = (True, True)
NEAR_SMALL = True

smooth_width = 0.1
leak_slope = 0.1


def leaky(pre):
    return jnp.where(pre > 0, pre, leak_slope * pre).astype(BF16)


def fold_rows(x):
    x = jnp.sum(x.reshape(-1, 8, x.shape[1]), axis=0)
    return sum(x[:, at : at + 128] for at in range(0, x.shape[1], 128))


def difference_terms(real, fake):
    difference = real.astype(F32) - fake.astype(F32)
    square = difference * difference + smooth_width * smooth_width
    inverse = lax.rsqrt(square)
    return difference * inverse, square * inverse


def dot(a, b):
    return jnp.dot(a, b, preferred_element_type=F32)


def dot_rows(a, b):
    return lax.dot_general(a, b, (((0,), (0,)), ((), ())), preferred_element_type=F32)


def dot_lanes(a, b):
    return lax.dot_general(a, b, (((1,), (1,)), ((), ())), preferred_element_type=F32)


def losses_split(first, second):
    value = jnp.sum(jnp.concatenate([first, second], axis=1), axis=0, keepdims=True)
    return split_rows(value, 0)


def split_rows(value, base):
    row = lax.broadcasted_iota(jnp.int32, (8, value.shape[1]), 0) - base
    high = value.astype(BF16).astype(F32)
    middle = (value - high).astype(BF16).astype(F32)
    low = value - high - middle
    out = jnp.where(row == 0, high, jnp.where(row == 1, middle, jnp.where(row == 2, low, 0.0)))
    return out.astype(BF16)


def strided_conv(take, cols, span, w, h_out, phases_out, loss, padded, *far):
    phases = far[0] if far else phases_out
    frames = span // 3
    rows = 2 * cols * frames
    width = w.shape[2]
    row = lax.broadcasted_iota(jnp.int32, (span, span), 0)
    col = lax.broadcasted_iota(jnp.int32, (span, span), 1)
    phase = jnp.where(row >= 2 * frames, 2, jnp.where(row >= frames, 1, 0))
    select = (col == 3 * (row - frames * phase) + phase).astype(F32).astype(BF16)
    for n in range(2 * cols):
        parts = dot(select, take(n)).astype(BF16)
        for p in range(3):
            phases[p, n * frames : (n + 1) * frames, :] = parts[p * frames : (p + 1) * frames]
    if far:
        copy_out = pltpu.make_async_copy(phases, phases_out, far[1])
        copy_out.start()
    padded[:, :8, :] = jnp.zeros((2 * cols, 8, width), F32)
    earlier = dot(phases[1], w[0]) + dot(phases[2], w[1])
    padded[:, 8 : 8 + frames, :] = earlier.reshape(2 * cols, frames, width)
    same = dot(phases[0], w[2]) + dot(phases[1], w[3]) + dot(phases[2], w[4])
    h = leaky(same + padded[:, 7 : 7 + frames, :].reshape(rows, width))
    h_out[...] = h
    _, root = difference_terms(h[: rows // 2], h[rows // 2 :])
    loss[...] = fold_rows(root - smooth_width)
    if far:
        copy_out.wait()


def copies_of(source, target, sems):
    return [
        pltpu.make_async_copy(source.at[n], target.at[n], sems.at[n])
        for n in range(source.shape[0])
    ]


def first_early_kernel(
    real, fake, w_hbm, h_out, phases_out, loss, w, rest,
    padded, held, held_sem, rest_sem, w_sem, *far_scratch,
):
    cols = held.shape[0] // 2
    span = held.shape[1]
    for n in range(2 * cols):
        source = real if n < cols else fake
        pltpu.make_async_copy(source.at[n % cols], held.at[n], held_sem.at[n]).start()
    w_copies = copies_of(w_hbm, w, w_sem)
    for copy in w_copies:
        copy.start()
    rest_copies = [
        pltpu.make_async_copy(x.at[cols:], rest.at[at * cols : (at + 1) * cols], rest_sem.at[at])
        for at, x in enumerate((real, fake))
    ]

    for copy in rest_copies:
        copy.start()

    def take(n):
        source = real if n < cols else fake
        pltpu.make_async_copy(source.at[n % cols], held.at[n], held_sem.at[n]).wait()
        if n == 2 * cols - 1:
            for copy in w_copies:
                copy.wait()
        return held[n]

    strided_conv(take, cols, span, w, h_out, phases_out, loss, padded, *far_scratch)
    for copy in rest_copies:
        copy.wait()


def first_late_kernel(rest, w, w_next_hbm, h_out, phases_out, loss, w_next, padded, sem, *far):
    copies = copies_of(w_next_hbm, w_next, sem)
    for copy in copies:
        copy.start()
    cols, span = rest.shape[0] // 2, rest.shape[1]
    strided_conv(lambda n: rest[n], cols, span, w, h_out, phases_out, loss, padded, *far)
    for copy in copies:
        copy.wait()


def second_kernel(
    normaliser, whole, near, s_ref, own, prev, following, far_r, far_f, w, loss_first,
    all_out, shifted_out, far_t, loss, *rest,
):
    if near:
        h_all, shifted = all_out, shifted_out
        *backs, padded, in_sems = rest
    else:
        *backs, padded, in_sems, h_all, shifted, all_sem, shifted_sem = rest
    rows, width = own.shape
    half = rows // 2
    taps = w.shape[0]
    frames = padded.shape[1] - 16
    s = s_ref[0]
    copies = []
    for x, away, top in (
        (own, 0, 0), (following, 1, 0), (far_r, 2, 0), (far_f, 2, half), (prev, 3, 0)
    ):
        at = pl.multiple_of(lax.rem(s + away, 4) * width, 256)
        target = h_all.at[top : top + x.shape[0], pl.ds(at, width)]
        copies.append(pltpu.make_async_copy(x, target, in_sems.at[len(copies)]))
        copies[-1].start()
    for copy in copies:
        copy.wait()
    if not near:
        copy_all = pltpu.make_async_copy(h_all, all_out, all_sem)
        copy_all.start()
    zeros = jnp.zeros((padded.shape[0], 8, width), F32)
    padded[:, :8, :] = zeros
    padded[:, 8 + frames :, :] = zeros
    pre = dot(h_all[...], w[2])
    for k in (0, 1, 3, 4):
        padded[:, 8 : 8 + frames, :] = dot(h_all[...], w[k]).reshape(-1, frames, width)
        pre = pre + padded[:, 6 + k : 6 + k + frames, :].reshape(rows, width)
    h = leaky(pre)
    slope, root = difference_terms(h[:half], h[half:])
    loss_rows = losses_split(loss_first[...], fold_rows(root - smooth_width))
    loss[...] = loss_rows
    slope = slope * (1.0 / normaliser)
    for value, sign, at in ((h[:half], 1.0, 0), (h[half:], -1.0, half // frames)):
        gate = jnp.where(value.astype(F32) > 0, 1.0, leak_slope)
        delta = (sign * slope * gate).astype(BF16).astype(F32)
        padded[at : at + half // frames, 8 : 8 + frames, :] = delta.reshape(-1, frames, width)
    for k in range(taps):
        moved = padded[:, 10 - k : 10 - k + frames, :].reshape(rows, width)
        shifted[:, k * width : (k + 1) * width] = moved.astype(BF16)
    if not near:
        copy_shifted = pltpu.make_async_copy(shifted, shifted_out, shifted_sem)
        copy_shifted.start()
    far_t[:rows] = back_term(s, 2, shifted, w)
    far_t[rows:] = loss_rows
    if whole:
        back_rest(s, shifted, w, loss_rows, 3, *backs)
    if not near:
        copy_all.wait()
        copy_shifted.wait()


def back_term(s, away, shifted, w):
    width = w.shape[2]
    at = pl.multiple_of(lax.rem(s + away, 4) * width, 256)
    term = None
    for k in range(w.shape[0]):
        part = dot_lanes(shifted[:, k * width : (k + 1) * width], w[k, pl.ds(at, width), :])
        term = part if term is None else term + part
    return term.astype(BF16)


def back_rest(s, shifted, w, loss_rows, with_loss, following, prev, own):
    rows = own.shape[0]
    for away, out in ((1, following), (3, prev)) if with_loss == 1 else ((3, prev), (1, following)):
        out[:rows] = back_term(s, away, shifted, w)
        out[rows:] = loss_rows if away == with_loss else jnp.zeros_like(loss_rows)
    own[...] = back_term(s, 0, shifted, w)


def back_kernel(s_ref, shifted, w, loss, following, prev, own, *rest):
    if rest:
        held, sem = rest
        copy = pltpu.make_async_copy(shifted, held, sem)
        copy.start()
        copy.wait()
        shifted = held
    back_rest(s_ref[0], shifted, w, loss[...], 1, following, prev, own)


def add_kernel(a, b, out):
    out[...] = (a[...].astype(F32) + b[...].astype(F32)).astype(BF16)


def put(g, c, outs, at, rows, k):
    count = g.shape[0] // (2 * rows)
    g = g.astype(BF16).reshape(count, 2, rows, g.shape[1])
    even, odd = g[:, 0], g[:, 1]
    mine, theirs = outs
    mine[at : at + count, k * rows : (k + 1) * rows] = jnp.where(c == 0, even, odd)
    theirs[at : at + count, k * rows : (k + 1) * rows] = jnp.where(c == 0, odd, even)


def weight_second_kernel(taps, nears, c_ref, h_a, h_b, shifted_a, shifted_b, mine, theirs, *rest):
    own_rows, width = mine.shape[1] // taps, mine.shape[2]
    c = c_ref[0]
    step = 256
    count = h_a.shape[1] // step
    rest = list(rest)
    pairs, first, later = [], [], [[] for _ in range(count)]
    for near, h, x in ((nears[0], h_a, shifted_a), (nears[1], h_b, shifted_b)):
        if not near:
            h_held, x_held, h_sem, x_sem = rest[:4]
            rest = rest[4:]
            first.append(pltpu.make_async_copy(x, x_held, x_sem))
            for q in range(count):
                cut = slice(q * step, (q + 1) * step)
                later[q].append(
                    pltpu.make_async_copy(h.at[:, cut], h_held.at[:, cut], h_sem.at[q])
                )
            h, x = h_held, x_held
        pairs.append((h, x))
    for copy in first + sum(later, []):
        copy.start()
    for copy in first:
        copy.wait()
    for q in range(count):
        for copy in later[q]:
            copy.wait()
        cut = slice(q * step, (q + 1) * step)
        g = sum(dot_rows(h[:, cut], x[...]) for h, x in pairs)
        for k in range(taps):
            put(g[:, k * width : (k + 1) * width], c, (mine, theirs),
                q * step // (2 * own_rows), own_rows, k)


def weight_first_kernel(
    normaliser, taps, nears, c_ref, loss_a, loss_b, *refs,
):
    *sources, phases_a, phases_b, mine, theirs, padded, moved = refs[:16]
    rest = list(refs[16:])
    rows, width = sources[0].shape
    half = rows // 2
    frames = padded.shape[1] - 8
    c = c_ref[0]
    small, large = [], []
    if not nears[0]:
        got, sems = rest[:2]
        rest = rest[2:]
        for n, x in enumerate(sources):
            small.append(pltpu.make_async_copy(x, got.at[n, : x.shape[0]], sems.at[n]))
        sources = [got.at[n, : x.shape[0]] for n, x in enumerate(sources)]
    phases = []
    for near, x in zip(nears[1:], (phases_a, phases_b)):
        if not near:
            held, sem = rest[:2]
            rest = rest[2:]
            large.append(pltpu.make_async_copy(x, held, sem))
            x = held
        phases.append(x)
    for copy in small + large:
        copy.start()
    for copy in small:
        copy.wait()
    padded[:, frames:, :] = jnp.zeros((padded.shape[0], 8, width), F32)
    for n in range(2):
        h, own, a, b = (sources[2 * at + n] for at in range(4))
        slope, _ = difference_terms(h[:half], h[half:rows])
        slope = slope * (1.0 / normaliser)
        for at, sign in ((0, 1.0), (half, -1.0)):
            cut = slice(at, at + half)
            up = own[cut].astype(F32) + a[cut].astype(F32) + b[cut].astype(F32)
            up = up.astype(BF16).astype(F32)
            gate = jnp.where(h[cut].astype(F32) > 0, 1.0, leak_slope)
            delta = ((sign * slope + up) * gate).astype(BF16)
            base = n * rows + at
            moved[base : base + half, :width] = delta
            cols, lead = half // frames, base // frames
            padded[lead : lead + cols, :frames, :] = delta.astype(F32).reshape(cols, frames, width)
    moved[:, width:] = padded[:, 1 : 1 + frames, :].reshape(2 * rows, width).astype(BF16)
    groups = mine.shape[0]
    own_rows = (mine.shape[1] - 8) // taps
    outs = (mine, theirs)
    for copy in large:
        copy.wait()
    for p in range(3):
        lanes = width if p == 0 else 2 * width
        g = dot_rows(phases[0][p], moved[:rows, :lanes])
        g = g + dot_rows(phases[1][p], moved[rows:, :lanes])
        put(g[:, :width], c, outs, 0, own_rows, 2 + p)
        if p > 0:
            put(g[:, width:], c, outs, 0, own_rows, p - 1)
    total = loss_a[...].astype(F32) + loss_b[...].astype(F32)
    for x in sources[4:]:
        total = total + x[rows:].astype(F32)
    lines = split_rows(jnp.sum(total, axis=0, keepdims=True), 3 * c)
    for x in outs:
        x[:, taps * own_rows :, :] = jnp.broadcast_to(lines[None], (groups, 8, width))


def join_kernel(at, a, b, joint, summed, sems):
    count = sems.shape[0]
    step = a.shape[0] // count
    copies = []
    for n in range(count):
        cut = slice(n * step, (n + 1) * step)
        summed[cut] = (a[cut].astype(F32) + b[cut].astype(F32)).astype(BF16)
        copies.append(
            pltpu.make_async_copy(
                summed.at[cut], joint.at[cut, at : at + summed.shape[1]], sems.at[n]
            )
        )
        copies[-1].start()
    for copy in copies:
        copy.wait()


def join_late_kernel(at, a, b, held, joint, summed, sem):
    del held
    join_kernel(at, a, b, joint, summed, sem)


def total_kernel(taps, count_all, blocks, second, first, loss):
    total = jnp.sum(blocks[...].astype(F32), axis=0)
    at = 0
    for out in (second, first):
        rows = taps * out.shape[1]
        out[...] = total[at : at + rows].reshape(out.shape)
        at += rows
    lines = total[at:]
    loss[0] = jnp.sum(lines[:, :128]) / count_all
    loss[1] = jnp.sum(lines[:, 128:]) / count_all


def call(
    kernel, operands, outs, scratch=(), smem=0, hbm=(), loose=(), after=(), smem_outs=(),
    hbm_outs=(), aliases={}, flops=0, cost=1, name=None,
):
    moved = sum(x.size * x.dtype.itemsize for x in operands)
    moved += sum(x.size * x.dtype.itemsize for x in outs)
    vmem, small = pl.BlockSpec(memory_space=pltpu.VMEM), pl.BlockSpec(memory_space=pltpu.SMEM)
    far, anywhere = pl.BlockSpec(memory_space=pltpu.HBM), pl.BlockSpec(memory_space=pl.ANY)
    count = len(operands)
    operands = tuple(
        pltpu.with_memory_space_constraint(x, pltpu.HBM) if at in hbm else x
        for at, x in enumerate(operands)
    )

    def body(*refs):
        kernel(*refs[:count], *refs[count + len(after) :])

    return pl.pallas_call(
        body,
        out_shape=[
            pltpu.HBM(x.shape, x.dtype) if at in hbm_outs else x for at, x in enumerate(outs)
        ],
        in_specs=[
            small if at < smem else far if at in hbm else anywhere if at in loose else vmem
            for at in range(count)
        ]
        + [anywhere] * len(after),
        out_specs=[
            small if at in smem_outs else far if at in hbm_outs else vmem
            for at in range(len(outs))
        ],
        scratch_shapes=list(scratch),
        input_output_aliases=aliases,
        compiler_params=pltpu.CompilerParams(vmem_limit_bytes=VMEM_LIMIT),
        cost_estimate=pl.CostEstimate(
            flops=int(flops * cost), bytes_accessed=int(moved * cost), transcendentals=0
        ),
        name=name,
    )(*operands, *after)


def like(shape, dtype=BF16):
    return jax.ShapeDtypeStruct(shape, dtype)


def turn(x, step):
    count = lax.axis_size("section")
    return lax.ppermute(x, "section", [(i, (i + step) % count) for i in range(count)])


def added(a, b, name, after=()):
    return call(add_kernel, (a, b), [like(a.shape)], after=after, name=name)[0]


def other_core(x):
    return lax.ppermute(x, "dp_2", [(0, 1), (1, 0)])


def shards(real_in, fake_in, kernel_first, kernel_second):
    replicas = lax.axis_size(DP)
    cols, span, in_width = real_in.shape
    frames = span // 3
    taps, width_all, width = kernel_second.shape
    normaliser = float(cols * frames)
    count_all = float(cols * replicas * frames * width_all)
    groups = replicas // 2
    part = cols // 2
    rows = cols * frames
    s = lax.axis_index("section").reshape(1).astype(jnp.int32)
    c = lax.axis_index("dp_2").reshape(1).astype(jnp.int32)
    dma = pltpu.SemaphoreType.DMA
    chunk_outs = [like((rows, width)), like((3, rows, in_width)), like((8, 128), F32)]
    conv_scratch = [pltpu.VMEM((cols, frames + 8, width), F32)]
    phases_far = [pltpu.VMEM((3, rows, in_width), BF16), dma]
    all_far = [pltpu.VMEM((rows, width_all), BF16), pltpu.VMEM((rows, taps * width), BF16)]
    flops = 2 * rows * taps * in_width * width

    h_a, phases_a, loss_a, w_first, rest = call(
        first_early_kernel,
        (real_in, fake_in, kernel_first),
        chunk_outs + [like(kernel_first.shape), like((cols, span, in_width))],
        conv_scratch
        + [pltpu.VMEM((cols, span, in_width), BF16), dma((cols,)), dma((2,)), dma((taps,))]
        + phases_far * (not NEAR_PHASES[0]),
        hbm=(0, 1, 2),
        hbm_outs=() if NEAR_PHASES[0] else (1,),
        flops=flops,
        name="first_a",
    )
    prev_a = turn(h_a, 1)
    following_a = turn(h_a, -1)
    h_b, phases_b, loss_b, w_second = call(
        first_late_kernel,
        (rest, w_first, kernel_second),
        chunk_outs + [like(kernel_second.shape)],
        conv_scratch + [dma((taps,))] + phases_far * (not NEAR_PHASES[1]),
        hbm=(2,),
        hbm_outs=() if NEAR_PHASES[1] else (1,),
        flops=flops,
        cost=1,
        name="first_b",
    )
    far_a = (turn(prev_a[: rows // 2], 1), turn(following_a[rows // 2 :], -1))
    following_b = turn(h_b, -1)
    prev_b = turn(h_b, 1)
    far_b = (turn(prev_b[: rows // 2], 1), turn(following_b[rows // 2 :], -1))

    second_outs = [like((rows, width_all)), like((rows, taps * width)), like((rows + 8, width)),
                   like((8, width))]
    back_outs = [like((rows + 8, width)), like((rows + 8, width)), like((rows, width))]
    second_scratch = [
        pltpu.VMEM((cols, frames + 16, width), F32), dma((5,)),
    ]
    copies = all_far + [dma, dma]
    flops = 2 * rows * taps * (width_all + width) * width
    all_a, shifted_a, far_t, loss_a, next_t, prev_t, own_a = call(
        functools.partial(second_kernel, normaliser, True, NEAR_ALL[0]),
        (s, h_a, prev_a, following_a, *far_a, w_second, loss_a),
        second_outs + back_outs,
        second_scratch + copies * (not NEAR_ALL[0]),
        smem=1,
        loose=(1, 2, 3, 4, 5),
        hbm_outs=() if NEAR_ALL[0] else (0, 1),
        cost=1,
        flops=flops,
        name="second_a",
    )
    pass_a = turn(far_t, 1)
    from_following_a = turn(prev_t, -1)
    relayed_a = added(next_t, pass_a, "relay_a")
    from_prev_a = turn(relayed_a, 1)

    all_b, shifted_b, far_t, loss_b = call(
        functools.partial(second_kernel, normaliser, False, NEAR_ALL[1]),
        (s, h_b, prev_b, following_b, *far_b, w_second, loss_b),
        second_outs,
        second_scratch + copies * (not NEAR_ALL[1]),
        smem=1,
        loose=(1, 2, 3, 4, 5),
        hbm_outs=() if NEAR_ALL[1] else (0, 1),
        cost=1,
        after=(own_a,),
        flops=flops,
        name="second_b",
    )
    pass_b = turn(far_t, -1)
    next_t, prev_t, own_b = call(
        back_kernel,
        (s, shifted_b, w_second, loss_b),
        back_outs,
        [] if NEAR_ALL[1] else [pltpu.VMEM((rows, taps * width), BF16), dma],
        smem=1,
        hbm=() if NEAR_ALL[1] else (1,),
        cost=4,
        flops=2 * rows * taps * width * width * 3,
        name="back_b",
    )
    from_prev_b = turn(next_t, 1)
    relayed_b = added(prev_t, pass_b, "relay_b")
    from_following_b = turn(relayed_b, -1)

    own_rows = width_all // replicas
    mine_second, theirs = call(
        functools.partial(weight_second_kernel, taps, NEAR_ALL),
        (c, all_a, all_b, shifted_a, shifted_b),
        [like((groups, taps * own_rows, width))] * 2,
        (all_far + [dma((width_all // 256,)), dma]) * (2 - sum(NEAR_ALL)),
        smem=1,
        hbm=tuple(at for at in (1, 2, 3, 4) if not NEAR_ALL[(at - 1) % 2]),
        cost=4,
        after=(relayed_a, relayed_b),
        flops=4 * rows * taps * width * width_all,
        name="weight_second",
    )
    first_rows = in_width // replicas
    size_second, size_first = taps * own_rows, taps * first_rows + 8
    joint_like = like((groups, size_second + size_first, width))
    (joint,) = call(
        functools.partial(join_kernel, 0),
        (mine_second, other_core(theirs)),
        [joint_like],
        [pltpu.VMEM((groups, size_second, width), BF16), dma((4,))],
        hbm_outs=(0,),
        name="join_second",
    )

    mine_first, theirs = call(
        functools.partial(weight_first_kernel, normaliser, taps, (NEAR_SMALL, *NEAR_PHASES)),
        (c, loss_a, loss_b, h_a, h_b, own_a, own_b, from_prev_a, from_prev_b, from_following_a,
         from_following_b, pass_a, pass_b, phases_a, phases_b),
        [like((groups, taps * first_rows + 8, width))] * 2,
        [pltpu.VMEM((2 * cols, frames + 8, width), F32), pltpu.VMEM((2 * rows, 2 * width), BF16)]
        + [pltpu.VMEM((10, rows + 8, width), BF16), dma((10,))] * (not NEAR_SMALL)
        + phases_far * (2 - sum(NEAR_PHASES)),
        smem=1,
        hbm=tuple(at for at in (13, 14) if not NEAR_PHASES[at - 13]),
        loose=() if NEAR_SMALL else tuple(range(3, 13)),
        cost=20,
        after=(mine_second,),
        flops=4 * rows * taps * width * in_width,
        name="weight_first",
    )
    (joint,) = call(
        functools.partial(join_late_kernel, size_second),
        (mine_first, other_core(theirs), joint),
        [joint_like],
        [pltpu.VMEM((groups, size_first, width), BF16), dma((4,))],
        hbm=(2,),
        hbm_outs=(0,),
        aliases={2: 0},
        name="join_first",
    )
    blocks = lax.all_to_all(joint, ZY, 0, 0)
    grad_second, grad_first, layer_loss = call(
        functools.partial(total_kernel, taps, count_all),
        (blocks,),
        [like((taps, own_rows, width), F32), like((taps, first_rows, width), F32),
         like((2,), F32)],
        smem_outs=(2,),
        name="total",
    )
    return (layer_loss, jnp.transpose(grad_first, (1, 0, 2)), jnp.transpose(grad_second, (1, 0, 2)))


def solution(mesh):
    finer = Mesh(
        mesh.devices.reshape(4, 4, 2, mesh.shape["section"]), ("dp_0", "dp_1", "dp_2", "section")
    )
    return jax.shard_map(
        shards,
        mesh=finer,
        in_specs=(
            P(DP, None, None),
            P(DP, None, None),
            P(None, None, "section"),
            P(None, None, "section"),
        ),
        out_specs=(P(), P(DP, None, "section"), P(DP, None, "section")),
        check_vma=False,
    )
```

```python
import functools

import jax
import jax.numpy as jnp
from jax import lax
from jax.experimental import pallas as pl
from jax.experimental.pallas import tpu as pltpu
from jax.sharding import Mesh
from jax.sharding import PartitionSpec as P

DP = ("dp_0", "dp_1", "dp_2")
ZY = ("dp_0", "dp_1")
F32 = jnp.float32
BF16 = jnp.bfloat16
VMEM_LIMIT = 16 << 20
NEAR_PHASES = (True, False)
NEAR_ALL = (True, True)
NEAR_SMALL = True

smooth_width = 0.1
leak_slope = 0.1


def leaky(pre):
    return jnp.where(pre > 0, pre, leak_slope * pre).astype(BF16)


def fold_rows(x):
    x = jnp.sum(x.reshape(-1, 8, x.shape[1]), axis=0)
    return sum(x[:, at : at + 128] for at in range(0, x.shape[1], 128))


def difference_terms(real, fake):
    difference = real.astype(F32) - fake.astype(F32)
    square = difference * difference + smooth_width * smooth_width
    inverse = lax.rsqrt(square)
    return difference * inverse, square * inverse


def dot(a, b):
    return jnp.dot(a, b, preferred_element_type=F32)


def dot_rows(a, b):
    return lax.dot_general(a, b, (((0,), (0,)), ((), ())), preferred_element_type=F32)


def dot_lanes(a, b):
    return lax.dot_general(a, b, (((1,), (1,)), ((), ())), preferred_element_type=F32)


def losses_split(first, second):
    value = jnp.sum(jnp.concatenate([first, second], axis=1), axis=0, keepdims=True)
    return split_rows(value, 0)


def split_rows(value, base):
    row = lax.broadcasted_iota(jnp.int32, (8, value.shape[1]), 0) - base
    high = value.astype(BF16).astype(F32)
    middle = (value - high).astype(BF16).astype(F32)
    low = value - high - middle
    out = jnp.where(row == 0, high, jnp.where(row == 1, middle, jnp.where(row == 2, low, 0.0)))
    return out.astype(BF16)


def strided_conv(take, cols, span, w, h_out, phases_out, loss, padded, *far):
    phases = far[0] if far else phases_out
    frames = span // 3
    rows = 2 * cols * frames
    width = w.shape[2]
    row = lax.broadcasted_iota(jnp.int32, (span, span), 0)
    col = lax.broadcasted_iota(jnp.int32, (span, span), 1)
    phase = jnp.where(row >= 2 * frames, 2, jnp.where(row >= frames, 1, 0))
    select = (col == 3 * (row - frames * phase) + phase).astype(F32).astype(BF16)
    for n in range(2 * cols):
        parts = dot(select, take(n)).astype(BF16)
        for p in range(3):
            phases[p, n * frames : (n + 1) * frames, :] = parts[p * frames : (p + 1) * frames]
    if far:
        copy_out = pltpu.make_async_copy(phases, phases_out, far[1])
        copy_out.start()
    padded[:, :8, :] = jnp.zeros((2 * cols, 8, width), F32)
    earlier = dot(phases[1], w[0]) + dot(phases[2], w[1])
    padded[:, 8 : 8 + frames, :] = earlier.reshape(2 * cols, frames, width)
    same = dot(phases[0], w[2]) + dot(phases[1], w[3]) + dot(phases[2], w[4])
    h = leaky(same + padded[:, 7 : 7 + frames, :].reshape(rows, width))
    h_out[...] = h
    _, root = difference_terms(h[: rows // 2], h[rows // 2 :])
    loss[...] = fold_rows(root - smooth_width)
    if far:
        copy_out.wait()


def copies_of(source, target, sems):
    return [
        pltpu.make_async_copy(source.at[n], target.at[n], sems.at[n])
        for n in range(source.shape[0])
    ]


def first_early_kernel(
    real, fake, w_hbm, h_out, phases_out, loss, w, rest,
    padded, held, held_sem, rest_sem, w_sem, *far_scratch,
):
    cols = held.shape[0] // 2
    span = held.shape[1]
    for n in range(2 * cols):
        source = real if n < cols else fake
        pltpu.make_async_copy(source.at[n % cols], held.at[n], held_sem.at[n]).start()
    w_copies = copies_of(w_hbm, w, w_sem)
    for copy in w_copies:
        copy.start()
    rest_copies = [
        pltpu.make_async_copy(x.at[cols:], rest.at[at * cols : (at + 1) * cols], rest_sem.at[at])
        for at, x in enumerate((real, fake))
    ]

    for copy in rest_copies:
        copy.start()

    def take(n):
        source = real if n < cols else fake
        pltpu.make_async_copy(source.at[n % cols], held.at[n], held_sem.at[n]).wait()
        if n == 2 * cols - 1:
            for copy in w_copies:
                copy.wait()
        return held[n]

    strided_conv(take, cols, span, w, h_out, phases_out, loss, padded, *far_scratch)
    for copy in rest_copies:
        copy.wait()


def first_late_kernel(rest, w, w_next_hbm, h_out, phases_out, loss, w_next, padded, sem, *far):
    copies = copies_of(w_next_hbm, w_next, sem)
    for copy in copies:
        copy.start()
    cols, span = rest.shape[0] // 2, rest.shape[1]
    strided_conv(lambda n: rest[n], cols, span, w, h_out, phases_out, loss, padded, *far)
    for copy in copies:
        copy.wait()


def second_kernel(
    normaliser, whole, near, s_ref, own, prev, following, far, w, loss_first,
    all_out, shifted_out, far_t, loss, *rest,
):
    if near:
        h_all, shifted = all_out, shifted_out
        *backs, padded, in_sems = rest
    else:
        *backs, padded, in_sems, h_all, shifted, all_sem, shifted_sem = rest
    rows, width = own.shape
    half = rows // 2
    taps = w.shape[0]
    frames = padded.shape[1] - 16
    s = s_ref[0]
    copies = []
    for away, x in enumerate((own, following, far, prev)):
        at = pl.multiple_of(lax.rem(s + away, 4) * width, 256)
        copies.append(
            pltpu.make_async_copy(x, h_all.at[:, pl.ds(at, width)], in_sems.at[away])
        )
        copies[-1].start()
    for copy in copies:
        copy.wait()
    if not near:
        copy_all = pltpu.make_async_copy(h_all, all_out, all_sem)
        copy_all.start()
    zeros = jnp.zeros((padded.shape[0], 8, width), F32)
    padded[:, :8, :] = zeros
    padded[:, 8 + frames :, :] = zeros
    pre = dot(h_all[...], w[2])
    for k in (0, 1, 3, 4):
        padded[:, 8 : 8 + frames, :] = dot(h_all[...], w[k]).reshape(-1, frames, width)
        pre = pre + padded[:, 6 + k : 6 + k + frames, :].reshape(rows, width)
    h = leaky(pre)
    slope, root = difference_terms(h[:half], h[half:])
    loss_rows = losses_split(loss_first[...], fold_rows(root - smooth_width))
    loss[...] = loss_rows
    slope = slope * (1.0 / normaliser)
    for value, sign, at in ((h[:half], 1.0, 0), (h[half:], -1.0, half // frames)):
        gate = jnp.where(value.astype(F32) > 0, 1.0, leak_slope)
        delta = (sign * slope * gate).astype(BF16).astype(F32)
        padded[at : at + half // frames, 8 : 8 + frames, :] = delta.reshape(-1, frames, width)
    for k in range(taps):
        moved = padded[:, 10 - k : 10 - k + frames, :].reshape(rows, width)
        shifted[:, k * width : (k + 1) * width] = moved.astype(BF16)
    if not near:
        copy_shifted = pltpu.make_async_copy(shifted, shifted_out, shifted_sem)
        copy_shifted.start()
    far_t[:rows] = back_term(s, 2, shifted, w)
    far_t[rows:] = loss_rows
    if whole:
        back_rest(s, shifted, w, loss_rows, 3, *backs)
    if not near:
        copy_all.wait()
        copy_shifted.wait()


def back_term(s, away, shifted, w):
    width = w.shape[2]
    at = pl.multiple_of(lax.rem(s + away, 4) * width, 256)
    term = None
    for k in range(w.shape[0]):
        part = dot_lanes(shifted[:, k * width : (k + 1) * width], w[k, pl.ds(at, width), :])
        term = part if term is None else term + part
    return term.astype(BF16)


def back_rest(s, shifted, w, loss_rows, with_loss, following, prev, own):
    rows = own.shape[0]
    for away, out in ((1, following), (3, prev)) if with_loss == 1 else ((3, prev), (1, following)):
        out[:rows] = back_term(s, away, shifted, w)
        out[rows:] = loss_rows if away == with_loss else jnp.zeros_like(loss_rows)
    own[...] = back_term(s, 0, shifted, w)


def back_kernel(s_ref, shifted, w, loss, following, prev, own, *rest):
    if rest:
        held, sem = rest
        copy = pltpu.make_async_copy(shifted, held, sem)
        copy.start()
        copy.wait()
        shifted = held
    back_rest(s_ref[0], shifted, w, loss[...], 1, following, prev, own)


def add_kernel(a, b, out):
    out[...] = (a[...].astype(F32) + b[...].astype(F32)).astype(BF16)


def put(g, c, outs, at, rows, k):
    count = g.shape[0] // (2 * rows)
    g = g.astype(BF16).reshape(count, 2, rows, g.shape[1])
    even, odd = g[:, 0], g[:, 1]
    mine, theirs = outs
    mine[at : at + count, k * rows : (k + 1) * rows] = jnp.where(c == 0, even, odd)
    theirs[at : at + count, k * rows : (k + 1) * rows] = jnp.where(c == 0, odd, even)


def weight_second_kernel(taps, nears, c_ref, h_a, h_b, shifted_a, shifted_b, mine, theirs, *rest):
    own_rows, width = mine.shape[1] // taps, mine.shape[2]
    c = c_ref[0]
    step = 256
    count = h_a.shape[1] // step
    rest = list(rest)
    pairs, first, later = [], [], [[] for _ in range(count)]
    for near, h, x in ((nears[0], h_a, shifted_a), (nears[1], h_b, shifted_b)):
        if not near:
            h_held, x_held, h_sem, x_sem = rest[:4]
            rest = rest[4:]
            first.append(pltpu.make_async_copy(x, x_held, x_sem))
            for q in range(count):
                cut = slice(q * step, (q + 1) * step)
                later[q].append(
                    pltpu.make_async_copy(h.at[:, cut], h_held.at[:, cut], h_sem.at[q])
                )
            h, x = h_held, x_held
        pairs.append((h, x))
    for copy in first + sum(later, []):
        copy.start()
    for copy in first:
        copy.wait()
    for q in range(count):
        for copy in later[q]:
            copy.wait()
        cut = slice(q * step, (q + 1) * step)
        g = sum(dot_rows(h[:, cut], x[...]) for h, x in pairs)
        for k in range(taps):
            put(g[:, k * width : (k + 1) * width], c, (mine, theirs),
                q * step // (2 * own_rows), own_rows, k)


def weight_first_kernel(
    normaliser, taps, nears, c_ref, loss_a, loss_b, *refs,
):
    *sources, phases_a, phases_b, mine, theirs, padded, moved = refs[:16]
    rest = list(refs[16:])
    rows, width = sources[0].shape
    half = rows // 2
    frames = padded.shape[1] - 8
    c = c_ref[0]
    small, large = [], []
    if not nears[0]:
        got, sems = rest[:2]
        rest = rest[2:]
        for n, x in enumerate(sources):
            small.append(pltpu.make_async_copy(x, got.at[n, : x.shape[0]], sems.at[n]))
        sources = [got.at[n, : x.shape[0]] for n, x in enumerate(sources)]
    phases = []
    for near, x in zip(nears[1:], (phases_a, phases_b)):
        if not near:
            held, sem = rest[:2]
            rest = rest[2:]
            large.append(pltpu.make_async_copy(x, held, sem))
            x = held
        phases.append(x)
    for copy in small + large:
        copy.start()
    for copy in small:
        copy.wait()
    padded[:, frames:, :] = jnp.zeros((padded.shape[0], 8, width), F32)
    for n in range(2):
        h, own, a, b = (sources[2 * at + n] for at in range(4))
        slope, _ = difference_terms(h[:half], h[half:rows])
        slope = slope * (1.0 / normaliser)
        for at, sign in ((0, 1.0), (half, -1.0)):
            cut = slice(at, at + half)
            up = own[cut].astype(F32) + a[cut].astype(F32) + b[cut].astype(F32)
            up = up.astype(BF16).astype(F32)
            gate = jnp.where(h[cut].astype(F32) > 0, 1.0, leak_slope)
            delta = ((sign * slope + up) * gate).astype(BF16)
            base = n * rows + at
            moved[base : base + half, :width] = delta
            cols, lead = half // frames, base // frames
            padded[lead : lead + cols, :frames, :] = delta.astype(F32).reshape(cols, frames, width)
    moved[:, width:] = padded[:, 1 : 1 + frames, :].reshape(2 * rows, width).astype(BF16)
    groups = mine.shape[0]
    own_rows = (mine.shape[1] - 8) // taps
    outs = (mine, theirs)
    for copy in large:
        copy.wait()
    for p in range(3):
        lanes = width if p == 0 else 2 * width
        g = dot_rows(phases[0][p], moved[:rows, :lanes])
        g = g + dot_rows(phases[1][p], moved[rows:, :lanes])
        put(g[:, :width], c, outs, 0, own_rows, 2 + p)
        if p > 0:
            put(g[:, width:], c, outs, 0, own_rows, p - 1)
    total = loss_a[...].astype(F32) + loss_b[...].astype(F32)
    for x in sources[4:]:
        total = total + x[rows:].astype(F32)
    lines = split_rows(jnp.sum(total, axis=0, keepdims=True), 3 * c)
    for x in outs:
        x[:, taps * own_rows :, :] = jnp.broadcast_to(lines[None], (groups, 8, width))


def same_kernel(a, out):
    out[...] = a[...]


def join_kernel(at, a, b, joint, summed, sems):
    count = sems.shape[0]
    step = a.shape[0] // count
    copies = []
    for n in range(count):
        cut = slice(n * step, (n + 1) * step)
        summed[cut] = (a[cut].astype(F32) + b[cut].astype(F32)).astype(BF16)
        copies.append(
            pltpu.make_async_copy(
                summed.at[cut], joint.at[cut, at : at + summed.shape[1]], sems.at[n]
            )
        )
        copies[-1].start()
    for copy in copies:
        copy.wait()


def join_late_kernel(at, a, b, held, joint, summed, sem):
    del held
    join_kernel(at, a, b, joint, summed, sem)


def total_kernel(taps, count_all, blocks, second, first, loss):
    total = jnp.sum(blocks[...].astype(F32), axis=0)
    at = 0
    for out in (second, first):
        rows = taps * out.shape[1]
        out[...] = total[at : at + rows].reshape(out.shape)
        at += rows
    lines = total[at:]
    loss[0] = jnp.sum(lines[:, :128]) / count_all
    loss[1] = jnp.sum(lines[:, 128:]) / count_all


def call(
    kernel, operands, outs, scratch=(), smem=0, hbm=(), loose=(), after=(), smem_outs=(),
    hbm_outs=(), aliases={}, flops=0, cost=1, name=None,
):
    moved = sum(x.size * x.dtype.itemsize for x in operands)
    moved += sum(x.size * x.dtype.itemsize for x in outs)
    vmem, small = pl.BlockSpec(memory_space=pltpu.VMEM), pl.BlockSpec(memory_space=pltpu.SMEM)
    far, anywhere = pl.BlockSpec(memory_space=pltpu.HBM), pl.BlockSpec(memory_space=pl.ANY)
    count = len(operands)
    operands = tuple(
        pltpu.with_memory_space_constraint(x, pltpu.HBM) if at in hbm else x
        for at, x in enumerate(operands)
    )

    def body(*refs):
        kernel(*refs[:count], *refs[count + len(after) :])

    return pl.pallas_call(
        body,
        out_shape=[
            pltpu.HBM(x.shape, x.dtype) if at in hbm_outs else x for at, x in enumerate(outs)
        ],
        in_specs=[
            small if at < smem else far if at in hbm else anywhere if at in loose else vmem
            for at in range(count)
        ]
        + [anywhere] * len(after),
        out_specs=[
            small if at in smem_outs else far if at in hbm_outs else vmem
            for at in range(len(outs))
        ],
        scratch_shapes=list(scratch),
        input_output_aliases=aliases,
        compiler_params=pltpu.CompilerParams(vmem_limit_bytes=VMEM_LIMIT),
        cost_estimate=pl.CostEstimate(
            flops=int(flops * cost), bytes_accessed=int(moved * cost), transcendentals=0
        ),
        name=name,
    )(*operands, *after)


def like(shape, dtype=BF16):
    return jax.ShapeDtypeStruct(shape, dtype)


def turn(x, step):
    count = lax.axis_size("section")
    return lax.ppermute(x, "section", [(i, (i + step) % count) for i in range(count)])


def later(x, after, name):
    return call(same_kernel, (x,), [like(x.shape)], after=after, name=name)[0]


def added(a, b, name, after=()):
    return call(add_kernel, (a, b), [like(a.shape)], after=after, name=name)[0]


def other_core(x):
    return lax.ppermute(x, "dp_2", [(0, 1), (1, 0)])


def shards(real_in, fake_in, kernel_first, kernel_second):
    replicas = lax.axis_size(DP)
    cols, span, in_width = real_in.shape
    frames = span // 3
    taps, width_all, width = kernel_second.shape
    normaliser = float(cols * frames)
    count_all = float(cols * replicas * frames * width_all)
    groups = replicas // 2
    part = cols // 2
    rows = cols * frames
    s = lax.axis_index("section").reshape(1).astype(jnp.int32)
    c = lax.axis_index("dp_2").reshape(1).astype(jnp.int32)
    dma = pltpu.SemaphoreType.DMA
    chunk_outs = [like((rows, width)), like((3, rows, in_width)), like((8, 128), F32)]
    conv_scratch = [pltpu.VMEM((cols, frames + 8, width), F32)]
    phases_far = [pltpu.VMEM((3, rows, in_width), BF16), dma]
    all_far = [pltpu.VMEM((rows, width_all), BF16), pltpu.VMEM((rows, taps * width), BF16)]
    flops = 2 * rows * taps * in_width * width

    h_a, phases_a, loss_a, w_first, rest = call(
        first_early_kernel,
        (real_in, fake_in, kernel_first),
        chunk_outs + [like(kernel_first.shape), like((cols, span, in_width))],
        conv_scratch
        + [pltpu.VMEM((cols, span, in_width), BF16), dma((cols,)), dma((2,)), dma((taps,))]
        + phases_far * (not NEAR_PHASES[0]),
        hbm=(0, 1, 2),
        hbm_outs=() if NEAR_PHASES[0] else (1,),
        flops=flops,
        name="first_a",
    )
    prev_a = turn(h_a, 1)
    following_a = turn(h_a, -1)
    h_b, phases_b, loss_b, w_second = call(
        first_late_kernel,
        (rest, w_first, kernel_second),
        chunk_outs + [like(kernel_second.shape)],
        conv_scratch + [dma((taps,))] + phases_far * (not NEAR_PHASES[1]),
        hbm=(2,),
        hbm_outs=() if NEAR_PHASES[1] else (1,),
        flops=flops,
        cost=1,
        name="first_b",
    )
    far_a = turn(prev_a, 1)
    following_b = turn(h_b, -1)
    prev_b = turn(later(h_b, (following_a,), "ordered"), 1)
    far_b = turn(following_b, -1)

    second_outs = [like((rows, width_all)), like((rows, taps * width)), like((rows + 8, width)),
                   like((8, width))]
    back_outs = [like((rows + 8, width)), like((rows + 8, width)), like((rows, width))]
    second_scratch = [
        pltpu.VMEM((cols, frames + 16, width), F32), dma((4,)),
    ]
    copies = all_far + [dma, dma]
    flops = 2 * rows * taps * (width_all + width) * width
    all_a, shifted_a, far_t, loss_a, next_t, prev_t, own_a = call(
        functools.partial(second_kernel, normaliser, True, NEAR_ALL[0]),
        (s, h_a, prev_a, following_a, far_a, w_second, loss_a),
        second_outs + back_outs,
        second_scratch + copies * (not NEAR_ALL[0]),
        smem=1,
        loose=(1, 2, 3, 4),
        hbm_outs=() if NEAR_ALL[0] else (0, 1),
        cost=1,
        flops=flops,
        name="second_a",
    )
    pass_a = turn(far_t, 1)
    from_following_a = turn(prev_t, -1)
    relayed_a = added(next_t, pass_a, "relay_a")
    from_prev_a = turn(relayed_a, 1)

    all_b, shifted_b, far_t, loss_b = call(
        functools.partial(second_kernel, normaliser, False, NEAR_ALL[1]),
        (s, h_b, prev_b, following_b, far_b, w_second, loss_b),
        second_outs,
        second_scratch + copies * (not NEAR_ALL[1]),
        smem=1,
        loose=(1, 2, 3, 4),
        hbm_outs=() if NEAR_ALL[1] else (0, 1),
        cost=1,
        after=(own_a,),
        flops=flops,
        name="second_b",
    )
    pass_b = turn(far_t, -1)
    next_t, prev_t, own_b = call(
        back_kernel,
        (s, shifted_b, w_second, loss_b),
        back_outs,
        [] if NEAR_ALL[1] else [pltpu.VMEM((rows, taps * width), BF16), dma],
        smem=1,
        hbm=() if NEAR_ALL[1] else (1,),
        cost=4,
        flops=2 * rows * taps * width * width * 3,
        name="back_b",
    )
    from_prev_b = turn(next_t, 1)
    relayed_b = added(prev_t, pass_b, "relay_b")
    from_following_b = turn(relayed_b, -1)

    own_rows = width_all // replicas
    mine_second, theirs = call(
        functools.partial(weight_second_kernel, taps, NEAR_ALL),
        (c, all_a, all_b, shifted_a, shifted_b),
        [like((groups, taps * own_rows, width))] * 2,
        (all_far + [dma((width_all // 256,)), dma]) * (2 - sum(NEAR_ALL)),
        smem=1,
        hbm=tuple(at for at in (1, 2, 3, 4) if not NEAR_ALL[(at - 1) % 2]),
        cost=4,
        after=(relayed_a, relayed_b),
        flops=4 * rows * taps * width * width_all,
        name="weight_second",
    )
    first_rows = in_width // replicas
    size_second, size_first = taps * own_rows, taps * first_rows + 8
    joint_like = like((groups, size_second + size_first, width))
    (joint,) = call(
        functools.partial(join_kernel, 0),
        (mine_second, other_core(theirs)),
        [joint_like],
        [pltpu.VMEM((groups, size_second, width), BF16), dma((4,))],
        hbm_outs=(0,),
        name="join_second",
    )

    mine_first, theirs = call(
        functools.partial(weight_first_kernel, normaliser, taps, (NEAR_SMALL, *NEAR_PHASES)),
        (c, loss_a, loss_b, h_a, h_b, own_a, own_b, from_prev_a, from_prev_b, from_following_a,
         from_following_b, pass_a, pass_b, phases_a, phases_b),
        [like((groups, taps * first_rows + 8, width))] * 2,
        [pltpu.VMEM((2 * cols, frames + 8, width), F32), pltpu.VMEM((2 * rows, 2 * width), BF16)]
        + [pltpu.VMEM((10, rows + 8, width), BF16), dma((10,))] * (not NEAR_SMALL)
        + phases_far * (2 - sum(NEAR_PHASES)),
        smem=1,
        hbm=tuple(at for at in (13, 14) if not NEAR_PHASES[at - 13]),
        loose=() if NEAR_SMALL else tuple(range(3, 13)),
        cost=20,
        after=(mine_second,),
        flops=4 * rows * taps * width * in_width,
        name="weight_first",
    )
    (joint,) = call(
        functools.partial(join_late_kernel, size_second),
        (mine_first, other_core(theirs), joint),
        [joint_like],
        [pltpu.VMEM((groups, size_first, width), BF16), dma((4,))],
        hbm=(2,),
        hbm_outs=(0,),
        aliases={2: 0},
        name="join_first",
    )
    blocks = lax.all_to_all(joint, ZY, 0, 0)
    grad_second, grad_first, layer_loss = call(
        functools.partial(total_kernel, taps, count_all),
        (blocks,),
        [like((taps, own_rows, width), F32), like((taps, first_rows, width), F32),
         like((2,), F32)],
        smem_outs=(2,),
        name="total",
    )
    return (layer_loss, jnp.transpose(grad_first, (1, 0, 2)), jnp.transpose(grad_second, (1, 0, 2)))


def solution(mesh):
    finer = Mesh(
        mesh.devices.reshape(4, 4, 2, mesh.shape["section"]), ("dp_0", "dp_1", "dp_2", "section")
    )
    return jax.shard_map(
        shards,
        mesh=finer,
        in_specs=(
            P(DP, None, None),
            P(DP, None, None),
            P(None, None, "section"),
            P(None, None, "section"),
        ),
        out_specs=(P(), P(DP, None, "section"), P(DP, None, "section")),
        check_vma=False,
    )
```

```python
import functools

import jax
import jax.numpy as jnp
from jax import lax
from jax.experimental import pallas as pl
from jax.experimental.pallas import tpu as pltpu
from jax.sharding import Mesh
from jax.sharding import PartitionSpec as P

DP = ("dp_0", "dp_1", "dp_2")
ZY = ("dp_0", "dp_1")
F32 = jnp.float32
BF16 = jnp.bfloat16
VMEM_LIMIT = 16 << 20
NEAR_PHASES = (True, False)
NEAR_ALL = (True, True)
NEAR_SMALL = True

smooth_width = 0.1
leak_slope = 0.1


def leaky(pre):
    return jnp.where(pre > 0, pre, leak_slope * pre).astype(BF16)


def fold_rows(x):
    x = jnp.sum(x.reshape(-1, 8, x.shape[1]), axis=0)
    return sum(x[:, at : at + 128] for at in range(0, x.shape[1], 128))


def difference_terms(real, fake):
    difference = real.astype(F32) - fake.astype(F32)
    square = difference * difference + smooth_width * smooth_width
    inverse = lax.rsqrt(square)
    return difference * inverse, square * inverse


def dot(a, b):
    return jnp.dot(a, b, preferred_element_type=F32)


def dot_rows(a, b):
    return lax.dot_general(a, b, (((0,), (0,)), ((), ())), preferred_element_type=F32)


def dot_lanes(a, b):
    return lax.dot_general(a, b, (((1,), (1,)), ((), ())), preferred_element_type=F32)


def losses_split(first, second):
    value = jnp.sum(jnp.concatenate([first, second], axis=1), axis=0, keepdims=True)
    return split_rows(value, 0)


def split_rows(value, base):
    row = lax.broadcasted_iota(jnp.int32, (8, value.shape[1]), 0) - base
    high = value.astype(BF16).astype(F32)
    middle = (value - high).astype(BF16).astype(F32)
    low = value - high - middle
    out = jnp.where(row == 0, high, jnp.where(row == 1, middle, jnp.where(row == 2, low, 0.0)))
    return out.astype(BF16)


def strided_conv(take, cols, span, w, h_out, phases_out, loss, padded, *far):
    phases = far[0] if far else phases_out
    frames = span // 3
    rows = 2 * cols * frames
    width = w.shape[2]
    row = lax.broadcasted_iota(jnp.int32, (span, span), 0)
    col = lax.broadcasted_iota(jnp.int32, (span, span), 1)
    phase = jnp.where(row >= 2 * frames, 2, jnp.where(row >= frames, 1, 0))
    select = (col == 3 * (row - frames * phase) + phase).astype(F32).astype(BF16)
    for n in range(2 * cols):
        parts = dot(select, take(n)).astype(BF16)
        for p in range(3):
            phases[p, n * frames : (n + 1) * frames, :] = parts[p * frames : (p + 1) * frames]
    if far:
        copy_out = pltpu.make_async_copy(phases, phases_out, far[1])
        copy_out.start()
    padded[:, :8, :] = jnp.zeros((2 * cols, 8, width), F32)
    earlier = dot(phases[1], w[0]) + dot(phases[2], w[1])
    padded[:, 8 : 8 + frames, :] = earlier.reshape(2 * cols, frames, width)
    same = dot(phases[0], w[2]) + dot(phases[1], w[3]) + dot(phases[2], w[4])
    h = leaky(same + padded[:, 7 : 7 + frames, :].reshape(rows, width))
    h_out[...] = h
    _, root = difference_terms(h[: rows // 2], h[rows // 2 :])
    loss[...] = fold_rows(root - smooth_width)
    if far:
        copy_out.wait()


def copies_of(source, target, sems):
    return [
        pltpu.make_async_copy(source.at[n], target.at[n], sems.at[n])
        for n in range(source.shape[0])
    ]


def first_early_kernel(
    real, fake, w_hbm, h_out, phases_out, loss, w, rest,
    padded, held, held_sem, rest_sem, w_sem, *far_scratch,
):
    cols = held.shape[0] // 2
    span = held.shape[1]
    for n in range(2 * cols):
        source = real if n < cols else fake
        pltpu.make_async_copy(source.at[n % cols], held.at[n], held_sem.at[n]).start()
    w_copies = copies_of(w_hbm, w, w_sem)
    for copy in w_copies:
        copy.start()
    rest_copies = [
        pltpu.make_async_copy(x.at[cols:], rest.at[at * cols : (at + 1) * cols], rest_sem.at[at])
        for at, x in enumerate((real, fake))
    ]

    for copy in rest_copies:
        copy.start()

    def take(n):
        source = real if n < cols else fake
        pltpu.make_async_copy(source.at[n % cols], held.at[n], held_sem.at[n]).wait()
        if n == 2 * cols - 1:
            for copy in w_copies:
                copy.wait()
        return held[n]

    strided_conv(take, cols, span, w, h_out, phases_out, loss, padded, *far_scratch)
    for copy in rest_copies:
        copy.wait()


def first_late_kernel(rest, w, w_next_hbm, h_out, phases_out, loss, w_next, padded, sem, *far):
    copies = copies_of(w_next_hbm, w_next, sem)
    for copy in copies:
        copy.start()
    cols, span = rest.shape[0] // 2, rest.shape[1]
    strided_conv(lambda n: rest[n], cols, span, w, h_out, phases_out, loss, padded, *far)
    for copy in copies:
        copy.wait()


def second_kernel(
    normaliser, whole, near, s_ref, own, prev, following, far, w, loss_first,
    all_out, shifted_out, far_t, loss, *rest,
):
    if near:
        h_all, shifted = all_out, shifted_out
        *backs, padded = rest
    else:
        *backs, padded, h_all, shifted, all_sem, shifted_sem = rest
    rows, width = own.shape
    half = rows // 2
    taps = w.shape[0]
    frames = padded.shape[1] - 16
    s = s_ref[0]
    for away, x in enumerate((own, following, far, prev)):
        at = pl.multiple_of(lax.rem(s + away, 4) * width, 256)
        h_all[:, pl.ds(at, width)] = x[...]
    if not near:
        copy_all = pltpu.make_async_copy(h_all, all_out, all_sem)
        copy_all.start()
    zeros = jnp.zeros((padded.shape[0], 8, width), F32)
    padded[:, :8, :] = zeros
    padded[:, 8 + frames :, :] = zeros
    pre = dot(h_all[...], w[2])
    for k in (0, 1, 3, 4):
        padded[:, 8 : 8 + frames, :] = dot(h_all[...], w[k]).reshape(-1, frames, width)
        pre = pre + padded[:, 6 + k : 6 + k + frames, :].reshape(rows, width)
    h = leaky(pre)
    slope, root = difference_terms(h[:half], h[half:])
    loss_rows = losses_split(loss_first[...], fold_rows(root - smooth_width))
    loss[...] = loss_rows
    slope = slope * (1.0 / normaliser)
    for value, sign, at in ((h[:half], 1.0, 0), (h[half:], -1.0, half // frames)):
        gate = jnp.where(value.astype(F32) > 0, 1.0, leak_slope)
        delta = (sign * slope * gate).astype(BF16).astype(F32)
        padded[at : at + half // frames, 8 : 8 + frames, :] = delta.reshape(-1, frames, width)
    for k in range(taps):
        moved = padded[:, 10 - k : 10 - k + frames, :].reshape(rows, width)
        shifted[:, k * width : (k + 1) * width] = moved.astype(BF16)
    if not near:
        copy_shifted = pltpu.make_async_copy(shifted, shifted_out, shifted_sem)
        copy_shifted.start()
    far_t[:rows] = back_term(s, 2, shifted, w)
    far_t[rows:] = loss_rows
    if whole:
        back_rest(s, shifted, w, loss_rows, 3, *backs)
    if not near:
        copy_all.wait()
        copy_shifted.wait()


def back_term(s, away, shifted, w):
    width = w.shape[2]
    at = pl.multiple_of(lax.rem(s + away, 4) * width, 256)
    term = None
    for k in range(w.shape[0]):
        part = dot_lanes(shifted[:, k * width : (k + 1) * width], w[k, pl.ds(at, width), :])
        term = part if term is None else term + part
    return term.astype(BF16)


def back_rest(s, shifted, w, loss_rows, with_loss, following, prev, own):
    rows = own.shape[0]
    for away, out in ((1, following), (3, prev)) if with_loss == 1 else ((3, prev), (1, following)):
        out[:rows] = back_term(s, away, shifted, w)
        out[rows:] = loss_rows if away == with_loss else jnp.zeros_like(loss_rows)
    own[...] = back_term(s, 0, shifted, w)


def back_kernel(s_ref, shifted, w, loss, following, prev, own, *rest):
    if rest:
        held, sem = rest
        copy = pltpu.make_async_copy(shifted, held, sem)
        copy.start()
        copy.wait()
        shifted = held
    back_rest(s_ref[0], shifted, w, loss[...], 1, following, prev, own)


def add_kernel(a, b, out):
    out[...] = (a[...].astype(F32) + b[...].astype(F32)).astype(BF16)


def put(g, c, outs, at, rows, k):
    count = g.shape[0] // (2 * rows)
    g = g.astype(BF16).reshape(count, 2, rows, g.shape[1])
    even, odd = g[:, 0], g[:, 1]
    mine, theirs = outs
    mine[at : at + count, k * rows : (k + 1) * rows] = jnp.where(c == 0, even, odd)
    theirs[at : at + count, k * rows : (k + 1) * rows] = jnp.where(c == 0, odd, even)


def weight_second_kernel(taps, nears, c_ref, h_a, h_b, shifted_a, shifted_b, mine, theirs, *rest):
    own_rows, width = mine.shape[1] // taps, mine.shape[2]
    c = c_ref[0]
    step = 256
    count = h_a.shape[1] // step
    rest = list(rest)
    pairs, first, later = [], [], [[] for _ in range(count)]
    for near, h, x in ((nears[0], h_a, shifted_a), (nears[1], h_b, shifted_b)):
        if not near:
            h_held, x_held, h_sem, x_sem = rest[:4]
            rest = rest[4:]
            first.append(pltpu.make_async_copy(x, x_held, x_sem))
            for q in range(count):
                cut = slice(q * step, (q + 1) * step)
                later[q].append(
                    pltpu.make_async_copy(h.at[:, cut], h_held.at[:, cut], h_sem.at[q])
                )
            h, x = h_held, x_held
        pairs.append((h, x))
    for copy in first + sum(later, []):
        copy.start()
    for copy in first:
        copy.wait()
    for q in range(count):
        for copy in later[q]:
            copy.wait()
        cut = slice(q * step, (q + 1) * step)
        g = sum(dot_rows(h[:, cut], x[...]) for h, x in pairs)
        for k in range(taps):
            put(g[:, k * width : (k + 1) * width], c, (mine, theirs),
                q * step // (2 * own_rows), own_rows, k)


def weight_first_kernel(
    normaliser, taps, nears, c_ref, loss_a, loss_b, *refs,
):
    *sources, phases_a, phases_b, mine, theirs, padded, moved = refs[:16]
    rest = list(refs[16:])
    rows, width = sources[0].shape
    half = rows // 2
    frames = padded.shape[1] - 8
    c = c_ref[0]
    small, large = [], []
    if not nears[0]:
        got, sems = rest[:2]
        rest = rest[2:]
        for n, x in enumerate(sources):
            small.append(pltpu.make_async_copy(x, got.at[n, : x.shape[0]], sems.at[n]))
        sources = [got.at[n, : x.shape[0]] for n, x in enumerate(sources)]
    phases = []
    for near, x in zip(nears[1:], (phases_a, phases_b)):
        if not near:
            held, sem = rest[:2]
            rest = rest[2:]
            large.append(pltpu.make_async_copy(x, held, sem))
            x = held
        phases.append(x)
    for copy in small + large:
        copy.start()
    for copy in small:
        copy.wait()
    padded[:, frames:, :] = jnp.zeros((padded.shape[0], 8, width), F32)
    for n in range(2):
        h, own, a, b = (sources[2 * at + n] for at in range(4))
        slope, _ = difference_terms(h[:half], h[half:rows])
        slope = slope * (1.0 / normaliser)
        for at, sign in ((0, 1.0), (half, -1.0)):
            cut = slice(at, at + half)
            up = own[cut].astype(F32) + a[cut].astype(F32) + b[cut].astype(F32)
            up = up.astype(BF16).astype(F32)
            gate = jnp.where(h[cut].astype(F32) > 0, 1.0, leak_slope)
            delta = ((sign * slope + up) * gate).astype(BF16)
            base = n * rows + at
            moved[base : base + half, :width] = delta
            cols, lead = half // frames, base // frames
            padded[lead : lead + cols, :frames, :] = delta.astype(F32).reshape(cols, frames, width)
    moved[:, width:] = padded[:, 1 : 1 + frames, :].reshape(2 * rows, width).astype(BF16)
    groups = mine.shape[0]
    own_rows = (mine.shape[1] - 8) // taps
    outs = (mine, theirs)
    for copy in large:
        copy.wait()
    for p in range(3):
        lanes = width if p == 0 else 2 * width
        g = dot_rows(phases[0][p], moved[:rows, :lanes])
        g = g + dot_rows(phases[1][p], moved[rows:, :lanes])
        put(g[:, :width], c, outs, 0, own_rows, 2 + p)
        if p > 0:
            put(g[:, width:], c, outs, 0, own_rows, p - 1)
    total = loss_a[...].astype(F32) + loss_b[...].astype(F32)
    for x in sources[4:]:
        total = total + x[rows:].astype(F32)
    lines = split_rows(jnp.sum(total, axis=0, keepdims=True), 3 * c)
    for x in outs:
        x[:, taps * own_rows :, :] = jnp.broadcast_to(lines[None], (groups, 8, width))


def same_kernel(a, out):
    out[...] = a[...]


def join_kernel(at, a, b, joint, summed, sems):
    count = sems.shape[0]
    step = a.shape[0] // count
    copies = []
    for n in range(count):
        cut = slice(n * step, (n + 1) * step)
        summed[cut] = (a[cut].astype(F32) + b[cut].astype(F32)).astype(BF16)
        copies.append(
            pltpu.make_async_copy(
                summed.at[cut], joint.at[cut, at : at + summed.shape[1]], sems.at[n]
            )
        )
        copies[-1].start()
    for copy in copies:
        copy.wait()


def join_late_kernel(at, a, b, held, joint, summed, sem):
    del held
    join_kernel(at, a, b, joint, summed, sem)


def total_kernel(taps, count_all, blocks, second, first, loss):
    total = jnp.sum(blocks[...].astype(F32), axis=0)
    at = 0
    for out in (second, first):
        rows = taps * out.shape[1]
        out[...] = total[at : at + rows].reshape(out.shape)
        at += rows
    lines = total[at:]
    loss[0] = jnp.sum(lines[:, :128]) / count_all
    loss[1] = jnp.sum(lines[:, 128:]) / count_all


def call(
    kernel, operands, outs, scratch=(), smem=0, hbm=(), loose=(), after=(), smem_outs=(),
    hbm_outs=(), aliases={}, flops=0, cost=1, name=None,
):
    moved = sum(x.size * x.dtype.itemsize for x in operands)
    moved += sum(x.size * x.dtype.itemsize for x in outs)
    vmem, small = pl.BlockSpec(memory_space=pltpu.VMEM), pl.BlockSpec(memory_space=pltpu.SMEM)
    far, anywhere = pl.BlockSpec(memory_space=pltpu.HBM), pl.BlockSpec(memory_space=pl.ANY)
    count = len(operands)
    operands = tuple(
        pltpu.with_memory_space_constraint(x, pltpu.HBM) if at in hbm else x
        for at, x in enumerate(operands)
    )

    def body(*refs):
        kernel(*refs[:count], *refs[count + len(after) :])

    return pl.pallas_call(
        body,
        out_shape=[
            pltpu.HBM(x.shape, x.dtype) if at in hbm_outs else x for at, x in enumerate(outs)
        ],
        in_specs=[
            small if at < smem else far if at in hbm else anywhere if at in loose else vmem
            for at in range(count)
        ]
        + [anywhere] * len(after),
        out_specs=[
            small if at in smem_outs else far if at in hbm_outs else vmem
            for at in range(len(outs))
        ],
        scratch_shapes=list(scratch),
        input_output_aliases=aliases,
        compiler_params=pltpu.CompilerParams(vmem_limit_bytes=VMEM_LIMIT),
        cost_estimate=pl.CostEstimate(
            flops=int(flops * cost), bytes_accessed=int(moved * cost), transcendentals=0
        ),
        name=name,
    )(*operands, *after)


def like(shape, dtype=BF16):
    return jax.ShapeDtypeStruct(shape, dtype)


def turn(x, step):
    count = lax.axis_size("section")
    return lax.ppermute(x, "section", [(i, (i + step) % count) for i in range(count)])


def later(x, after, name):
    return call(same_kernel, (x,), [like(x.shape)], after=after, name=name)[0]


def added(a, b, name, after=()):
    return call(add_kernel, (a, b), [like(a.shape)], after=after, name=name)[0]


def other_core(x):
    return lax.ppermute(x, "dp_2", [(0, 1), (1, 0)])


def shards(real_in, fake_in, kernel_first, kernel_second):
    replicas = lax.axis_size(DP)
    cols, span, in_width = real_in.shape
    frames = span // 3
    taps, width_all, width = kernel_second.shape
    normaliser = float(cols * frames)
    count_all = float(cols * replicas * frames * width_all)
    groups = replicas // 2
    part = cols // 2
    rows = cols * frames
    s = lax.axis_index("section").reshape(1).astype(jnp.int32)
    c = lax.axis_index("dp_2").reshape(1).astype(jnp.int32)
    dma = pltpu.SemaphoreType.DMA
    chunk_outs = [like((rows, width)), like((3, rows, in_width)), like((8, 128), F32)]
    conv_scratch = [pltpu.VMEM((cols, frames + 8, width), F32)]
    phases_far = [pltpu.VMEM((3, rows, in_width), BF16), dma]
    all_far = [pltpu.VMEM((rows, width_all), BF16), pltpu.VMEM((rows, taps * width), BF16)]
    flops = 2 * rows * taps * in_width * width

    h_a, phases_a, loss_a, w_first, rest = call(
        first_early_kernel,
        (real_in, fake_in, kernel_first),
        chunk_outs + [like(kernel_first.shape), like((cols, span, in_width))],
        conv_scratch
        + [pltpu.VMEM((cols, span, in_width), BF16), dma((cols,)), dma((2,)), dma((taps,))]
        + phases_far * (not NEAR_PHASES[0]),
        hbm=(0, 1, 2),
        hbm_outs=() if NEAR_PHASES[0] else (1,),
        flops=flops,
        name="first_a",
    )
    prev_a = turn(h_a, 1)
    following_a = turn(h_a, -1)
    h_b, phases_b, loss_b, w_second = call(
        first_late_kernel,
        (rest, w_first, kernel_second),
        chunk_outs + [like(kernel_second.shape)],
        conv_scratch + [dma((taps,))] + phases_far * (not NEAR_PHASES[1]),
        hbm=(2,),
        hbm_outs=() if NEAR_PHASES[1] else (1,),
        flops=flops,
        cost=1,
        name="first_b",
    )
    far_a = turn(prev_a, 1)
    following_b = turn(h_b, -1)
    prev_b = turn(later(h_b, (following_a,), "ordered"), 1)
    far_b = turn(following_b, -1)

    second_outs = [like((rows, width_all)), like((rows, taps * width)), like((rows + 8, width)),
                   like((8, width))]
    back_outs = [like((rows + 8, width)), like((rows + 8, width)), like((rows, width))]
    second_scratch = [
        pltpu.VMEM((cols, frames + 16, width), F32),
    ]
    copies = all_far + [dma, dma]
    flops = 2 * rows * taps * (width_all + width) * width
    all_a, shifted_a, far_t, loss_a, next_t, prev_t, own_a = call(
        functools.partial(second_kernel, normaliser, True, NEAR_ALL[0]),
        (s, h_a, prev_a, following_a, far_a, w_second, loss_a),
        second_outs + back_outs,
        second_scratch + copies * (not NEAR_ALL[0]),
        smem=1,
        hbm_outs=() if NEAR_ALL[0] else (0, 1),
        cost=1,
        flops=flops,
        name="second_a",
    )
    pass_a = turn(far_t, 1)
    from_following_a = turn(prev_t, -1)
    relayed_a = added(next_t, pass_a, "relay_a")
    from_prev_a = turn(relayed_a, 1)

    all_b, shifted_b, far_t, loss_b = call(
        functools.partial(second_kernel, normaliser, False, NEAR_ALL[1]),
        (s, h_b, prev_b, following_b, far_b, w_second, loss_b),
        second_outs,
        second_scratch + copies * (not NEAR_ALL[1]),
        smem=1,
        hbm_outs=() if NEAR_ALL[1] else (0, 1),
        cost=1,
        after=(own_a,),
        flops=flops,
        name="second_b",
    )
    pass_b = turn(far_t, -1)
    next_t, prev_t, own_b = call(
        back_kernel,
        (s, shifted_b, w_second, loss_b),
        back_outs,
        [] if NEAR_ALL[1] else [pltpu.VMEM((rows, taps * width), BF16), dma],
        smem=1,
        hbm=() if NEAR_ALL[1] else (1,),
        cost=4,
        flops=2 * rows * taps * width * width * 3,
        name="back_b",
    )
    from_prev_b = turn(next_t, 1)
    relayed_b = added(prev_t, pass_b, "relay_b")
    from_following_b = turn(relayed_b, -1)

    own_rows = width_all // replicas
    mine_second, theirs = call(
        functools.partial(weight_second_kernel, taps, NEAR_ALL),
        (c, all_a, all_b, shifted_a, shifted_b),
        [like((groups, taps * own_rows, width))] * 2,
        (all_far + [dma((width_all // 256,)), dma]) * (2 - sum(NEAR_ALL)),
        smem=1,
        hbm=tuple(at for at in (1, 2, 3, 4) if not NEAR_ALL[(at - 1) % 2]),
        cost=4,
        after=(relayed_a, relayed_b),
        flops=4 * rows * taps * width * width_all,
        name="weight_second",
    )
    first_rows = in_width // replicas
    size_second, size_first = taps * own_rows, taps * first_rows + 8
    joint_like = like((groups, size_second + size_first, width))
    (joint,) = call(
        functools.partial(join_kernel, 0),
        (mine_second, other_core(theirs)),
        [joint_like],
        [pltpu.VMEM((groups, size_second, width), BF16), dma((4,))],
        hbm_outs=(0,),
        name="join_second",
    )

    mine_first, theirs = call(
        functools.partial(weight_first_kernel, normaliser, taps, (NEAR_SMALL, *NEAR_PHASES)),
        (c, loss_a, loss_b, h_a, h_b, own_a, own_b, from_prev_a, from_prev_b, from_following_a,
         from_following_b, pass_a, pass_b, phases_a, phases_b),
        [like((groups, taps * first_rows + 8, width))] * 2,
        [pltpu.VMEM((2 * cols, frames + 8, width), F32), pltpu.VMEM((2 * rows, 2 * width), BF16)]
        + [pltpu.VMEM((10, rows + 8, width), BF16), dma((10,))] * (not NEAR_SMALL)
        + phases_far * (2 - sum(NEAR_PHASES)),
        smem=1,
        hbm=tuple(at for at in (13, 14) if not NEAR_PHASES[at - 13]),
        loose=() if NEAR_SMALL else tuple(range(3, 13)),
        cost=20,
        after=(mine_second,),
        flops=4 * rows * taps * width * in_width,
        name="weight_first",
    )
    (joint,) = call(
        functools.partial(join_late_kernel, size_second),
        (mine_first, other_core(theirs), joint),
        [joint_like],
        [pltpu.VMEM((groups, size_first, width), BF16), dma((4,))],
        hbm=(2,),
        hbm_outs=(0,),
        aliases={2: 0},
        name="join_first",
    )
    blocks = lax.all_to_all(joint, ZY, 0, 0)
    grad_second, grad_first, layer_loss = call(
        functools.partial(total_kernel, taps, count_all),
        (blocks,),
        [like((taps, own_rows, width), F32), like((taps, first_rows, width), F32),
         like((2,), F32)],
        smem_outs=(2,),
        name="total",
    )
    return (layer_loss, jnp.transpose(grad_first, (1, 0, 2)), jnp.transpose(grad_second, (1, 0, 2)))


def solution(mesh):
    finer = Mesh(
        mesh.devices.reshape(4, 4, 2, mesh.shape["section"]), ("dp_0", "dp_1", "dp_2", "section")
    )
    return jax.shard_map(
        shards,
        mesh=finer,
        in_specs=(
            P(DP, None, None),
            P(DP, None, None),
            P(None, None, "section"),
            P(None, None, "section"),
        ),
        out_specs=(P(), P(DP, None, "section"), P(DP, None, "section")),
        check_vma=False,
    )
```

```python
import functools

import jax
import jax.numpy as jnp
from jax import lax
from jax.experimental import pallas as pl
from jax.experimental.pallas import tpu as pltpu
from jax.sharding import Mesh
from jax.sharding import PartitionSpec as P

DP = ("dp_0", "dp_1", "dp_2")
ZY = ("dp_0", "dp_1")
F32 = jnp.float32
BF16 = jnp.bfloat16
VMEM_LIMIT = 16 << 20
NEAR_PHASES = (True, False)
NEAR_ALL = (True, True)
NEAR_SMALL = True

smooth_width = 0.1
leak_slope = 0.1


def leaky(pre):
    return jnp.where(pre > 0, pre, leak_slope * pre).astype(BF16)


def fold_rows(x):
    x = jnp.sum(x.reshape(-1, 8, x.shape[1]), axis=0)
    return sum(x[:, at : at + 128] for at in range(0, x.shape[1], 128))


def difference_terms(real, fake):
    difference = real.astype(F32) - fake.astype(F32)
    square = difference * difference + smooth_width * smooth_width
    inverse = lax.rsqrt(square)
    return difference * inverse, square * inverse


def dot(a, b):
    return jnp.dot(a, b, preferred_element_type=F32)


def dot_rows(a, b):
    return lax.dot_general(a, b, (((0,), (0,)), ((), ())), preferred_element_type=F32)


def dot_lanes(a, b):
    return lax.dot_general(a, b, (((1,), (1,)), ((), ())), preferred_element_type=F32)


def losses_split(first, second):
    value = jnp.sum(jnp.concatenate([first, second], axis=1), axis=0, keepdims=True)
    return split_rows(value, 0)


def split_rows(value, base):
    row = lax.broadcasted_iota(jnp.int32, (8, value.shape[1]), 0) - base
    high = value.astype(BF16).astype(F32)
    middle = (value - high).astype(BF16).astype(F32)
    low = value - high - middle
    out = jnp.where(row == 0, high, jnp.where(row == 1, middle, jnp.where(row == 2, low, 0.0)))
    return out.astype(BF16)


def strided_conv(take, cols, span, w, h_out, phases_out, loss, padded, *far):
    phases = far[0] if far else phases_out
    frames = span // 3
    rows = 2 * cols * frames
    width = w.shape[2]
    row = lax.broadcasted_iota(jnp.int32, (span, span), 0)
    col = lax.broadcasted_iota(jnp.int32, (span, span), 1)
    phase = jnp.where(row >= 2 * frames, 2, jnp.where(row >= frames, 1, 0))
    select = (col == 3 * (row - frames * phase) + phase).astype(F32).astype(BF16)
    for n in range(2 * cols):
        parts = dot(select, take(n)).astype(BF16)
        for p in range(3):
            phases[p, n * frames : (n + 1) * frames, :] = parts[p * frames : (p + 1) * frames]
    if far:
        copy_out = pltpu.make_async_copy(phases, phases_out, far[1])
        copy_out.start()
    padded[:, :8, :] = jnp.zeros((2 * cols, 8, width), F32)
    earlier = dot(phases[1], w[0]) + dot(phases[2], w[1])
    padded[:, 8 : 8 + frames, :] = earlier.reshape(2 * cols, frames, width)
    same = dot(phases[0], w[2]) + dot(phases[1], w[3]) + dot(phases[2], w[4])
    h = leaky(same + padded[:, 7 : 7 + frames, :].reshape(rows, width))
    h_out[...] = h
    _, root = difference_terms(h[: rows // 2], h[rows // 2 :])
    loss[...] = fold_rows(root - smooth_width)
    if far:
        copy_out.wait()


def copies_of(source, target, sems):
    return [
        pltpu.make_async_copy(source.at[n], target.at[n], sems.at[n])
        for n in range(source.shape[0])
    ]


def first_early_kernel(
    real, fake, w_hbm, h_out, phases_out, loss, w, rest,
    padded, held, held_sem, rest_sem, w_sem, *far_scratch,
):
    cols = held.shape[0] // 2
    span = held.shape[1]
    for n in range(2 * cols):
        source = real if n < cols else fake
        pltpu.make_async_copy(source.at[n % cols], held.at[n], held_sem.at[n]).start()
    w_copies = copies_of(w_hbm, w, w_sem)
    for copy in w_copies:
        copy.start()
    rest_copies = [
        pltpu.make_async_copy(x.at[cols:], rest.at[at * cols : (at + 1) * cols], rest_sem.at[at])
        for at, x in enumerate((real, fake))
    ]

    for copy in rest_copies:
        copy.start()

    def take(n):
        source = real if n < cols else fake
        pltpu.make_async_copy(source.at[n % cols], held.at[n], held_sem.at[n]).wait()
        if n == 2 * cols - 1:
            for copy in w_copies:
                copy.wait()
        return held[n]

    strided_conv(take, cols, span, w, h_out, phases_out, loss, padded, *far_scratch)
    for copy in rest_copies:
        copy.wait()


def first_late_kernel(rest, w, w_next_hbm, h_out, phases_out, loss, w_next, padded, sem, *far):
    copies = copies_of(w_next_hbm, w_next, sem)
    for copy in copies:
        copy.start()
    cols, span = rest.shape[0] // 2, rest.shape[1]
    strided_conv(lambda n: rest[n], cols, span, w, h_out, phases_out, loss, padded, *far)
    for copy in copies:
        copy.wait()


def second_kernel(
    normaliser, whole, near, s_ref, own, prev, following, far, w, loss_first,
    all_out, shifted_out, far_t, loss, *rest,
):
    if near:
        h_all, shifted = all_out, shifted_out
        *backs, padded, in_sems = rest
    else:
        *backs, padded, in_sems, h_all, shifted, all_sem, shifted_sem = rest
    rows, width = own.shape
    half = rows // 2
    taps = w.shape[0]
    frames = padded.shape[1] - 16
    s = s_ref[0]
    copies = []
    for away, x in enumerate((own, following, far, prev)):
        at = pl.multiple_of(lax.rem(s + away, 4) * width, 256)
        copies.append(
            pltpu.make_async_copy(x, h_all.at[:, pl.ds(at, width)], in_sems.at[away])
        )
        copies[-1].start()
    for copy in copies:
        copy.wait()
    if not near:
        copy_all = pltpu.make_async_copy(h_all, all_out, all_sem)
        copy_all.start()
    zeros = jnp.zeros((padded.shape[0], 8, width), F32)
    padded[:, :8, :] = zeros
    padded[:, 8 + frames :, :] = zeros
    pre = dot(h_all[...], w[2])
    for k in (0, 1, 3, 4):
        padded[:, 8 : 8 + frames, :] = dot(h_all[...], w[k]).reshape(-1, frames, width)
        pre = pre + padded[:, 6 + k : 6 + k + frames, :].reshape(rows, width)
    h = leaky(pre)
    slope, root = difference_terms(h[:half], h[half:])
    loss_rows = losses_split(loss_first[...], fold_rows(root - smooth_width))
    loss[...] = loss_rows
    slope = slope * (1.0 / normaliser)
    for value, sign, at in ((h[:half], 1.0, 0), (h[half:], -1.0, half // frames)):
        gate = jnp.where(value.astype(F32) > 0, 1.0, leak_slope)
        delta = (sign * slope * gate).astype(BF16).astype(F32)
        padded[at : at + half // frames, 8 : 8 + frames, :] = delta.reshape(-1, frames, width)
    for k in range(taps):
        moved = padded[:, 10 - k : 10 - k + frames, :].reshape(rows, width)
        shifted[:, k * width : (k + 1) * width] = moved.astype(BF16)
    if not near:
        copy_shifted = pltpu.make_async_copy(shifted, shifted_out, shifted_sem)
        copy_shifted.start()
    far_t[:rows] = back_term(s, 2, shifted, w)
    far_t[rows:] = loss_rows
    if whole:
        back_rest(s, shifted, w, loss_rows, 3, *backs)
    if not near:
        copy_all.wait()
        copy_shifted.wait()


def back_term(s, away, shifted, w):
    width = w.shape[2]
    at = pl.multiple_of(lax.rem(s + away, 4) * width, 256)
    term = None
    for k in range(w.shape[0]):
        part = dot_lanes(shifted[:, k * width : (k + 1) * width], w[k, pl.ds(at, width), :])
        term = part if term is None else term + part
    return term.astype(BF16)


def back_rest(s, shifted, w, loss_rows, with_loss, following, prev, own):
    rows = own.shape[0]
    for away, out in ((1, following), (3, prev)) if with_loss == 1 else ((3, prev), (1, following)):
        out[:rows] = back_term(s, away, shifted, w)
        out[rows:] = loss_rows if away == with_loss else jnp.zeros_like(loss_rows)
    own[...] = back_term(s, 0, shifted, w)


def back_kernel(s_ref, shifted, w, loss, following, prev, own, *rest):
    if rest:
        held, sem = rest
        copy = pltpu.make_async_copy(shifted, held, sem)
        copy.start()
        copy.wait()
        shifted = held
    back_rest(s_ref[0], shifted, w, loss[...], 1, following, prev, own)


def add_kernel(a, b, out):
    out[...] = (a[...].astype(F32) + b[...].astype(F32)).astype(BF16)


def put(g, c, outs, at, rows, k):
    count = g.shape[0] // (2 * rows)
    g = g.astype(BF16).reshape(count, 2, rows, g.shape[1])
    even, odd = g[:, 0], g[:, 1]
    mine, theirs = outs
    mine[at : at + count, k * rows : (k + 1) * rows] = jnp.where(c == 0, even, odd)
    theirs[at : at + count, k * rows : (k + 1) * rows] = jnp.where(c == 0, odd, even)


def weight_second_kernel(taps, nears, c_ref, h_a, h_b, shifted_a, shifted_b, mine, theirs, *rest):
    own_rows, width = mine.shape[1] // taps, mine.shape[2]
    c = c_ref[0]
    step = 256
    count = h_a.shape[1] // step
    rest = list(rest)
    pairs, first, later = [], [], [[] for _ in range(count)]
    for near, h, x in ((nears[0], h_a, shifted_a), (nears[1], h_b, shifted_b)):
        if not near:
            h_held, x_held, h_sem, x_sem = rest[:4]
            rest = rest[4:]
            first.append(pltpu.make_async_copy(x, x_held, x_sem))
            for q in range(count):
                cut = slice(q * step, (q + 1) * step)
                later[q].append(
                    pltpu.make_async_copy(h.at[:, cut], h_held.at[:, cut], h_sem.at[q])
                )
            h, x = h_held, x_held
        pairs.append((h, x))
    for copy in first + sum(later, []):
        copy.start()
    for copy in first:
        copy.wait()
    for q in range(count):
        for copy in later[q]:
            copy.wait()
        cut = slice(q * step, (q + 1) * step)
        g = sum(dot_rows(h[:, cut], x[...]) for h, x in pairs)
        for k in range(taps):
            put(g[:, k * width : (k + 1) * width], c, (mine, theirs),
                q * step // (2 * own_rows), own_rows, k)


def weight_first_kernel(
    normaliser, taps, nears, c_ref, loss_a, loss_b, *refs,
):
    *sources, phases_a, phases_b, mine, theirs, padded, moved = refs[:16]
    rest = list(refs[16:])
    rows, width = sources[0].shape
    half = rows // 2
    frames = padded.shape[1] - 8
    c = c_ref[0]
    small, large = [], []
    if not nears[0]:
        got, sems = rest[:2]
        rest = rest[2:]
        for n, x in enumerate(sources):
            small.append(pltpu.make_async_copy(x, got.at[n, : x.shape[0]], sems.at[n]))
        sources = [got.at[n, : x.shape[0]] for n, x in enumerate(sources)]
    phases = []
    for near, x in zip(nears[1:], (phases_a, phases_b)):
        if not near:
            held, sem = rest[:2]
            rest = rest[2:]
            large.append(pltpu.make_async_copy(x, held, sem))
            x = held
        phases.append(x)
    for copy in small + large:
        copy.start()
    for copy in small:
        copy.wait()
    padded[:, frames:, :] = jnp.zeros((padded.shape[0], 8, width), F32)
    for n in range(2):
        h, own, a, b = (sources[2 * at + n] for at in range(4))
        slope, _ = difference_terms(h[:half], h[half:rows])
        slope = slope * (1.0 / normaliser)
        for at, sign in ((0, 1.0), (half, -1.0)):
            cut = slice(at, at + half)
            up = own[cut].astype(F32) + a[cut].astype(F32) + b[cut].astype(F32)
            up = up.astype(BF16).astype(F32)
            gate = jnp.where(h[cut].astype(F32) > 0, 1.0, leak_slope)
            delta = ((sign * slope + up) * gate).astype(BF16)
            base = n * rows + at
            moved[base : base + half, :width] = delta
            cols, lead = half // frames, base // frames
            padded[lead : lead + cols, :frames, :] = delta.astype(F32).reshape(cols, frames, width)
    moved[:, width:] = padded[:, 1 : 1 + frames, :].reshape(2 * rows, width).astype(BF16)
    groups = mine.shape[0]
    own_rows = (mine.shape[1] - 8) // taps
    outs = (mine, theirs)
    for copy in large:
        copy.wait()
    for p in range(3):
        lanes = width if p == 0 else 2 * width
        g = dot_rows(phases[0][p], moved[:rows, :lanes])
        g = g + dot_rows(phases[1][p], moved[rows:, :lanes])
        put(g[:, :width], c, outs, 0, own_rows, 2 + p)
        if p > 0:
            put(g[:, width:], c, outs, 0, own_rows, p - 1)
    total = loss_a[...].astype(F32) + loss_b[...].astype(F32)
    for x in sources[4:]:
        total = total + x[rows:].astype(F32)
    lines = split_rows(jnp.sum(total, axis=0, keepdims=True), 3 * c)
    for x in outs:
        x[:, taps * own_rows :, :] = jnp.broadcast_to(lines[None], (groups, 8, width))


def same_kernel(a, out):
    out[...] = a[...]


def join_kernel(at, a, b, joint, summed, sems):
    count = sems.shape[0]
    step = a.shape[0] // count
    copies = []
    for n in range(count):
        cut = slice(n * step, (n + 1) * step)
        summed[cut] = (a[cut].astype(F32) + b[cut].astype(F32)).astype(BF16)
        copies.append(
            pltpu.make_async_copy(
                summed.at[cut], joint.at[cut, at : at + summed.shape[1]], sems.at[n]
            )
        )
        copies[-1].start()
    for copy in copies:
        copy.wait()


def join_late_kernel(at, a, b, held, joint, summed, sem):
    del held
    join_kernel(at, a, b, joint, summed, sem)


def total_kernel(taps, count_all, blocks, second, first, loss):
    total = jnp.sum(blocks[...].astype(F32), axis=0)
    at = 0
    for out in (second, first):
        rows = taps * out.shape[1]
        out[...] = total[at : at + rows].reshape(out.shape)
        at += rows
    lines = total[at:]
    loss[0] = jnp.sum(lines[:, :128]) / count_all
    loss[1] = jnp.sum(lines[:, 128:]) / count_all


def call(
    kernel, operands, outs, scratch=(), smem=0, hbm=(), loose=(), after=(), smem_outs=(),
    hbm_outs=(), aliases={}, flops=0, cost=1, name=None,
):
    moved = sum(x.size * x.dtype.itemsize for x in operands)
    moved += sum(x.size * x.dtype.itemsize for x in outs)
    vmem, small = pl.BlockSpec(memory_space=pltpu.VMEM), pl.BlockSpec(memory_space=pltpu.SMEM)
    far, anywhere = pl.BlockSpec(memory_space=pltpu.HBM), pl.BlockSpec(memory_space=pl.ANY)
    count = len(operands)
    operands = tuple(
        pltpu.with_memory_space_constraint(x, pltpu.HBM) if at in hbm else x
        for at, x in enumerate(operands)
    )

    def body(*refs):
        kernel(*refs[:count], *refs[count + len(after) :])

    return pl.pallas_call(
        body,
        out_shape=[
            pltpu.HBM(x.shape, x.dtype) if at in hbm_outs else x for at, x in enumerate(outs)
        ],
        in_specs=[
            small if at < smem else far if at in hbm else anywhere if at in loose else vmem
            for at in range(count)
        ]
        + [anywhere] * len(after),
        out_specs=[
            small if at in smem_outs else far if at in hbm_outs else vmem
            for at in range(len(outs))
        ],
        scratch_shapes=list(scratch),
        input_output_aliases=aliases,
        compiler_params=pltpu.CompilerParams(vmem_limit_bytes=VMEM_LIMIT),
        cost_estimate=pl.CostEstimate(
            flops=int(flops * cost), bytes_accessed=int(moved * cost), transcendentals=0
        ),
        name=name,
    )(*operands, *after)


def like(shape, dtype=BF16):
    return jax.ShapeDtypeStruct(shape, dtype)


def turn(x, step):
    count = lax.axis_size("section")
    return lax.ppermute(x, "section", [(i, (i + step) % count) for i in range(count)])


def later(x, after, name):
    return call(same_kernel, (x,), [like(x.shape)], after=after, name=name)[0]


def added(a, b, name, after=()):
    return call(add_kernel, (a, b), [like(a.shape)], after=after, name=name)[0]


def other_core(x):
    return lax.ppermute(x, "dp_2", [(0, 1), (1, 0)])


def shards(real_in, fake_in, kernel_first, kernel_second):
    replicas = lax.axis_size(DP)
    cols, span, in_width = real_in.shape
    frames = span // 3
    taps, width_all, width = kernel_second.shape
    normaliser = float(cols * frames)
    count_all = float(cols * replicas * frames * width_all)
    groups = replicas // 2
    part = cols // 2
    rows = cols * frames
    s = lax.axis_index("section").reshape(1).astype(jnp.int32)
    c = lax.axis_index("dp_2").reshape(1).astype(jnp.int32)
    dma = pltpu.SemaphoreType.DMA
    chunk_outs = [like((rows, width)), like((3, rows, in_width)), like((8, 128), F32)]
    conv_scratch = [pltpu.VMEM((cols, frames + 8, width), F32)]
    phases_far = [pltpu.VMEM((3, rows, in_width), BF16), dma]
    all_far = [pltpu.VMEM((rows, width_all), BF16), pltpu.VMEM((rows, taps * width), BF16)]
    flops = 2 * rows * taps * in_width * width

    h_a, phases_a, loss_a, w_first, rest = call(
        first_early_kernel,
        (real_in, fake_in, kernel_first),
        chunk_outs + [like(kernel_first.shape), like((cols, span, in_width))],
        conv_scratch
        + [pltpu.VMEM((cols, span, in_width), BF16), dma((cols,)), dma((2,)), dma((taps,))]
        + phases_far * (not NEAR_PHASES[0]),
        hbm=(0, 1, 2),
        hbm_outs=() if NEAR_PHASES[0] else (1,),
        flops=flops,
        name="first_a",
    )
    prev_a = turn(h_a, 1)
    following_a = turn(h_a, -1)
    h_b, phases_b, loss_b, w_second = call(
        first_late_kernel,
        (rest, w_first, kernel_second),
        chunk_outs + [like(kernel_second.shape)],
        conv_scratch + [dma((taps,))] + phases_far * (not NEAR_PHASES[1]),
        hbm=(2,),
        hbm_outs=() if NEAR_PHASES[1] else (1,),
        flops=flops,
        cost=1,
        name="first_b",
    )
    far_a = turn(prev_a, 1)
    following_b = turn(h_b, -1)
    prev_b = turn(later(h_b, (following_a,), "ordered"), 1)
    far_b = turn(following_b, -1)

    second_outs = [like((rows, width_all)), like((rows, taps * width)), like((rows + 8, width)),
                   like((8, width))]
    back_outs = [like((rows + 8, width)), like((rows + 8, width)), like((rows, width))]
    second_scratch = [
        pltpu.VMEM((cols, frames + 16, width), F32), dma((4,)),
    ]
    copies = all_far + [dma, dma]
    flops = 2 * rows * taps * (width_all + width) * width
    all_a, shifted_a, far_t, loss_a, next_t, prev_t, own_a = call(
        functools.partial(second_kernel, normaliser, True, NEAR_ALL[0]),
        (s, h_a, prev_a, following_a, far_a, w_second, loss_a),
        second_outs + back_outs,
        second_scratch + copies * (not NEAR_ALL[0]),
        smem=1,
        loose=(1, 2, 3, 4),
        hbm_outs=() if NEAR_ALL[0] else (0, 1),
        cost=1,
        flops=flops,
        name="second_a",
    )
    pass_a = turn(far_t, 1)
    from_following_a = turn(prev_t, -1)
    relayed_a = added(next_t, pass_a, "relay_a", after=(from_following_a,))
    from_prev_a = turn(relayed_a, 1)

    all_b, shifted_b, far_t, loss_b = call(
        functools.partial(second_kernel, normaliser, False, NEAR_ALL[1]),
        (s, h_b, prev_b, following_b, far_b, w_second, loss_b),
        second_outs,
        second_scratch + copies * (not NEAR_ALL[1]),
        smem=1,
        loose=(1, 2, 3, 4),
        hbm_outs=() if NEAR_ALL[1] else (0, 1),
        cost=1,
        after=(own_a,),
        flops=flops,
        name="second_b",
    )
    pass_b = turn(far_t, -1)
    next_t, prev_t, own_b = call(
        back_kernel,
        (s, shifted_b, w_second, loss_b),
        back_outs,
        [] if NEAR_ALL[1] else [pltpu.VMEM((rows, taps * width), BF16), dma],
        smem=1,
        hbm=() if NEAR_ALL[1] else (1,),
        cost=4,
        flops=2 * rows * taps * width * width * 3,
        name="back_b",
    )
    from_prev_b = turn(next_t, 1)
    relayed_b = added(prev_t, pass_b, "relay_b")
    from_following_b = turn(relayed_b, -1)

    own_rows = width_all // replicas
    mine_second, theirs = call(
        functools.partial(weight_second_kernel, taps, NEAR_ALL),
        (c, all_a, all_b, shifted_a, shifted_b),
        [like((groups, taps * own_rows, width))] * 2,
        (all_far + [dma((width_all // 256,)), dma]) * (2 - sum(NEAR_ALL)),
        smem=1,
        hbm=tuple(at for at in (1, 2, 3, 4) if not NEAR_ALL[(at - 1) % 2]),
        cost=4,
        after=(relayed_a, relayed_b),
        flops=4 * rows * taps * width * width_all,
        name="weight_second",
    )
    first_rows = in_width // replicas
    size_second, size_first = taps * own_rows, taps * first_rows + 8
    joint_like = like((groups, size_second + size_first, width))
    (joint,) = call(
        functools.partial(join_kernel, 0),
        (mine_second, other_core(theirs)),
        [joint_like],
        [pltpu.VMEM((groups, size_second, width), BF16), dma((4,))],
        hbm_outs=(0,),
        name="join_second",
    )

    mine_first, theirs = call(
        functools.partial(weight_first_kernel, normaliser, taps, (NEAR_SMALL, *NEAR_PHASES)),
        (c, loss_a, loss_b, h_a, h_b, own_a, own_b, from_prev_a, from_prev_b, from_following_a,
         from_following_b, pass_a, pass_b, phases_a, phases_b),
        [like((groups, taps * first_rows + 8, width))] * 2,
        [pltpu.VMEM((2 * cols, frames + 8, width), F32), pltpu.VMEM((2 * rows, 2 * width), BF16)]
        + [pltpu.VMEM((10, rows + 8, width), BF16), dma((10,))] * (not NEAR_SMALL)
        + phases_far * (2 - sum(NEAR_PHASES)),
        smem=1,
        hbm=tuple(at for at in (13, 14) if not NEAR_PHASES[at - 13]),
        loose=() if NEAR_SMALL else tuple(range(3, 13)),
        cost=20,
        after=(mine_second,),
        flops=4 * rows * taps * width * in_width,
        name="weight_first",
    )
    (joint,) = call(
        functools.partial(join_late_kernel, size_second),
        (mine_first, other_core(theirs), joint),
        [joint_like],
        [pltpu.VMEM((groups, size_first, width), BF16), dma((4,))],
        hbm=(2,),
        hbm_outs=(0,),
        aliases={2: 0},
        name="join_first",
    )
    blocks = lax.all_to_all(joint, ZY, 0, 0)
    grad_second, grad_first, layer_loss = call(
        functools.partial(total_kernel, taps, count_all),
        (blocks,),
        [like((taps, own_rows, width), F32), like((taps, first_rows, width), F32),
         like((2,), F32)],
        smem_outs=(2,),
        name="total",
    )
    return (layer_loss, jnp.transpose(grad_first, (1, 0, 2)), jnp.transpose(grad_second, (1, 0, 2)))


def solution(mesh):
    finer = Mesh(
        mesh.devices.reshape(4, 4, 2, mesh.shape["section"]), ("dp_0", "dp_1", "dp_2", "section")
    )
    return jax.shard_map(
        shards,
        mesh=finer,
        in_specs=(
            P(DP, None, None),
            P(DP, None, None),
            P(None, None, "section"),
            P(None, None, "section"),
        ),
        out_specs=(P(), P(DP, None, "section"), P(DP, None, "section")),
        check_vma=False,
    )
```

```python
import functools

import jax
import jax.numpy as jnp
from jax import lax
from jax.experimental import pallas as pl
from jax.experimental.pallas import tpu as pltpu
from jax.sharding import Mesh
from jax.sharding import PartitionSpec as P

DP = ("dp_0", "dp_1", "dp_2")
ZY = ("dp_0", "dp_1")
F32 = jnp.float32
BF16 = jnp.bfloat16
VMEM_LIMIT = 16 << 20
NEAR_PHASES = (True, False)
NEAR_ALL = (True, True)
NEAR_SMALL = True

smooth_width = 0.1
leak_slope = 0.1


def leaky(pre):
    return jnp.where(pre > 0, pre, leak_slope * pre).astype(BF16)


def fold_rows(x):
    x = jnp.sum(x.reshape(-1, 8, x.shape[1]), axis=0)
    return sum(x[:, at : at + 128] for at in range(0, x.shape[1], 128))


def difference_terms(real, fake):
    difference = real.astype(F32) - fake.astype(F32)
    square = difference * difference + smooth_width * smooth_width
    inverse = lax.rsqrt(square)
    return difference * inverse, square * inverse


def dot(a, b):
    return jnp.dot(a, b, preferred_element_type=F32)


def dot_rows(a, b):
    return lax.dot_general(a, b, (((0,), (0,)), ((), ())), preferred_element_type=F32)


def dot_lanes(a, b):
    return lax.dot_general(a, b, (((1,), (1,)), ((), ())), preferred_element_type=F32)


def losses_split(first, second):
    value = jnp.sum(jnp.concatenate([first, second], axis=1), axis=0, keepdims=True)
    return split_rows(value, 0)


def split_rows(value, base):
    row = lax.broadcasted_iota(jnp.int32, (8, value.shape[1]), 0) - base
    high = value.astype(BF16).astype(F32)
    middle = (value - high).astype(BF16).astype(F32)
    low = value - high - middle
    out = jnp.where(row == 0, high, jnp.where(row == 1, middle, jnp.where(row == 2, low, 0.0)))
    return out.astype(BF16)


def strided_conv(take, cols, span, w, h_out, phases_out, loss, padded, *far):
    phases = far[0] if far else phases_out
    frames = span // 3
    rows = 2 * cols * frames
    width = w.shape[2]
    row = lax.broadcasted_iota(jnp.int32, (span, span), 0)
    col = lax.broadcasted_iota(jnp.int32, (span, span), 1)
    phase = jnp.where(row >= 2 * frames, 2, jnp.where(row >= frames, 1, 0))
    select = (col == 3 * (row - frames * phase) + phase).astype(F32).astype(BF16)
    for n in range(2 * cols):
        parts = dot(select, take(n)).astype(BF16)
        for p in range(3):
            phases[p, n * frames : (n + 1) * frames, :] = parts[p * frames : (p + 1) * frames]
    if far:
        copy_out = pltpu.make_async_copy(phases, phases_out, far[1])
        copy_out.start()
    padded[:, :8, :] = jnp.zeros((2 * cols, 8, width), F32)
    earlier = dot(phases[1], w[0]) + dot(phases[2], w[1])
    padded[:, 8 : 8 + frames, :] = earlier.reshape(2 * cols, frames, width)
    same = dot(phases[0], w[2]) + dot(phases[1], w[3]) + dot(phases[2], w[4])
    h = leaky(same + padded[:, 7 : 7 + frames, :].reshape(rows, width))
    h_out[...] = h
    _, root = difference_terms(h[: rows // 2], h[rows // 2 :])
    loss[...] = fold_rows(root - smooth_width)
    if far:
        copy_out.wait()


def copies_of(source, target, sems):
    return [
        pltpu.make_async_copy(source.at[n], target.at[n], sems.at[n])
        for n in range(source.shape[0])
    ]


def first_early_kernel(
    real, fake, w_hbm, h_out, phases_out, loss, w, rest,
    padded, held, held_sem, rest_sem, w_sem, *far_scratch,
):
    cols = held.shape[0] // 2
    span = held.shape[1]
    for n in range(2 * cols):
        source = real if n < cols else fake
        pltpu.make_async_copy(source.at[n % cols], held.at[n], held_sem.at[n]).start()
    w_copies = copies_of(w_hbm, w, w_sem)
    for copy in w_copies:
        copy.start()
    rest_copies = [
        pltpu.make_async_copy(x.at[cols:], rest.at[at * cols : (at + 1) * cols], rest_sem.at[at])
        for at, x in enumerate((real, fake))
    ]

    for copy in rest_copies:
        copy.start()

    def take(n):
        source = real if n < cols else fake
        pltpu.make_async_copy(source.at[n % cols], held.at[n], held_sem.at[n]).wait()
        if n == 2 * cols - 1:
            for copy in w_copies:
                copy.wait()
        return held[n]

    strided_conv(take, cols, span, w, h_out, phases_out, loss, padded, *far_scratch)
    for copy in rest_copies:
        copy.wait()


def first_late_kernel(rest, w, w_next_hbm, h_out, phases_out, loss, w_next, padded, sem, *far):
    copies = copies_of(w_next_hbm, w_next, sem)
    for copy in copies:
        copy.start()
    cols, span = rest.shape[0] // 2, rest.shape[1]
    strided_conv(lambda n: rest[n], cols, span, w, h_out, phases_out, loss, padded, *far)
    for copy in copies:
        copy.wait()


def second_kernel(
    normaliser, whole, near, s_ref, own, prev, following, far, w, loss_first,
    all_out, shifted_out, far_t, loss, *rest,
):
    if near:
        h_all, shifted = all_out, shifted_out
        *backs, padded, in_sems = rest
    else:
        *backs, padded, in_sems, h_all, shifted, all_sem, shifted_sem = rest
    rows, width = own.shape
    half = rows // 2
    taps = w.shape[0]
    frames = padded.shape[1] - 16
    s = s_ref[0]
    copies = []
    for away, x in enumerate((own, following, far, prev)):
        at = pl.multiple_of(lax.rem(s + away, 4) * width, 256)
        copies.append(
            pltpu.make_async_copy(x, h_all.at[:, pl.ds(at, width)], in_sems.at[away])
        )
        copies[-1].start()
    for copy in copies:
        copy.wait()
    if not near:
        copy_all = pltpu.make_async_copy(h_all, all_out, all_sem)
        copy_all.start()
    zeros = jnp.zeros((padded.shape[0], 8, width), F32)
    padded[:, :8, :] = zeros
    padded[:, 8 + frames :, :] = zeros
    pre = dot(h_all[...], w[2])
    for k in (0, 1, 3, 4):
        padded[:, 8 : 8 + frames, :] = dot(h_all[...], w[k]).reshape(-1, frames, width)
        pre = pre + padded[:, 6 + k : 6 + k + frames, :].reshape(rows, width)
    h = leaky(pre)
    slope, root = difference_terms(h[:half], h[half:])
    loss_rows = losses_split(loss_first[...], fold_rows(root - smooth_width))
    loss[...] = loss_rows
    slope = slope * (1.0 / normaliser)
    for value, sign, at in ((h[:half], 1.0, 0), (h[half:], -1.0, half // frames)):
        gate = jnp.where(value.astype(F32) > 0, 1.0, leak_slope)
        delta = (sign * slope * gate).astype(BF16).astype(F32)
        padded[at : at + half // frames, 8 : 8 + frames, :] = delta.reshape(-1, frames, width)
    for k in range(taps):
        moved = padded[:, 10 - k : 10 - k + frames, :].reshape(rows, width)
        shifted[:, k * width : (k + 1) * width] = moved.astype(BF16)
    if not near:
        copy_shifted = pltpu.make_async_copy(shifted, shifted_out, shifted_sem)
        copy_shifted.start()
    far_t[:rows] = back_term(s, 2, shifted, w)
    far_t[rows:] = loss_rows
    if whole:
        back_rest(s, shifted, w, loss_rows, 3, *backs)
    if not near:
        copy_all.wait()
        copy_shifted.wait()


def back_term(s, away, shifted, w):
    width = w.shape[2]
    at = pl.multiple_of(lax.rem(s + away, 4) * width, 256)
    term = None
    for k in range(w.shape[0]):
        part = dot_lanes(shifted[:, k * width : (k + 1) * width], w[k, pl.ds(at, width), :])
        term = part if term is None else term + part
    return term.astype(BF16)


def back_rest(s, shifted, w, loss_rows, with_loss, following, prev, own):
    rows = own.shape[0]
    for away, out in ((1, following), (3, prev)) if with_loss == 1 else ((3, prev), (1, following)):
        out[:rows] = back_term(s, away, shifted, w)
        out[rows:] = loss_rows if away == with_loss else jnp.zeros_like(loss_rows)
    own[...] = back_term(s, 0, shifted, w)


def back_kernel(s_ref, shifted, w, loss, following, prev, own, *rest):
    if rest:
        held, sem = rest
        copy = pltpu.make_async_copy(shifted, held, sem)
        copy.start()
        copy.wait()
        shifted = held
    back_rest(s_ref[0], shifted, w, loss[...], 1, following, prev, own)


def add_kernel(a, b, out):
    out[...] = (a[...].astype(F32) + b[...].astype(F32)).astype(BF16)


def put(g, c, outs, at, rows, k):
    count = g.shape[0] // (2 * rows)
    g = g.astype(BF16).reshape(count, 2, rows, g.shape[1])
    even, odd = g[:, 0], g[:, 1]
    mine, theirs = outs
    mine[at : at + count, k * rows : (k + 1) * rows] = jnp.where(c == 0, even, odd)
    theirs[at : at + count, k * rows : (k + 1) * rows] = jnp.where(c == 0, odd, even)


def weight_second_kernel(taps, nears, c_ref, h_a, h_b, shifted_a, shifted_b, mine, theirs, *rest):
    own_rows, width = mine.shape[1] // taps, mine.shape[2]
    c = c_ref[0]
    step = 256
    count = h_a.shape[1] // step
    rest = list(rest)
    pairs, first, later = [], [], [[] for _ in range(count)]
    for near, h, x in ((nears[0], h_a, shifted_a), (nears[1], h_b, shifted_b)):
        if not near:
            h_held, x_held, h_sem, x_sem = rest[:4]
            rest = rest[4:]
            first.append(pltpu.make_async_copy(x, x_held, x_sem))
            for q in range(count):
                cut = slice(q * step, (q + 1) * step)
                later[q].append(
                    pltpu.make_async_copy(h.at[:, cut], h_held.at[:, cut], h_sem.at[q])
                )
            h, x = h_held, x_held
        pairs.append((h, x))
    for copy in first + sum(later, []):
        copy.start()
    for copy in first:
        copy.wait()
    for q in range(count):
        for copy in later[q]:
            copy.wait()
        cut = slice(q * step, (q + 1) * step)
        g = sum(dot_rows(h[:, cut], x[...]) for h, x in pairs)
        for k in range(taps):
            put(g[:, k * width : (k + 1) * width], c, (mine, theirs),
                q * step // (2 * own_rows), own_rows, k)


def weight_first_kernel(
    normaliser, taps, nears, c_ref, loss_a, loss_b, *refs,
):
    *sources, phases_a, phases_b, mine, theirs, padded, moved = refs[:16]
    rest = list(refs[16:])
    rows, width = sources[0].shape
    half = rows // 2
    frames = padded.shape[1] - 8
    c = c_ref[0]
    small, large = [], []
    if not nears[0]:
        got, sems = rest[:2]
        rest = rest[2:]
        for n, x in enumerate(sources):
            small.append(pltpu.make_async_copy(x, got.at[n, : x.shape[0]], sems.at[n]))
        sources = [got.at[n, : x.shape[0]] for n, x in enumerate(sources)]
    phases = []
    for near, x in zip(nears[1:], (phases_a, phases_b)):
        if not near:
            held, sem = rest[:2]
            rest = rest[2:]
            large.append(pltpu.make_async_copy(x, held, sem))
            x = held
        phases.append(x)
    for copy in small + large:
        copy.start()
    for copy in small:
        copy.wait()
    padded[:, frames:, :] = jnp.zeros((padded.shape[0], 8, width), F32)
    for n in range(2):
        h, own, a, b = (sources[2 * at + n] for at in range(4))
        slope, _ = difference_terms(h[:half], h[half:rows])
        slope = slope * (1.0 / normaliser)
        for at, sign in ((0, 1.0), (half, -1.0)):
            cut = slice(at, at + half)
            up = own[cut].astype(F32) + a[cut].astype(F32) + b[cut].astype(F32)
            up = up.astype(BF16).astype(F32)
            gate = jnp.where(h[cut].astype(F32) > 0, 1.0, leak_slope)
            delta = ((sign * slope + up) * gate).astype(BF16)
            base = n * rows + at
            moved[base : base + half, :width] = delta
            cols, lead = half // frames, base // frames
            padded[lead : lead + cols, :frames, :] = delta.astype(F32).reshape(cols, frames, width)
    moved[:, width:] = padded[:, 1 : 1 + frames, :].reshape(2 * rows, width).astype(BF16)
    groups = mine.shape[0]
    own_rows = (mine.shape[1] - 8) // taps
    outs = (mine, theirs)
    for copy in large:
        copy.wait()
    for p in range(3):
        lanes = width if p == 0 else 2 * width
        g = dot_rows(phases[0][p], moved[:rows, :lanes])
        g = g + dot_rows(phases[1][p], moved[rows:, :lanes])
        put(g[:, :width], c, outs, 0, own_rows, 2 + p)
        if p > 0:
            put(g[:, width:], c, outs, 0, own_rows, p - 1)
    total = loss_a[...].astype(F32) + loss_b[...].astype(F32)
    for x in sources[4:]:
        total = total + x[rows:].astype(F32)
    lines = split_rows(jnp.sum(total, axis=0, keepdims=True), 3 * c)
    for x in outs:
        x[:, taps * own_rows :, :] = jnp.broadcast_to(lines[None], (groups, 8, width))


def same_kernel(a, out):
    out[...] = a[...]


def join_kernel(at, a, b, joint, summed, sems):
    count = sems.shape[0]
    step = a.shape[0] // count
    copies = []
    for n in range(count):
        cut = slice(n * step, (n + 1) * step)
        summed[cut] = (a[cut].astype(F32) + b[cut].astype(F32)).astype(BF16)
        copies.append(
            pltpu.make_async_copy(
                summed.at[cut], joint.at[cut, at : at + summed.shape[1]], sems.at[n]
            )
        )
        copies[-1].start()
    for copy in copies:
        copy.wait()


def join_late_kernel(at, a, b, held, joint, summed, sem):
    del held
    join_kernel(at, a, b, joint, summed, sem)


def total_kernel(taps, count_all, blocks, second, first, loss):
    total = jnp.sum(blocks[...].astype(F32), axis=0)
    at = 0
    for out in (second, first):
        rows = taps * out.shape[1]
        out[...] = total[at : at + rows].reshape(out.shape)
        at += rows
    lines = total[at:]
    loss[0] = jnp.sum(lines[:, :128]) / count_all
    loss[1] = jnp.sum(lines[:, 128:]) / count_all


def call(
    kernel, operands, outs, scratch=(), smem=0, hbm=(), loose=(), after=(), smem_outs=(),
    hbm_outs=(), aliases={}, flops=0, cost=1, name=None,
):
    moved = sum(x.size * x.dtype.itemsize for x in operands)
    moved += sum(x.size * x.dtype.itemsize for x in outs)
    vmem, small = pl.BlockSpec(memory_space=pltpu.VMEM), pl.BlockSpec(memory_space=pltpu.SMEM)
    far, anywhere = pl.BlockSpec(memory_space=pltpu.HBM), pl.BlockSpec(memory_space=pl.ANY)
    count = len(operands)
    operands = tuple(
        pltpu.with_memory_space_constraint(x, pltpu.HBM) if at in hbm else x
        for at, x in enumerate(operands)
    )

    def body(*refs):
        kernel(*refs[:count], *refs[count + len(after) :])

    return pl.pallas_call(
        body,
        out_shape=[
            pltpu.HBM(x.shape, x.dtype) if at in hbm_outs else x for at, x in enumerate(outs)
        ],
        in_specs=[
            small if at < smem else far if at in hbm else anywhere if at in loose else vmem
            for at in range(count)
        ]
        + [anywhere] * len(after),
        out_specs=[
            small if at in smem_outs else far if at in hbm_outs else vmem
            for at in range(len(outs))
        ],
        scratch_shapes=list(scratch),
        input_output_aliases=aliases,
        compiler_params=pltpu.CompilerParams(vmem_limit_bytes=VMEM_LIMIT),
        cost_estimate=pl.CostEstimate(
            flops=int(flops * cost), bytes_accessed=int(moved * cost), transcendentals=0
        ),
        name=name,
    )(*operands, *after)


def like(shape, dtype=BF16):
    return jax.ShapeDtypeStruct(shape, dtype)


def turn(x, step):
    count = lax.axis_size("section")
    return lax.ppermute(x, "section", [(i, (i + step) % count) for i in range(count)])


def later(x, after, name):
    return call(same_kernel, (x,), [like(x.shape)], after=after, name=name)[0]


def added(a, b, name, after=()):
    return call(add_kernel, (a, b), [like(a.shape)], after=after, name=name)[0]


def other_core(x):
    return lax.ppermute(x, "dp_2", [(0, 1), (1, 0)])


def shards(real_in, fake_in, kernel_first, kernel_second):
    replicas = lax.axis_size(DP)
    cols, span, in_width = real_in.shape
    frames = span // 3
    taps, width_all, width = kernel_second.shape
    normaliser = float(cols * frames)
    count_all = float(cols * replicas * frames * width_all)
    groups = replicas // 2
    part = cols // 2
    rows = cols * frames
    s = lax.axis_index("section").reshape(1).astype(jnp.int32)
    c = lax.axis_index("dp_2").reshape(1).astype(jnp.int32)
    dma = pltpu.SemaphoreType.DMA
    chunk_outs = [like((rows, width)), like((3, rows, in_width)), like((8, 128), F32)]
    conv_scratch = [pltpu.VMEM((cols, frames + 8, width), F32)]
    phases_far = [pltpu.VMEM((3, rows, in_width), BF16), dma]
    all_far = [pltpu.VMEM((rows, width_all), BF16), pltpu.VMEM((rows, taps * width), BF16)]
    flops = 2 * rows * taps * in_width * width

    h_a, phases_a, loss_a, w_first, rest = call(
        first_early_kernel,
        (real_in, fake_in, kernel_first),
        chunk_outs + [like(kernel_first.shape), like((cols, span, in_width))],
        conv_scratch
        + [pltpu.VMEM((cols, span, in_width), BF16), dma((cols,)), dma((2,)), dma((taps,))]
        + phases_far * (not NEAR_PHASES[0]),
        hbm=(0, 1, 2),
        hbm_outs=() if NEAR_PHASES[0] else (1,),
        flops=flops,
        name="first_a",
    )
    prev_a = turn(h_a, 1)
    following_a = turn(h_a, -1)
    h_b, phases_b, loss_b, w_second = call(
        first_late_kernel,
        (rest, w_first, kernel_second),
        chunk_outs + [like(kernel_second.shape)],
        conv_scratch + [dma((taps,))] + phases_far * (not NEAR_PHASES[1]),
        hbm=(2,),
        hbm_outs=() if NEAR_PHASES[1] else (1,),
        flops=flops,
        cost=1,
        name="first_b",
    )
    far_a = turn(prev_a, 1)
    following_b = turn(h_b, -1)
    prev_b = turn(later(h_b, (following_a,), "ordered"), 1)
    far_b = turn(following_b, -1)

    second_outs = [like((rows, width_all)), like((rows, taps * width)), like((rows + 8, width)),
                   like((8, width))]
    back_outs = [like((rows + 8, width)), like((rows + 8, width)), like((rows, width))]
    second_scratch = [
        pltpu.VMEM((cols, frames + 16, width), F32), dma((4,)),
    ]
    copies = all_far + [dma, dma]
    flops = 2 * rows * taps * (width_all + width) * width
    all_a, shifted_a, far_t, loss_a, next_t, prev_t, own_a = call(
        functools.partial(second_kernel, normaliser, True, NEAR_ALL[0]),
        (s, h_a, prev_a, following_a, far_a, w_second, loss_a),
        second_outs + back_outs,
        second_scratch + copies * (not NEAR_ALL[0]),
        smem=1,
        loose=(1, 2, 3, 4),
        hbm_outs=() if NEAR_ALL[0] else (0, 1),
        cost=1,
        flops=flops,
        name="second_a",
    )
    pass_a = turn(far_t, 1)
    from_following_a = turn(prev_t, -1)
    relayed_a = added(next_t, pass_a, "relay_a")
    from_prev_a = turn(relayed_a, 1)

    all_b, shifted_b, far_t, loss_b = call(
        functools.partial(second_kernel, normaliser, False, NEAR_ALL[1]),
        (s, h_b, prev_b, following_b, far_b, w_second, loss_b),
        second_outs,
        second_scratch + copies * (not NEAR_ALL[1]),
        smem=1,
        loose=(1, 2, 3, 4),
        hbm_outs=() if NEAR_ALL[1] else (0, 1),
        cost=1,
        after=(loss_a,),
        flops=flops,
        name="second_b",
    )
    pass_b = turn(far_t, -1)
    next_t, prev_t, own_b = call(
        back_kernel,
        (s, shifted_b, w_second, loss_b),
        back_outs,
        [] if NEAR_ALL[1] else [pltpu.VMEM((rows, taps * width), BF16), dma],
        smem=1,
        hbm=() if NEAR_ALL[1] else (1,),
        cost=4,
        flops=2 * rows * taps * width * width * 3,
        name="back_b",
    )
    from_prev_b = turn(next_t, 1)
    relayed_b = added(prev_t, pass_b, "relay_b", after=(from_following_a,))
    from_following_b = turn(relayed_b, -1)

    own_rows = width_all // replicas
    mine_second, theirs = call(
        functools.partial(weight_second_kernel, taps, NEAR_ALL),
        (c, all_a, all_b, shifted_a, shifted_b),
        [like((groups, taps * own_rows, width))] * 2,
        (all_far + [dma((width_all // 256,)), dma]) * (2 - sum(NEAR_ALL)),
        smem=1,
        hbm=tuple(at for at in (1, 2, 3, 4) if not NEAR_ALL[(at - 1) % 2]),
        cost=4,
        after=(relayed_a, relayed_b),
        flops=4 * rows * taps * width * width_all,
        name="weight_second",
    )
    first_rows = in_width // replicas
    size_second, size_first = taps * own_rows, taps * first_rows + 8
    joint_like = like((groups, size_second + size_first, width))
    (joint,) = call(
        functools.partial(join_kernel, 0),
        (mine_second, other_core(theirs)),
        [joint_like],
        [pltpu.VMEM((groups, size_second, width), BF16), dma((4,))],
        hbm_outs=(0,),
        name="join_second",
    )

    mine_first, theirs = call(
        functools.partial(weight_first_kernel, normaliser, taps, (NEAR_SMALL, *NEAR_PHASES)),
        (c, loss_a, loss_b, h_a, h_b, own_a, own_b, from_prev_a, from_prev_b, from_following_a,
         from_following_b, pass_a, pass_b, phases_a, phases_b),
        [like((groups, taps * first_rows + 8, width))] * 2,
        [pltpu.VMEM((2 * cols, frames + 8, width), F32), pltpu.VMEM((2 * rows, 2 * width), BF16)]
        + [pltpu.VMEM((10, rows + 8, width), BF16), dma((10,))] * (not NEAR_SMALL)
        + phases_far * (2 - sum(NEAR_PHASES)),
        smem=1,
        hbm=tuple(at for at in (13, 14) if not NEAR_PHASES[at - 13]),
        loose=() if NEAR_SMALL else tuple(range(3, 13)),
        cost=20,
        after=(mine_second,),
        flops=4 * rows * taps * width * in_width,
        name="weight_first",
    )
    (joint,) = call(
        functools.partial(join_late_kernel, size_second),
        (mine_first, other_core(theirs), joint),
        [joint_like],
        [pltpu.VMEM((groups, size_first, width), BF16), dma((4,))],
        hbm=(2,),
        hbm_outs=(0,),
        aliases={2: 0},
        name="join_first",
    )
    blocks = lax.all_to_all(joint, ZY, 0, 0)
    grad_second, grad_first, layer_loss = call(
        functools.partial(total_kernel, taps, count_all),
        (blocks,),
        [like((taps, own_rows, width), F32), like((taps, first_rows, width), F32),
         like((2,), F32)],
        smem_outs=(2,),
        name="total",
    )
    return (layer_loss, jnp.transpose(grad_first, (1, 0, 2)), jnp.transpose(grad_second, (1, 0, 2)))


def solution(mesh):
    finer = Mesh(
        mesh.devices.reshape(4, 4, 2, mesh.shape["section"]), ("dp_0", "dp_1", "dp_2", "section")
    )
    return jax.shard_map(
        shards,
        mesh=finer,
        in_specs=(
            P(DP, None, None),
            P(DP, None, None),
            P(None, None, "section"),
            P(None, None, "section"),
        ),
        out_specs=(P(), P(DP, None, "section"), P(DP, None, "section")),
        check_vma=False,
    )
```

```python
import functools

import jax
import jax.numpy as jnp
from jax import lax
from jax.experimental import pallas as pl
from jax.experimental.pallas import tpu as pltpu
from jax.sharding import Mesh
from jax.sharding import PartitionSpec as P

DP = ("dp_0", "dp_1", "dp_2")
ZY = ("dp_0", "dp_1")
F32 = jnp.float32
BF16 = jnp.bfloat16
VMEM_LIMIT = 16 << 20
NEAR_PHASES = (True, False)
NEAR_ALL = (True, True)
NEAR_SMALL = True

smooth_width = 0.1
leak_slope = 0.1


def leaky(pre):
    return jnp.where(pre > 0, pre, leak_slope * pre).astype(BF16)


def fold_rows(x):
    x = jnp.sum(x.reshape(-1, 8, x.shape[1]), axis=0)
    return sum(x[:, at : at + 128] for at in range(0, x.shape[1], 128))


def difference_terms(real, fake):
    difference = real.astype(F32) - fake.astype(F32)
    square = difference * difference + smooth_width * smooth_width
    inverse = lax.rsqrt(square)
    return difference * inverse, square * inverse


def dot(a, b):
    return jnp.dot(a, b, preferred_element_type=F32)


def dot_rows(a, b):
    return lax.dot_general(a, b, (((0,), (0,)), ((), ())), preferred_element_type=F32)


def dot_lanes(a, b):
    return lax.dot_general(a, b, (((1,), (1,)), ((), ())), preferred_element_type=F32)


def losses_split(first, second):
    value = jnp.sum(jnp.concatenate([first, second], axis=1), axis=0, keepdims=True)
    return split_rows(value, 0)


def split_rows(value, base):
    row = lax.broadcasted_iota(jnp.int32, (8, value.shape[1]), 0) - base
    high = value.astype(BF16).astype(F32)
    middle = (value - high).astype(BF16).astype(F32)
    low = value - high - middle
    out = jnp.where(row == 0, high, jnp.where(row == 1, middle, jnp.where(row == 2, low, 0.0)))
    return out.astype(BF16)


def strided_conv(take, cols, span, w, h_out, phases_out, loss, padded, *far):
    phases = far[0] if far else phases_out
    frames = span // 3
    rows = 2 * cols * frames
    width = w.shape[2]
    row = lax.broadcasted_iota(jnp.int32, (span, span), 0)
    col = lax.broadcasted_iota(jnp.int32, (span, span), 1)
    phase = jnp.where(row >= 2 * frames, 2, jnp.where(row >= frames, 1, 0))
    select = (col == 3 * (row - frames * phase) + phase).astype(F32).astype(BF16)
    for n in range(2 * cols):
        parts = dot(select, take(n)).astype(BF16)
        for p in range(3):
            phases[p, n * frames : (n + 1) * frames, :] = parts[p * frames : (p + 1) * frames]
    if far:
        copy_out = pltpu.make_async_copy(phases, phases_out, far[1])
        copy_out.start()
    padded[:, :8, :] = jnp.zeros((2 * cols, 8, width), F32)
    earlier = dot(phases[1], w[0]) + dot(phases[2], w[1])
    padded[:, 8 : 8 + frames, :] = earlier.reshape(2 * cols, frames, width)
    same = dot(phases[0], w[2]) + dot(phases[1], w[3]) + dot(phases[2], w[4])
    h = leaky(same + padded[:, 7 : 7 + frames, :].reshape(rows, width))
    h_out[...] = h
    _, root = difference_terms(h[: rows // 2], h[rows // 2 :])
    loss[...] = fold_rows(root - smooth_width)
    if far:
        copy_out.wait()


def copies_of(source, target, sems):
    return [
        pltpu.make_async_copy(source.at[n], target.at[n], sems.at[n])
        for n in range(source.shape[0])
    ]


def first_early_kernel(
    real, fake, w_hbm, h_out, phases_out, loss, w, rest,
    padded, held, held_sem, rest_sem, w_sem, *far_scratch,
):
    cols = held.shape[0] // 2
    span = held.shape[1]
    for n in range(2 * cols):
        source = real if n < cols else fake
        pltpu.make_async_copy(source.at[n % cols], held.at[n], held_sem.at[n]).start()
    w_copies = copies_of(w_hbm, w, w_sem)
    for copy in w_copies:
        copy.start()
    rest_copies = [
        pltpu.make_async_copy(x.at[cols + n], rest.at[at * cols + n], rest_sem.at[at * cols + n])
        for at, x in enumerate((real, fake))
        for n in range(cols)
    ]

    for copy in rest_copies:
        copy.start()

    def take(n):
        source = real if n < cols else fake
        pltpu.make_async_copy(source.at[n % cols], held.at[n], held_sem.at[n]).wait()
        if n == 2 * cols - 1:
            for copy in w_copies:
                copy.wait()
        return held[n]

    strided_conv(take, cols, span, w, h_out, phases_out, loss, padded, *far_scratch)
    for copy in rest_copies:
        copy.wait()


def first_late_kernel(rest, w, w_next_hbm, h_out, phases_out, loss, w_next, padded, sem, *far):
    copies = copies_of(w_next_hbm, w_next, sem)
    for copy in copies:
        copy.start()
    cols, span = rest.shape[0] // 2, rest.shape[1]
    strided_conv(lambda n: rest[n], cols, span, w, h_out, phases_out, loss, padded, *far)
    for copy in copies:
        copy.wait()


def second_kernel(
    normaliser, whole, near, s_ref, own, prev, following, far, w, loss_first,
    all_out, shifted_out, far_t, loss, *rest,
):
    if near:
        h_all, shifted = all_out, shifted_out
        *backs, padded, in_sems = rest
    else:
        *backs, padded, in_sems, h_all, shifted, all_sem, shifted_sem = rest
    rows, width = own.shape
    half = rows // 2
    taps = w.shape[0]
    frames = padded.shape[1] - 16
    s = s_ref[0]
    copies = []
    for away, x in enumerate((own, following, far, prev)):
        at = pl.multiple_of(lax.rem(s + away, 4) * width, 256)
        copies.append(
            pltpu.make_async_copy(x, h_all.at[:, pl.ds(at, width)], in_sems.at[away])
        )
        copies[-1].start()
    for copy in copies:
        copy.wait()
    if not near:
        copy_all = pltpu.make_async_copy(h_all, all_out, all_sem)
        copy_all.start()
    zeros = jnp.zeros((padded.shape[0], 8, width), F32)
    padded[:, :8, :] = zeros
    padded[:, 8 + frames :, :] = zeros
    pre = dot(h_all[...], w[2])
    for k in (0, 1, 3, 4):
        padded[:, 8 : 8 + frames, :] = dot(h_all[...], w[k]).reshape(-1, frames, width)
        pre = pre + padded[:, 6 + k : 6 + k + frames, :].reshape(rows, width)
    h = leaky(pre)
    slope, root = difference_terms(h[:half], h[half:])
    loss_rows = losses_split(loss_first[...], fold_rows(root - smooth_width))
    loss[...] = loss_rows
    slope = slope * (1.0 / normaliser)
    for value, sign, at in ((h[:half], 1.0, 0), (h[half:], -1.0, half // frames)):
        gate = jnp.where(value.astype(F32) > 0, 1.0, leak_slope)
        delta = (sign * slope * gate).astype(BF16).astype(F32)
        padded[at : at + half // frames, 8 : 8 + frames, :] = delta.reshape(-1, frames, width)
    for k in range(taps):
        moved = padded[:, 10 - k : 10 - k + frames, :].reshape(rows, width)
        shifted[:, k * width : (k + 1) * width] = moved.astype(BF16)
    if not near:
        copy_shifted = pltpu.make_async_copy(shifted, shifted_out, shifted_sem)
        copy_shifted.start()
    far_t[:rows] = back_term(s, 2, shifted, w)
    far_t[rows:] = loss_rows
    if whole:
        back_rest(s, shifted, w, loss_rows, 3, *backs)
    if not near:
        copy_all.wait()
        copy_shifted.wait()


def back_term(s, away, shifted, w):
    width = w.shape[2]
    at = pl.multiple_of(lax.rem(s + away, 4) * width, 256)
    term = None
    for k in range(w.shape[0]):
        part = dot_lanes(shifted[:, k * width : (k + 1) * width], w[k, pl.ds(at, width), :])
        term = part if term is None else term + part
    return term.astype(BF16)


def back_rest(s, shifted, w, loss_rows, with_loss, following, prev, own):
    rows = own.shape[0]
    for away, out in ((1, following), (3, prev)) if with_loss == 1 else ((3, prev), (1, following)):
        out[:rows] = back_term(s, away, shifted, w)
        out[rows:] = loss_rows if away == with_loss else jnp.zeros_like(loss_rows)
    own[...] = back_term(s, 0, shifted, w)


def back_kernel(s_ref, shifted, w, loss, following, prev, own, *rest):
    if rest:
        held, sem = rest
        copy = pltpu.make_async_copy(shifted, held, sem)
        copy.start()
        copy.wait()
        shifted = held
    back_rest(s_ref[0], shifted, w, loss[...], 1, following, prev, own)


def add_kernel(a, b, out):
    out[...] = (a[...].astype(F32) + b[...].astype(F32)).astype(BF16)


def put(g, c, outs, at, rows, k):
    count = g.shape[0] // (2 * rows)
    g = g.astype(BF16).reshape(count, 2, rows, g.shape[1])
    even, odd = g[:, 0], g[:, 1]
    mine, theirs = outs
    mine[at : at + count, k * rows : (k + 1) * rows] = jnp.where(c == 0, even, odd)
    theirs[at : at + count, k * rows : (k + 1) * rows] = jnp.where(c == 0, odd, even)


def weight_second_kernel(taps, nears, c_ref, h_a, h_b, shifted_a, shifted_b, mine, theirs, *rest):
    own_rows, width = mine.shape[1] // taps, mine.shape[2]
    c = c_ref[0]
    step = 256
    count = h_a.shape[1] // step
    rest = list(rest)
    pairs, first, later = [], [], [[] for _ in range(count)]
    for near, h, x in ((nears[0], h_a, shifted_a), (nears[1], h_b, shifted_b)):
        if not near:
            h_held, x_held, h_sem, x_sem = rest[:4]
            rest = rest[4:]
            first.append(pltpu.make_async_copy(x, x_held, x_sem))
            for q in range(count):
                cut = slice(q * step, (q + 1) * step)
                later[q].append(
                    pltpu.make_async_copy(h.at[:, cut], h_held.at[:, cut], h_sem.at[q])
                )
            h, x = h_held, x_held
        pairs.append((h, x))
    for copy in first + sum(later, []):
        copy.start()
    for copy in first:
        copy.wait()
    for q in range(count):
        for copy in later[q]:
            copy.wait()
        cut = slice(q * step, (q + 1) * step)
        g = sum(dot_rows(h[:, cut], x[...]) for h, x in pairs)
        for k in range(taps):
            put(g[:, k * width : (k + 1) * width], c, (mine, theirs),
                q * step // (2 * own_rows), own_rows, k)


def weight_first_kernel(
    normaliser, taps, nears, c_ref, loss_a, loss_b, *refs,
):
    *sources, phases_a, phases_b, mine, theirs, padded, moved = refs[:16]
    rest = list(refs[16:])
    rows, width = sources[0].shape
    half = rows // 2
    frames = padded.shape[1] - 8
    c = c_ref[0]
    small, large = [], []
    if not nears[0]:
        got, sems = rest[:2]
        rest = rest[2:]
        for n, x in enumerate(sources):
            small.append(pltpu.make_async_copy(x, got.at[n, : x.shape[0]], sems.at[n]))
        sources = [got.at[n, : x.shape[0]] for n, x in enumerate(sources)]
    phases = []
    for near, x in zip(nears[1:], (phases_a, phases_b)):
        if not near:
            held, sem = rest[:2]
            rest = rest[2:]
            large.append(pltpu.make_async_copy(x, held, sem))
            x = held
        phases.append(x)
    for copy in small + large:
        copy.start()
    for copy in small:
        copy.wait()
    padded[:, frames:, :] = jnp.zeros((padded.shape[0], 8, width), F32)
    for n in range(2):
        h, own, a, b = (sources[2 * at + n] for at in range(4))
        slope, _ = difference_terms(h[:half], h[half:rows])
        slope = slope * (1.0 / normaliser)
        for at, sign in ((0, 1.0), (half, -1.0)):
            cut = slice(at, at + half)
            up = own[cut].astype(F32) + a[cut].astype(F32) + b[cut].astype(F32)
            up = up.astype(BF16).astype(F32)
            gate = jnp.where(h[cut].astype(F32) > 0, 1.0, leak_slope)
            delta = ((sign * slope + up) * gate).astype(BF16)
            base = n * rows + at
            moved[base : base + half, :width] = delta
            cols, lead = half // frames, base // frames
            padded[lead : lead + cols, :frames, :] = delta.astype(F32).reshape(cols, frames, width)
    moved[:, width:] = padded[:, 1 : 1 + frames, :].reshape(2 * rows, width).astype(BF16)
    groups = mine.shape[0]
    own_rows = (mine.shape[1] - 8) // taps
    outs = (mine, theirs)
    for copy in large:
        copy.wait()
    for p in range(3):
        lanes = width if p == 0 else 2 * width
        g = dot_rows(phases[0][p], moved[:rows, :lanes])
        g = g + dot_rows(phases[1][p], moved[rows:, :lanes])
        put(g[:, :width], c, outs, 0, own_rows, 2 + p)
        if p > 0:
            put(g[:, width:], c, outs, 0, own_rows, p - 1)
    total = loss_a[...].astype(F32) + loss_b[...].astype(F32)
    for x in sources[4:]:
        total = total + x[rows:].astype(F32)
    lines = split_rows(jnp.sum(total, axis=0, keepdims=True), 3 * c)
    for x in outs:
        x[:, taps * own_rows :, :] = jnp.broadcast_to(lines[None], (groups, 8, width))


def same_kernel(a, out):
    out[...] = a[...]


def join_kernel(at, a, b, joint, summed, sems):
    count = sems.shape[0]
    step = a.shape[0] // count
    copies = []
    for n in range(count):
        cut = slice(n * step, (n + 1) * step)
        summed[cut] = (a[cut].astype(F32) + b[cut].astype(F32)).astype(BF16)
        copies.append(
            pltpu.make_async_copy(
                summed.at[cut], joint.at[cut, at : at + summed.shape[1]], sems.at[n]
            )
        )
        copies[-1].start()
    for copy in copies:
        copy.wait()


def join_late_kernel(at, a, b, held, joint, summed, sem):
    del held
    join_kernel(at, a, b, joint, summed, sem)


def total_kernel(taps, count_all, blocks, second, first, loss):
    total = jnp.sum(blocks[...].astype(F32), axis=0)
    at = 0
    for out in (second, first):
        rows = taps * out.shape[1]
        out[...] = total[at : at + rows].reshape(out.shape)
        at += rows
    lines = total[at:]
    loss[0] = jnp.sum(lines[:, :128]) / count_all
    loss[1] = jnp.sum(lines[:, 128:]) / count_all


def call(
    kernel, operands, outs, scratch=(), smem=0, hbm=(), loose=(), after=(), smem_outs=(),
    hbm_outs=(), aliases={}, flops=0, cost=1, name=None,
):
    moved = sum(x.size * x.dtype.itemsize for x in operands)
    moved += sum(x.size * x.dtype.itemsize for x in outs)
    vmem, small = pl.BlockSpec(memory_space=pltpu.VMEM), pl.BlockSpec(memory_space=pltpu.SMEM)
    far, anywhere = pl.BlockSpec(memory_space=pltpu.HBM), pl.BlockSpec(memory_space=pl.ANY)
    count = len(operands)
    operands = tuple(
        pltpu.with_memory_space_constraint(x, pltpu.HBM) if at in hbm else x
        for at, x in enumerate(operands)
    )

    def body(*refs):
        kernel(*refs[:count], *refs[count + len(after) :])

    return pl.pallas_call(
        body,
        out_shape=[
            pltpu.HBM(x.shape, x.dtype) if at in hbm_outs else x for at, x in enumerate(outs)
        ],
        in_specs=[
            small if at < smem else far if at in hbm else anywhere if at in loose else vmem
            for at in range(count)
        ]
        + [anywhere] * len(after),
        out_specs=[
            small if at in smem_outs else far if at in hbm_outs else vmem
            for at in range(len(outs))
        ],
        scratch_shapes=list(scratch),
        input_output_aliases=aliases,
        compiler_params=pltpu.CompilerParams(vmem_limit_bytes=VMEM_LIMIT),
        cost_estimate=pl.CostEstimate(
            flops=int(flops * cost), bytes_accessed=int(moved * cost), transcendentals=0
        ),
        name=name,
    )(*operands, *after)


def like(shape, dtype=BF16):
    return jax.ShapeDtypeStruct(shape, dtype)


def turn(x, step):
    count = lax.axis_size("section")
    return lax.ppermute(x, "section", [(i, (i + step) % count) for i in range(count)])


def later(x, after, name):
    return call(same_kernel, (x,), [like(x.shape)], after=after, name=name)[0]


def added(a, b, name, after=()):
    return call(add_kernel, (a, b), [like(a.shape)], after=after, name=name)[0]


def other_core(x):
    return lax.ppermute(x, "dp_2", [(0, 1), (1, 0)])


def shards(real_in, fake_in, kernel_first, kernel_second):
    replicas = lax.axis_size(DP)
    cols, span, in_width = real_in.shape
    frames = span // 3
    taps, width_all, width = kernel_second.shape
    normaliser = float(cols * frames)
    count_all = float(cols * replicas * frames * width_all)
    groups = replicas // 2
    part = cols // 2
    rows = cols * frames
    s = lax.axis_index("section").reshape(1).astype(jnp.int32)
    c = lax.axis_index("dp_2").reshape(1).astype(jnp.int32)
    dma = pltpu.SemaphoreType.DMA
    chunk_outs = [like((rows, width)), like((3, rows, in_width)), like((8, 128), F32)]
    conv_scratch = [pltpu.VMEM((cols, frames + 8, width), F32)]
    phases_far = [pltpu.VMEM((3, rows, in_width), BF16), dma]
    all_far = [pltpu.VMEM((rows, width_all), BF16), pltpu.VMEM((rows, taps * width), BF16)]
    flops = 2 * rows * taps * in_width * width

    h_a, phases_a, loss_a, w_first, rest = call(
        first_early_kernel,
        (real_in, fake_in, kernel_first),
        chunk_outs + [like(kernel_first.shape), like((cols, span, in_width))],
        conv_scratch
        + [pltpu.VMEM((cols, span, in_width), BF16), dma((cols,)), dma((cols,)), dma((taps,))]
        + phases_far * (not NEAR_PHASES[0]),
        hbm=(0, 1, 2),
        hbm_outs=() if NEAR_PHASES[0] else (1,),
        flops=flops,
        name="first_a",
    )
    prev_a = turn(h_a, 1)
    following_a = turn(h_a, -1)
    h_b, phases_b, loss_b, w_second = call(
        first_late_kernel,
        (rest, w_first, kernel_second),
        chunk_outs + [like(kernel_second.shape)],
        conv_scratch + [dma((taps,))] + phases_far * (not NEAR_PHASES[1]),
        hbm=(2,),
        hbm_outs=() if NEAR_PHASES[1] else (1,),
        flops=flops,
        cost=1,
        name="first_b",
    )
    far_a = turn(prev_a, 1)
    following_b = turn(h_b, -1)
    prev_b = turn(later(h_b, (following_a,), "ordered"), 1)
    far_b = turn(following_b, -1)

    second_outs = [like((rows, width_all)), like((rows, taps * width)), like((rows + 8, width)),
                   like((8, width))]
    back_outs = [like((rows + 8, width)), like((rows + 8, width)), like((rows, width))]
    second_scratch = [
        pltpu.VMEM((cols, frames + 16, width), F32), dma((4,)),
    ]
    copies = all_far + [dma, dma]
    flops = 2 * rows * taps * (width_all + width) * width
    all_a, shifted_a, far_t, loss_a, next_t, prev_t, own_a = call(
        functools.partial(second_kernel, normaliser, True, NEAR_ALL[0]),
        (s, h_a, prev_a, following_a, far_a, w_second, loss_a),
        second_outs + back_outs,
        second_scratch + copies * (not NEAR_ALL[0]),
        smem=1,
        loose=(1, 2, 3, 4),
        hbm_outs=() if NEAR_ALL[0] else (0, 1),
        cost=1,
        flops=flops,
        name="second_a",
    )
    pass_a = turn(far_t, 1)
    from_following_a = turn(prev_t, -1)
    relayed_a = added(next_t, pass_a, "relay_a")
    from_prev_a = turn(relayed_a, 1)

    all_b, shifted_b, far_t, loss_b = call(
        functools.partial(second_kernel, normaliser, False, NEAR_ALL[1]),
        (s, h_b, prev_b, following_b, far_b, w_second, loss_b),
        second_outs,
        second_scratch + copies * (not NEAR_ALL[1]),
        smem=1,
        loose=(1, 2, 3, 4),
        hbm_outs=() if NEAR_ALL[1] else (0, 1),
        cost=1,
        after=(own_a,),
        flops=flops,
        name="second_b",
    )
    pass_b = turn(far_t, -1)
    next_t, prev_t, own_b = call(
        back_kernel,
        (s, shifted_b, w_second, loss_b),
        back_outs,
        [] if NEAR_ALL[1] else [pltpu.VMEM((rows, taps * width), BF16), dma],
        smem=1,
        hbm=() if NEAR_ALL[1] else (1,),
        cost=4,
        flops=2 * rows * taps * width * width * 3,
        name="back_b",
    )
    from_prev_b = turn(next_t, 1)
    relayed_b = added(prev_t, pass_b, "relay_b")
    from_following_b = turn(relayed_b, -1)

    own_rows = width_all // replicas
    mine_second, theirs = call(
        functools.partial(weight_second_kernel, taps, NEAR_ALL),
        (c, all_a, all_b, shifted_a, shifted_b),
        [like((groups, taps * own_rows, width))] * 2,
        (all_far + [dma((width_all // 256,)), dma]) * (2 - sum(NEAR_ALL)),
        smem=1,
        hbm=tuple(at for at in (1, 2, 3, 4) if not NEAR_ALL[(at - 1) % 2]),
        cost=4,
        after=(relayed_a, relayed_b),
        flops=4 * rows * taps * width * width_all,
        name="weight_second",
    )
    first_rows = in_width // replicas
    size_second, size_first = taps * own_rows, taps * first_rows + 8
    joint_like = like((groups, size_second + size_first, width))
    (joint,) = call(
        functools.partial(join_kernel, 0),
        (mine_second, other_core(theirs)),
        [joint_like],
        [pltpu.VMEM((groups, size_second, width), BF16), dma((4,))],
        hbm_outs=(0,),
        name="join_second",
    )

    mine_first, theirs = call(
        functools.partial(weight_first_kernel, normaliser, taps, (NEAR_SMALL, *NEAR_PHASES)),
        (c, loss_a, loss_b, h_a, h_b, own_a, own_b, from_prev_a, from_prev_b, from_following_a,
         from_following_b, pass_a, pass_b, phases_a, phases_b),
        [like((groups, taps * first_rows + 8, width))] * 2,
        [pltpu.VMEM((2 * cols, frames + 8, width), F32), pltpu.VMEM((2 * rows, 2 * width), BF16)]
        + [pltpu.VMEM((10, rows + 8, width), BF16), dma((10,))] * (not NEAR_SMALL)
        + phases_far * (2 - sum(NEAR_PHASES)),
        smem=1,
        hbm=tuple(at for at in (13, 14) if not NEAR_PHASES[at - 13]),
        loose=() if NEAR_SMALL else tuple(range(3, 13)),
        cost=20,
        after=(mine_second,),
        flops=4 * rows * taps * width * in_width,
        name="weight_first",
    )
    (joint,) = call(
        functools.partial(join_late_kernel, size_second),
        (mine_first, other_core(theirs), joint),
        [joint_like],
        [pltpu.VMEM((groups, size_first, width), BF16), dma((4,))],
        hbm=(2,),
        hbm_outs=(0,),
        aliases={2: 0},
        name="join_first",
    )
    blocks = lax.all_to_all(joint, ZY, 0, 0)
    grad_second, grad_first, layer_loss = call(
        functools.partial(total_kernel, taps, count_all),
        (blocks,),
        [like((taps, own_rows, width), F32), like((taps, first_rows, width), F32),
         like((2,), F32)],
        smem_outs=(2,),
        name="total",
    )
    return (layer_loss, jnp.transpose(grad_first, (1, 0, 2)), jnp.transpose(grad_second, (1, 0, 2)))


def solution(mesh):
    finer = Mesh(
        mesh.devices.reshape(4, 4, 2, mesh.shape["section"]), ("dp_0", "dp_1", "dp_2", "section")
    )
    return jax.shard_map(
        shards,
        mesh=finer,
        in_specs=(
            P(DP, None, None),
            P(DP, None, None),
            P(None, None, "section"),
            P(None, None, "section"),
        ),
        out_specs=(P(), P(DP, None, "section"), P(DP, None, "section")),
        check_vma=False,
    )
```
